768 devices in a mesh: blocks: 64 (over y, x, core), group: 12 (over z).
Axes of the slice: x: 4, y: 8, z: 12, core: 2. Of those that a mesh axis runs over, the one named last changes fastest.
Arguments:
- ocean_state: float32 [36, 4, 512, 1536], P(None, None, 'blocks', 'group'), may hold values from -6 to 6
- surface_height: float32 [512, 1536], P('blocks', 'group'), may hold values from -6 to 6
- surface_damping: float32 [512, 1536], P('blocks', 'group'), may hold values from 0.05 to 1
- land_mask: int32 [512, 1536], P('blocks', 'group'), may hold values from 0 to 1, as said below
Outputs:
- new_state: float32 [36, 4, 512, 1536], P(None, None, 'blocks', 'group')
- surface: float32 [512, 1536], P('blocks', 'group')
The draws below stay inside these ranges and needn't reach their ends.
Inputs may be any that keep to these rules, and one draw needn't show every extreme that they name: `land_mask`: 1 marks an ocean cell.
All inputs are finite; a program needn't handle non-finite values.
Results may differ from the reference program's by a relative error of at most 0.0003.
Values sent between devices are 32-bit elements; how exact they have to be, the bound alone decides.
A program may use at most 32 MiB of HBM per device.

```python
import math
import jax
import jax.numpy as jnp
from jax import lax

LEV = 36
ITERS = 3
NX = 512
NY = 1536


def draw_ocean_state(key, part):
    shape = (LEV, 4, NX, NY)
    return jnp.clip(jax.random.normal(key, shape, jnp.float32), -4.0, 4.0)


def draw_land_mask(key, part):
    rows = jnp.arange(NX, dtype=jnp.int32)[:, None]
    limit = 256 + 768 * rows // NX
    picked = jax.random.randint(key, (NX, NY), 0, 1024, dtype=jnp.int32)
    return (picked < limit).astype(jnp.int32)


def shard_levels(stream_key, extent, cuts, low, high):
    level = 1.0
    for axis_at, shards_of in cuts:
        draws = jax.random.uniform(jax.random.fold_in(jax.random.fold_in(stream_key, 6), axis_at), (shards_of,), jnp.float32, low / len(cuts), high / len(cuts))
        level = level * jnp.repeat(jnp.exp(draws), extent[axis_at] // shards_of).reshape((-1,) + (1,) * (len(extent) - 1 - axis_at))
    return level


def bell_draw(rng, dims, scale, most, split=(), kind=jnp.bfloat16):
    loudness = shard_levels(rng, dims, split, -0.22, 0.18) if split else 1.0
    result = jax.random.normal(rng, dims, jnp.float32) * scale * loudness
    return jnp.minimum(jnp.maximum(result, -most), most).astype(kind)


def setup_inputs(seed: int = 0) -> dict:
    arg_keys = jax.random.split(jax.random.key(seed), 5)
    return {
        "ocean_state": draw_ocean_state(jax.random.fold_in(arg_keys[4], 71), 0),
        "surface_height": bell_draw(arg_keys[1], (NX, NY), 1.0, 6.0, ((0, 64), (1, 12)), jnp.float32),
        "surface_damping": jnp.clip(jnp.exp(math.log(1.0) - 2.9957323 * jax.random.uniform(arg_keys[2], (NX, NY), jnp.float32) ** shard_levels(arg_keys[2], (NX, NY), ((0, 64), (1, 12)), -0.2, 0.2)), 0.05, 1.0),
        "land_mask": draw_land_mask(jax.random.fold_in(arg_keys[4], 71), 0),
    }


time_step = 0.25
hyper_visc = 0.025
mixing = 0.2
gravity = 4.0
rotation = 0.2


def laplace(padded):
    return (padded[..., 2:, 1:-1] + padded[..., :-2, 1:-1] + padded[..., 1:-1, 2:] + padded[..., 1:-1, :-2]) - 4.0 * padded[..., 1:-1, 1:-1]


def pad_plane(values):
    return jnp.pad(values, [(0, 0)] * (values.ndim - 2) + [(1, 1), (1, 1)])


def level_update(level_now, level_above, level_below, sea_mask, coriolis):
    padded = pad_plane(level_now)
    lap_once = laplace(padded)
    biharm = laplace(pad_plane(lap_once))
    slope_east = 0.5 * (padded[:, 2:, 1:-1] - padded[:, :-2, 1:-1])
    slope_north = 0.5 * (padded[:, 1:-1, 2:] - padded[:, 1:-1, :-2])
    east_flow = level_now[2:3]
    north_flow = level_now[3:4]
    advect = east_flow * slope_east + north_flow * slope_north
    vertical = level_above + level_below - 2.0 * level_now
    zeros_two = jnp.zeros_like(level_now[0:2])
    rotated = jnp.concatenate([zeros_two, coriolis * north_flow, -coriolis * east_flow], axis=0)
    updated = level_now + time_step * (rotated - advect) - hyper_visc * biharm + mixing * vertical
    return sea_mask * updated


def surface_operator(surface_field, damping, sea_mask):
    padded = jnp.pad(surface_field, 1)
    beside = padded[2:, 1:-1] + padded[:-2, 1:-1] + padded[1:-1, 2:] + padded[1:-1, :-2]
    return sea_mask * ((4.0 + damping) * surface_field - beside)


def reference(ocean_state, surface_height, surface_damping, land_mask):
    sea_mask = land_mask.astype(jnp.float32)
    masked = ocean_state * sea_mask
    coriolis = rotation * (2.0 * (jnp.arange(NY).astype(jnp.float32) + 0.5) / NY - 1.0)

    def one_level(level):
        above = jnp.maximum(level - 1, 0).astype(jnp.int32)
        below = jnp.minimum(level + 1, LEV - 1).astype(jnp.int32)
        return level_update(masked[level], masked[above], masked[below], sea_mask, coriolis)

    new_state = lax.map(one_level, jnp.arange(LEV, dtype=jnp.int32))
    transport = jnp.sum(new_state[:, 2:4], axis=0) / LEV
    padded = pad_plane(transport)
    divergence = 0.5 * (padded[0, 2:, 1:-1] - padded[0, :-2, 1:-1] + padded[1, 1:-1, 2:] - padded[1, 1:-1, :-2])
    right_side = sea_mask * (surface_damping * surface_height - gravity * divergence)
    solution = jnp.zeros_like(right_side)
    residual = right_side
    direction = right_side
    norm_now = jnp.sum(residual * residual)
    for iteration in range(ITERS):
        applied = surface_operator(direction, surface_damping, sea_mask)
        step_size = norm_now / jnp.sum(direction * applied)
        solution = solution + step_size * direction
        residual = residual - step_size * applied
        norm_next = jnp.sum(residual * residual)
        direction = residual + (norm_next / norm_now) * direction
        norm_now = norm_next
    return new_state, solution
```

```python
import functools

import jax
import jax.numpy as jnp
from jax import lax
from jax.experimental import pallas as pl
from jax.experimental.pallas import tpu as pltpu
from jax.sharding import PartitionSpec as P

MESH = pl.DeviceIdType.MESH

time_step = 0.25
hyper_visc = 0.025
mixing = 0.2
gravity = 4.0
rotation = 0.2

SHIFT = 4.5
SCALE = 4.0
LOW, HIGH = 0.05, 9.0

GROUP_LEVELS = 6
NEAR = ((-1, 0), (1, 0), (0, -1), (0, 1), (-1, -1), (-1, 1), (1, -1), (1, 1))
OPPOSITE = (1, 0, 3, 2, 7, 6, 5, 4)
UP, DOWN, LEFT, RIGHT, UP_LEFT, UP_RIGHT, DOWN_LEFT, DOWN_RIGHT = range(8)


def roll(x, shift, axis):
    return pltpu.roll(x, shift % x.shape[axis], axis)


def kernel(
    n_blocks, n_group, inner,
    ocean, height, damping, land,
    out, surface,
    ext, sea_int, geo, geo_near, sea_ext, packed, packed_near, corner_near, halo,
    stepped, transport, transport_near, sums, sum_rows,
    load_sems, out_sems, send_sems, near_sems, sum_sems,
):
    levels = ocean.shape[0]
    groups = levels // GROUP_LEVELS
    block = lax.axis_index("blocks")
    part = lax.axis_index("group")
    outer = n_blocks // inner

    def near(n):
        db, dg = NEAR[n]
        return (lax.rem(block + (n_blocks + db), n_blocks), lax.rem(part + (n_group + dg), n_group))

    base = (block // inner) * inner
    phases = []
    phases.append([(base + lax.rem(block - base + s, inner), part) for s in range(1, inner)])
    phases.append([(lax.rem(block + s * inner, n_blocks), part) for s in range(1, outer)])
    phases.append([(block, lax.rem(part + s, n_group)) for s in range(1, n_group)])

    loads = [
        pltpu.make_async_copy(land, sea_int, load_sems.at[0]),
        pltpu.make_async_copy(damping, geo.at[1], load_sems.at[1]),
        pltpu.make_async_copy(height, geo.at[2], load_sems.at[2]),
        pltpu.make_async_copy(ocean, ext.at[1 : levels + 1, :, 8:16, :], load_sems.at[3]),
        pltpu.make_async_copy(ocean.at[0], ext.at[0, :, 8:16, :], load_sems.at[4]),
        pltpu.make_async_copy(ocean.at[levels - 1], ext.at[levels + 1, :, 8:16, :], load_sems.at[5]),
    ]
    for load in loads:
        load.start()

    barrier = pltpu.get_barrier_semaphore()
    partners = [near(n) for n in range(8)] + [p for phase in phases for p in phase]
    for partner in partners:
        pl.semaphore_signal(barrier, inc=1, device_id=partner, device_id_type=MESH)

    row = lax.broadcasted_iota(jnp.int32, (8, 128), 0)
    lane = lax.broadcasted_iota(jnp.int32, (8, 128), 1)
    first_row, last_row = row == 0, row == 7
    first_lane, last_lane = lane == 0, lane == 127
    quarter = lax.rem(lane, 4)
    field_of = lane // 4

    for load in loads[:3]:
        load.wait()
    sea = sea_int[...].astype(jnp.float32)
    geo[0] = sea
    for load in loads[3:]:
        load.wait()

    @pl.loop(0, groups)
    def _(group):
        held = jnp.zeros((8, 128), jnp.float32)
        for i in range(4 * GROUP_LEVELS):
            field = ext[group * GROUP_LEVELS + (i // 4 + 1), i % 4, 8:16, :]
            held = jnp.where(field_of == i, roll(field, 2 + 4 * i, 1), held)
        tiled = jnp.zeros((8, 128), jnp.float32)
        packed[group] = held * packed_sea(sea, quarter, tiled)

    pl.semaphore_wait(barrier, len(partners))

    sends = []

    def send(source, target, n, sem):
        copy = pltpu.make_async_remote_copy(
            src_ref=source, dst_ref=target, send_sem=send_sems.at[len(sends)], recv_sem=near_sems.at[sem],
            device_id=near(n), device_id_type=MESH,
        )
        copy.start()
        sends.append(copy)
        return copy

    rows = [
        send(ocean.at[:, :, 0:2, :], ext.at[1 : levels + 1, :, 16:18, :], UP, 0),
        send(ocean.at[:, :, 6:8, :], ext.at[1 : levels + 1, :, 6:8, :], DOWN, 1),
    ]
    shapes = [send(geo, geo_near.at[OPPOSITE[n]], n, 2 + n) for n in range(8)]
    sides = [send(packed, packed_near.at[OPPOSITE[n] - 2], n, 8 + n) for n in (LEFT, RIGHT)]
    corners = [
        send(packed.at[:, 0:1, :], corner_near.at[OPPOSITE[n] - 4, :, 0:1, :], n, 8 + n) for n in (UP_LEFT, UP_RIGHT)
    ] + [
        send(packed.at[:, 7:8, :], corner_near.at[OPPOSITE[n] - 4, :, 0:1, :], n, 8 + n) for n in (DOWN_LEFT, DOWN_RIGHT)
    ]

    def flag(condition):
        return jnp.where(condition, jnp.float32(1.0), jnp.float32(0.0))

    has_up, has_down = flag(block > 0), flag(block < n_blocks - 1)
    has_left, has_right = flag(part > 0), flag(part < n_group - 1)
    exists = (
        has_up, has_down, has_left, has_right,
        has_up * has_left, has_up * has_right, has_down * has_left, has_down * has_right,
    )

    for copy in shapes + sides + corners:
        copy.wait_recv()

    sea_ext[0:8, :] = geo_near[UP, 0] * has_up
    sea_ext[8:16, :] = sea
    sea_ext[16:24, :] = geo_near[DOWN, 0] * has_down
    sea_n2, sea_n1 = sea_ext[6:14, :], sea_ext[7:15, :]
    sea_s1, sea_s2 = sea_ext[9:17, :], sea_ext[10:18, :]

    @pl.loop(0, groups)
    def _(group):
        own = packed[group]
        left = packed_near[0, group] * has_left
        right = packed_near[1, group] * has_right
        up_left = jnp.broadcast_to(corner_near[0, group, 0:1, :] * exists[UP_LEFT], (8, 128))
        up_right = jnp.broadcast_to(corner_near[1, group, 0:1, :] * exists[UP_RIGHT], (8, 128))
        down_left = jnp.broadcast_to(corner_near[2, group, 0:1, :] * exists[DOWN_LEFT], (8, 128))
        down_right = jnp.broadcast_to(corner_near[3, group, 0:1, :] * exists[DOWN_RIGHT], (8, 128))
        left_rows = jnp.where(first_row, up_left, roll(left, 1, 0)) + jnp.where(last_row, down_left, roll(left, -1, 0))
        right_rows = jnp.where(first_row, up_right, roll(right, 1, 0)) + jnp.where(
            last_row, down_right, roll(right, -1, 0)
        )
        at_left = (2.0 * left_rows + roll(left, 1, 1) + roll(own, -1, 1) - 4.0 * left) * has_left
        at_right = (2.0 * right_rows + roll(right, -1, 1) + roll(own, 1, 1) - 4.0 * right) * has_right
        halo[group] = jnp.where(
            quarter == 0,
            roll(right, -2, 1),
            jnp.where(quarter == 1, left, jnp.where(quarter == 2, at_right, roll(at_left, 2, 1))),
        )

    column = (part * 128 + lane).astype(jnp.float32)
    coriolis = (rotation * time_step) * (2.0 * (column + 0.5) / (128 * n_group) - 1.0)
    middle = 2.0 - jnp.where(first_row, 1.0 - has_up, 0.0) - jnp.where(last_row, 1.0 - has_down, 0.0)

    for copy in rows:
        copy.wait_recv()

    def center(level, c):
        return ext[level, c, 8:16, :] * sea

    def step(group, total):
        total_east, total_north = total
        edges = halo[group]
        for l in range(GROUP_LEVELS):
            level = group * GROUP_LEVELS + (l + 1)
            now = [center(level, c) for c in range(4)]
            u, v = now[2], now[3]
            east, north = (0.5 * time_step) * u, (0.5 * time_step) * v
            for c in range(4):
                i = 4 * l + c
                g = now[c]
                n1, s1 = ext[level, c, 7:15, :] * sea_n1, ext[level, c, 9:17, :] * sea_s1
                n2, s2 = ext[level, c, 6:14, :] * sea_n2, ext[level, c, 10:18, :] * sea_s2
                edge = roll(edges, -(4 * i + 1), 1)
                edge_twice = roll(edges, -(4 * i + 3), 1)
                west = jnp.where(first_lane, edge, roll(g, 1, 1))
                east_of = jnp.where(last_lane, edge, roll(g, -1, 1))
                twice = 2.0 * (n1 + s1) + (west + east_of) - 4.0 * g
                biharm = (
                    (n2 + s2)
                    + middle * g
                    - 4.0 * twice
                    + jnp.where(first_lane, edge_twice, roll(twice, 1, 1))
                    + jnp.where(last_lane, edge_twice, roll(twice, -1, 1))
                )
                advect = east * (s1 - n1) + north * (east_of - west)
                vertical = center(level - 1, c) + center(level + 1, c) - 2.0 * g
                new = g - advect - hyper_visc * biharm + mixing * vertical
                if c == 2:
                    new = new + coriolis * v
                elif c == 3:
                    new = new - coriolis * u
                new = new * sea
                stepped[group * GROUP_LEVELS + l, c] = new
                if c == 2:
                    total_east = total_east + new
                elif c == 3:
                    total_north = total_north + new
        return total_east, total_north

    zero = jnp.zeros((8, 128), jnp.float32)
    total_east, total_north = lax.fori_loop(0, groups, step, (zero, zero))
    transport[0] = total_east / levels
    transport[1] = total_north / levels

    beside = [send(transport, transport_near.at[OPPOSITE[n]], n, 16 + n) for n in range(8)]
    stores = [
        pltpu.make_async_copy(
            stepped.at[k * GROUP_LEVELS : (k + 1) * GROUP_LEVELS],
            out.at[k * GROUP_LEVELS : (k + 1) * GROUP_LEVELS],
            out_sems.at[k],
        )
        for k in range(groups)
    ]
    for store in stores:
        store.start()

    def around(own, others):
        low, west_half = row < 4, lane < 64
        side = jnp.where(west_half, others[RIGHT], others[LEFT])
        over = jnp.where(low, others[DOWN], others[UP])
        corner = jnp.where(
            low,
            jnp.where(west_half, others[DOWN_RIGHT], others[DOWN_LEFT]),
            jnp.where(west_half, others[UP_RIGHT], others[UP_LEFT]),
        )
        return jnp.concatenate(
            [jnp.concatenate([own, side], axis=1), jnp.concatenate([over, corner], axis=1)], axis=0
        )

    sea_near = [geo_near[n, 0] * exists[n] for n in range(8)]
    sea_all = around(sea, sea_near)
    damping_all = around(geo[1], [geo_near[n, 1] for n in range(8)])
    forced = sea_all * damping_all * around(geo[2], [geo_near[n, 2] for n in range(8)])
    own_part = sea_all * ((4.0 - SHIFT + damping_all) * (1.0 / SCALE))
    beside_part = sea_all * (1.0 / SCALE)

    for copy in beside:
        copy.wait_recv()
    east_all = sea_all * around(transport[0], [transport_near[n, 0] for n in range(8)])
    north_all = sea_all * around(transport[1], [transport_near[n, 1] for n in range(8)])
    divergence = 0.5 * (roll(east_all, -1, 0) - roll(east_all, 1, 0) + roll(north_all, -1, 1) - roll(north_all, 1, 1))
    v0 = forced - (gravity * sea_all) * divergence

    def apply(s):
        return own_part * s - beside_part * (roll(s, -1, 0) + roll(s, 1, 0) + roll(s, -1, 1) + roll(s, 1, 1))

    v1 = apply(v0)
    v2 = apply(v1)
    v3 = apply(v2)
    v0, v1, v2, v3 = (v[0:8, 0:128] for v in (v0, v1, v2, v3))

    moments = (v0 * v0, v0 * v1, v1 * v1, v1 * v2, v2 * v2, v2 * v3)
    stacked = zero
    for m, moment in enumerate(moments):
        stacked = jnp.where(row == m, jnp.sum(moment, axis=0, keepdims=True), stacked)
    stacked = jnp.sum(stacked, axis=1, keepdims=True)
    partial = jnp.sum(jnp.where(lane == row, stacked, 0.0), axis=0, keepdims=True)

    at = 0
    for number, phase in enumerate(phases):
        count = len(phase)
        if count == 0:
            continue
        size = sum_rows.shape[1]
        sums[number, 0:1, :] = partial
        sum_rows[number, count:size, :] = jnp.zeros((size - count, 128), jnp.float32)
        copies = []
        for s, partner in enumerate(phase):
            copy = pltpu.make_async_remote_copy(
                src_ref=sums.at[number, 0:1, :], dst_ref=sum_rows.at[number, s : s + 1, :],
                send_sem=send_sems.at[len(sends)], recv_sem=sum_sems.at[at],
                device_id=partner, device_id_type=MESH,
            )
            copy.start()
            copies.append(copy)
            sends.append(copy)
            at += 1
        for copy in copies:
            copy.wait_recv()
        partial = partial + jnp.sum(sum_rows[number], axis=0, keepdims=True)

    spread = jnp.broadcast_to(partial, (8, 128))
    mu = [jnp.sum(jnp.where(lane == m, spread, 0.0), axis=1, keepdims=True) for m in range(6)]
    c0, c1, c2 = coefficients(mu)
    surface[...] = c0 * v0 + c1 * v1 + c2 * v2

    for copy in sends:
        copy.wait_send()
    for store in stores:
        store.wait()


def packed_sea(sea, quarter, held):
    lane = lax.broadcasted_iota(jnp.int32, (8, 128), 1)
    held = jnp.where(lane < 4, roll(sea, 2, 1), held)
    for shift in (4, 8, 16, 32, 64):
        held = held + roll(held, shift, 1)
    return held


def coefficients(mu):
    def inner(p, q, offset=0):
        total = None
        by_power = {}
        for i, a in enumerate(p):
            for j, b in enumerate(q):
                term = a * b
                by_power[i + j] = term if i + j not in by_power else by_power[i + j] + term
        for power, weight in by_power.items():
            term = weight * mu[power + offset]
            total = term if total is None else total + term
        return total

    def alpha_of(rr, d):
        image = SHIFT * inner(d, d) + SCALE * inner(d, d, 1)
        return jnp.clip(rr / image, 1.0 / HIGH, 1.0 / LOW)

    one = jnp.ones_like(mu[0])
    r, d = [one], [one]
    rr = mu[0]
    x = []
    for iteration in range(3):
        alpha = alpha_of(rr, d)
        x = [alpha * a + (x[i] if i < len(x) else 0.0) for i, a in enumerate(d)]
        if iteration == 2:
            break
        image = [SHIFT * (d[i] if i < len(d) else 0.0) + (SCALE * d[i - 1] if i > 0 else 0.0) for i in range(len(d) + 1)]
        r = [(r[i] if i < len(r) else 0.0) - alpha * image[i] for i in range(len(image))]
        new = jnp.maximum(inner(r, r), 0.0)
        beta = jnp.clip(new / rr, 0.0, HIGH / LOW)
        d = [r[i] + (beta * d[i] if i < len(d) else 0.0) for i in range(len(r))]
        rr = new
    return x


def on_device(n_blocks, n_group, inner, ocean_state, surface_height, surface_damping, land_mask):
    levels = ocean_state.shape[0]
    groups = levels // GROUP_LEVELS
    f32 = jnp.float32
    any_space = pl.BlockSpec(memory_space=pl.ANY)
    n_sums = (inner - 1) + (n_blocks // inner - 1) + (n_group - 1)
    dma = pltpu.SemaphoreType.DMA
    return pl.pallas_call(
        functools.partial(kernel, n_blocks, n_group, inner),
        out_shape=(
            jax.ShapeDtypeStruct(ocean_state.shape, f32),
            jax.ShapeDtypeStruct(surface_height.shape, f32),
        ),
        in_specs=[any_space] * 4,
        out_specs=(any_space, pl.BlockSpec(memory_space=pltpu.VMEM)),
        scratch_shapes=[
            pltpu.VMEM((levels + 2, 4, 24, 128), f32),
            pltpu.VMEM((8, 128), jnp.int32),
            pltpu.VMEM((3, 8, 128), f32),
            pltpu.VMEM((8, 3, 8, 128), f32),
            pltpu.VMEM((24, 128), f32),
            pltpu.VMEM((groups, 8, 128), f32),
            pltpu.VMEM((2, groups, 8, 128), f32),
            pltpu.VMEM((4, groups, 8, 128), f32),
            pltpu.VMEM((groups, 8, 128), f32),
            pltpu.VMEM((levels, 4, 8, 128), f32),
            pltpu.VMEM((2, 8, 128), f32),
            pltpu.VMEM((8, 2, 8, 128), f32),
            pltpu.VMEM((3, 8, 128), f32),
            pltpu.VMEM((3, 16, 128), f32),
            dma((6,)),
            dma((groups,)),
            dma((24 + n_sums,)),
            dma((24,)),
            dma((n_sums,)),
        ],
        compiler_params=pltpu.CompilerParams(collective_id=0, has_side_effects=True),
    )(ocean_state, surface_height, surface_damping, land_mask)


def solution(mesh):
    n_blocks, n_group = mesh.shape["blocks"], mesh.shape["group"]
    inner = 8 if n_blocks % 8 == 0 and n_blocks > 8 else max(1, n_blocks // 2)
    placed = (
        P(None, None, "blocks", "group"),
        P("blocks", "group"),
        P("blocks", "group"),
        P("blocks", "group"),
    )
    return jax.shard_map(
        functools.partial(on_device, n_blocks, n_group, inner),
        mesh=mesh,
        in_specs=placed,
        out_specs=(P(None, None, "blocks", "group"), P("blocks", "group")),
        check_vma=False,
    )
```

```python
import functools

import jax
import jax.numpy as jnp
from jax import lax
from jax.experimental import pallas as pl
from jax.experimental.pallas import tpu as pltpu
from jax.sharding import PartitionSpec as P

MESH = pl.DeviceIdType.MESH

time_step = 0.25
hyper_visc = 0.025
mixing = 0.2
gravity = 4.0
rotation = 0.2

LOW, HIGH = 0.05, 9.0
REACH = 1.125

GROUP_LEVELS = 6
NEAR = ((-1, 0), (1, 0), (0, -1), (0, 1), (-1, -1), (-1, 1), (1, -1), (1, 1))
OPPOSITE = (1, 0, 3, 2, 7, 6, 5, 4)
UP, DOWN, LEFT, RIGHT, UP_LEFT, UP_RIGHT, DOWN_LEFT, DOWN_RIGHT = range(8)
ROUNDS = ((1, 1), (2, 2), (1, 2))


def roll(x, shift, axis):
    return pltpu.roll(x, shift % x.shape[axis], axis)


def two_sum(a, b):
    s = a + b
    t = s - a
    return s, (a - (s - t)) + (b - t)


def quick_sum(a, b):
    s = a + b
    return s, b - (s - a)


def split(a):
    c = 4097.0 * a
    high = c - (c - a)
    return high, a - high


def two_prod(a, b):
    p = a * b
    (ah, al), (bh, bl) = split(a), split(b)
    return p, ((ah * bh - p) + ah * bl + al * bh) + al * bl


def add(a, b):
    s, e = two_sum(a[0], b[0])
    return quick_sum(s, e + (a[1] + b[1]))


def scale(a, power_of_two):
    return a[0] * power_of_two, a[1] * power_of_two


def minus(a, b):
    return add(a, (-b[0], -b[1]))


def mul(a, b):
    p, e = two_prod(a[0], b[0])
    return quick_sum(p, e + (a[0] * b[1] + a[1] * b[0]))


def div(a, b):
    first = a[0] / b[0]
    rest = minus(a, mul(b, (first, jnp.zeros_like(first))))
    return quick_sum(first, rest[0] / b[0])


def sum_rows_of(x):
    parts = [(x[i : i + 8], None) for i in range(0, x.shape[0], 8)]
    while len(parts) > 1:
        parts = [join(*parts[i : i + 2]) for i in range(0, len(parts), 2)]
    part = parts[0]
    for shift in (4, 2, 1):
        other = (roll(part[0], shift, 0), None if part[1] is None else roll(part[1], shift, 0))
        part = join(part, other)
    return part


def join(a, b=None):
    if b is None:
        return a
    s, e = two_sum(a[0], b[0])
    for low in (a[1], b[1]):
        if low is not None:
            e = e + low
    return s, e


def kernel(
    n_blocks, n_group, inner,
    ocean, height, damping, land,
    out, surface,
    own, sea_int, geo, geo_near, rows_own, rows_near, rows_fix, packed, packed_near, corner_near, packed_fix,
    sums_own, sums_near, transport, transport_near, row_out, rows_in,
    load_sems, send_sems, near_sems, sum_sems, greet_sems,
):
    levels = ocean.shape[0]
    groups = levels // GROUP_LEVELS
    block = lax.axis_index("blocks")
    part = lax.axis_index("group")
    outer = n_blocks // inner

    def near(n):
        db, dg = NEAR[n]
        return (lax.rem(block + (n_blocks + db), n_blocks), lax.rem(part + (n_group + dg), n_group))

    base = (block // inner) * inner

    def along_blocks(distance):
        return (lax.rem(block + (distance % n_blocks), n_blocks), part)

    def along_group(distance):
        return (block, lax.rem(part + (distance % n_group), n_group))

    def far_first(n):
        return sorted(range(1, n), key=lambda s: -min(s, n - s))

    phases = [[along_blocks(s) for s in far_first(n_blocks)], [along_group(s) for s in far_first(n_group)]]
    rounds = []
    for rows_off, group_off in ROUNDS:
        targets = []
        if rows_off % outer:
            targets += [along_blocks(rows_off * inner), along_blocks(-rows_off * inner)]
        if group_off % n_group:
            targets += [along_group(group_off), along_group(-group_off)]
        rounds.append(targets)

    loads = [
        pltpu.make_async_copy(land, sea_int, load_sems.at[0]),
        pltpu.make_async_copy(damping, geo.at[1], load_sems.at[1]),
        pltpu.make_async_copy(height, geo.at[2], load_sems.at[2]),
        pltpu.make_async_copy(ocean, own.at[1 : levels + 1], load_sems.at[3]),
        pltpu.make_async_copy(ocean.at[0], own.at[0], load_sems.at[4]),
        pltpu.make_async_copy(ocean.at[levels - 1], own.at[levels + 1], load_sems.at[5]),
        pltpu.make_async_copy(ocean.at[:, 2, 0, :], rows_own.at[0], load_sems.at[6]),
        pltpu.make_async_copy(ocean.at[:, 2, 7, :], rows_own.at[1], load_sems.at[7]),
    ]

    barrier = pltpu.get_barrier_semaphore()
    partners = (
        [near(n) for n in range(8)]
        + [(base + lax.rem(block - base + s, inner), part) for s in range(1, inner)]
        + ([along_blocks(inner), along_blocks(-inner)] if outer > 1 else [])
    )
    for partner in partners:
        pl.semaphore_signal(barrier, inc=1, device_id=partner, device_id_type=MESH)
    for load in loads:
        load.start()

    row = lax.broadcasted_iota(jnp.int32, (8, 128), 0)
    lane = lax.broadcasted_iota(jnp.int32, (8, 128), 1)
    first_row, last_row = row == 0, row == 7
    first_lane, last_lane = lane == 0, lane == 127
    quarter = lax.rem(lane, 4)
    field_of = lane // 4
    zero = jnp.zeros((8, 128), jnp.float32)

    def flag(condition):
        return jnp.where(condition, jnp.float32(1.0), jnp.float32(0.0))

    has_up, has_down = flag(block > 0), flag(block < n_blocks - 1)
    has_left, has_right = flag(part > 0), flag(part < n_group - 1)
    exists = (
        has_up, has_down, has_left, has_right,
        has_up * has_left, has_up * has_right, has_down * has_left, has_down * has_right,
    )

    sends = []

    def send(source, target, partner, sem):
        copy = pltpu.make_async_remote_copy(
            src_ref=source, dst_ref=target, send_sem=send_sems.at[len(sends)], recv_sem=sem,
            device_id=partner, device_id_type=MESH,
        )
        copy.start()
        sends.append(copy)
        return copy

    pl.semaphore_wait(barrier, len(partners))

    def greet(n):
        for target in rounds[n]:
            pl.semaphore_signal(greet_sems.at[n], inc=1, device_id=target, device_id_type=MESH)

    def greeted(n):
        if rounds[n]:
            pl.semaphore_wait(greet_sems.at[n], len(rounds[n]))

    greet(0)

    def send_rows(c):
        copies = []
        for r in range(2):
            copies.append(send(ocean.at[:, c, r, :], rows_near.at[1, r, c], near(UP), near_sems.at[4 * c + r]))
            copies.append(
                send(ocean.at[:, c, 7 - r, :], rows_near.at[0, r, c], near(DOWN), near_sems.at[4 * c + 2 + r])
            )
        return copies

    flow_rows = send_rows(2) + send_rows(3)

    for load in loads[:3]:
        load.wait()
    sea = sea_int[...].astype(jnp.float32)
    geo[0] = sea
    at = 16
    shapes = [send(geo, geo_near.at[OPPOSITE[n]], near(n), near_sems.at[at + n]) for n in range(8)]

    sea_packed = jnp.where(lane < 4, roll(sea, 2, 1), 0.0)
    for shift in (4, 8, 16, 32, 64):
        sea_packed = sea_packed + roll(sea_packed, shift, 1)

    for load in loads[3:]:
        load.wait()

    @pl.loop(0, groups)
    def _(group):
        held = [zero, zero, zero]
        for i in range(4 * GROUP_LEVELS):
            field = own[group * GROUP_LEVELS + (i // 4 + 1), i % 4]
            held[i % 3] = jnp.where(field_of == i, roll(field, 2 + 4 * i, 1), held[i % 3])
        packed[group] = (held[0] + held[1] + held[2]) * sea_packed

    at = 24
    sides = [
        send(packed, packed_near.at[OPPOSITE[n] - 2], near(n), near_sems.at[at + n - 2]) for n in (LEFT, RIGHT)
    ]
    at = 26
    corners = []
    for n in (UP_LEFT, UP_RIGHT, DOWN_LEFT, DOWN_RIGHT):
        edge = 0 if NEAR[n][0] < 0 else 7
        corners.append(
            send(
                packed.at[:, edge : edge + 1, :],
                corner_near.at[OPPOSITE[n] - 4, :, 0:1, :],
                near(n),
                near_sems.at[at + n - 4],
            )
        )
    tracer_rows = send_rows(0) + send_rows(1)

    column = (part * 128 + lane).astype(jnp.float32)
    coriolis = (rotation * time_step) * (2.0 * (column + 0.5) / (128 * n_group) - 1.0)
    middle = 2.0 - jnp.where(first_row, 1.0 - has_up, 0.0) - jnp.where(last_row, 1.0 - has_down, 0.0)
    not_first, not_last = flag(row > 0), flag(row < 7)

    def step(level, carry):
        totals, above, now = carry
        below = tuple(own[level + 2, c] * sea for c in range(4))
        u, v = now[2], now[3]
        east, north = (0.5 * time_step) * u, (0.5 * time_step) * v
        totals = list(totals)
        for c in range(4):
            g = now[c]
            n1, s1 = not_first * roll(g, 1, 0), not_last * roll(g, -1, 0)
            n2, s2 = not_first * roll(n1, 1, 0), not_last * roll(s1, -1, 0)
            west = jnp.where(first_lane, 0.0, roll(g, 1, 1))
            east_of = jnp.where(last_lane, 0.0, roll(g, -1, 1))
            twice = 2.0 * (n1 + s1) + (west + east_of) - 4.0 * g
            biharm = (
                (n2 + s2)
                + middle * g
                - 4.0 * twice
                + jnp.where(first_lane, 0.0, roll(twice, 1, 1))
                + jnp.where(last_lane, 0.0, roll(twice, -1, 1))
            )
            advect = east * (s1 - n1) + north * (east_of - west)
            vertical = above[c] + below[c] - 2.0 * g
            new = g - advect - hyper_visc * biharm + mixing * vertical
            if c == 2:
                new = new + coriolis * v
            elif c == 3:
                new = new - coriolis * u
            new = new * sea
            out[level, c] = new
            if c >= 2:
                totals[c - 2] = totals[c - 2] + new
                totals[c] = totals[c] + g
        return tuple(totals), now, below

    top = tuple(own[0, c] * sea for c in range(4))
    now = tuple(own[1, c] * sea for c in range(4))
    totals, _, _ = lax.fori_loop(0, levels, step, ((zero, zero, zero, zero), top, now))
    sums_own[0] = totals[2]
    sums_own[1] = totals[3]
    at = 30
    shared = [send(sums_own, sums_near.at[OPPOSITE[n]], near(n), near_sems.at[at + n]) for n in range(8)]
    greeted(0)
    greet(1)

    own_flow = []
    for group in range(groups):
        flow = jnp.where(lax.rem(field_of, 4) == 3, packed[group], 0.0)
        flow = flow + roll(flow, -4, 1)
        own_flow.append((0.5 * time_step) * (flow + roll(flow, -8, 1)))

    for copy in shapes[:4] + sides + flow_rows:
        copy.wait_recv()

    sea_rows = (
        (geo_near[UP, 0, 7:8, :] * has_up, geo_near[UP, 0, 6:7, :] * has_up),
        (geo_near[DOWN, 0, 0:1, :] * has_down, geo_near[DOWN, 0, 1:2, :] * has_down),
    )
    own_rows = ((geo[0, 0:1, :], geo[0, 1:2, :]), (geo[0, 7:8, :], geo[0, 6:7, :]))
    edge_lane = lax.broadcasted_iota(jnp.int32, (levels, 128), 1)
    no_west, no_east = edge_lane == 0, edge_lane == 127

    def fix_rows(c):
        totals = []
        for side in range(2):
            outer_sign = (0.5 * time_step) if side == 0 else -(0.5 * time_step)
            a = rows_near[side, 0, c] * sea_rows[side][0]
            b = rows_near[side, 1, c] * sea_rows[side][1]
            across = jnp.where(no_west, 0.0, roll(a, 1, 1)) + jnp.where(no_east, 0.0, roll(a, -1, 1))
            nearest = (
                -hyper_visc * (b - 8.0 * a + 2.0 * across) + (outer_sign * own_rows[side][0]) * rows_own[side] * a
            ) * own_rows[side][0]
            second = (-hyper_visc * a) * own_rows[side][1]
            rows_fix[side, 0, c] = nearest
            rows_fix[side, 1, c] = second
            totals.append(jnp.sum(nearest, axis=0, keepdims=True))
            totals.append(jnp.sum(second, axis=0, keepdims=True))
        first, second, last, before_last = (jnp.broadcast_to(t, (8, 128)) for t in totals)
        return jnp.where(
            first_row,
            first,
            jnp.where(row == 1, second, jnp.where(last_row, last, jnp.where(row == 6, before_last, 0.0))),
        )

    def fix_columns(group):
        mine = packed[group]
        left = packed_near[0, group] * has_left
        right = packed_near[1, group] * has_right
        left_rows = not_first * roll(left, 1, 0) + not_last * roll(left, -1, 0)
        right_rows = not_first * roll(right, 1, 0) + not_last * roll(right, -1, 0)
        at_left = 2.0 * left_rows + roll(left, 1, 1) + has_left * roll(mine, -1, 1) - 8.0 * left
        at_right = 2.0 * right_rows + roll(right, -1, 1) + has_right * roll(mine, 1, 1) - 8.0 * right
        flow = own_flow[group]
        fixed = jnp.where(
            quarter == 0,
            -hyper_visc * roll(right, -2, 1),
            jnp.where(
                quarter == 1,
                -hyper_visc * roll(at_right, -1, 1) - flow * roll(right, -1, 1),
                jnp.where(
                    quarter == 2,
                    -hyper_visc * roll(at_left, 1, 1) + flow * roll(left, 1, 1),
                    -hyper_visc * roll(left, 2, 1),
                ),
            ),
        )
        return fixed * sea_packed

    beside_edges = (lane < 2) | (lane >= 126)
    columns_total = zero
    for group in range(groups):
        fixed = fix_columns(group)
        packed_fix[group] = fixed
        columns_total = columns_total + fixed
    gathered = columns_total
    for l in range(1, GROUP_LEVELS):
        gathered = gathered + roll(columns_total, -16 * l, 1)
    for c in (2, 3):
        at_columns = jnp.where(beside_edges, roll(gathered, -(4 * c + 2), 1), 0.0)
        transport[c - 2] = (totals[c - 2] + fix_rows(c) + at_columns) / levels

    at = 38
    beside = [send(transport, transport_near.at[OPPOSITE[n]], near(n), near_sems.at[at + n]) for n in range(8)]
    greeted(1)
    greet(2)

    for copy in shapes[4:] + corners + tracer_rows + shared:
        copy.wait_recv()

    fix_rows(0)
    fix_rows(1)

    def finish(group, carry):
        def at_corner(n):
            return jnp.broadcast_to(corner_near[n - 4, group, 0:1, :] * exists[n], (8, 128))

        left_corner = jnp.where(first_row, at_corner(UP_LEFT), jnp.where(last_row, at_corner(DOWN_LEFT), 0.0))
        right_corner = jnp.where(first_row, at_corner(UP_RIGHT), jnp.where(last_row, at_corner(DOWN_RIGHT), 0.0))
        corner = jnp.where(
            quarter == 1, roll(right_corner, -1, 1), jnp.where(quarter == 2, roll(left_corner, 1, 1), 0.0)
        )
        fixed = packed_fix[group] - (2.0 * hyper_visc) * corner * sea_packed
        for i in range(4 * GROUP_LEVELS):
            level, c = group * GROUP_LEVELS + i // 4, i % 4
            first, second, last, before_last = (
                jnp.broadcast_to(rows_fix[side, r, c, pl.ds(level, 1), :], (8, 128))
                for side in range(2)
                for r in range(2)
            )
            by_rows = jnp.where(
                first_row,
                first,
                jnp.where(row == 1, second, jnp.where(last_row, last, jnp.where(row == 6, before_last, 0.0))),
            )
            by_columns = jnp.where(beside_edges, roll(fixed, -(4 * i + 2), 1), 0.0)
            out[level, c] = out[level, c] + by_rows + by_columns
        return carry

    lax.fori_loop(0, groups, finish, 0)

    def around(mine, others):
        low, west_half = row < 4, lane < 64
        side = jnp.where(west_half, others[RIGHT], others[LEFT])
        over = jnp.where(low, others[DOWN], others[UP])
        corner = jnp.where(
            low,
            jnp.where(west_half, others[DOWN_RIGHT], others[DOWN_LEFT]),
            jnp.where(west_half, others[UP_RIGHT], others[UP_LEFT]),
        )
        return jnp.concatenate(
            [jnp.concatenate([mine, side], axis=1), jnp.concatenate([over, corner], axis=1)], axis=0
        )

    ring_row = lax.broadcasted_iota(jnp.int32, (16, 256), 0)
    ring_lane = lax.broadcasted_iota(jnp.int32, (16, 256), 1)

    def over_corners(x):
        x = jnp.where(
            (ring_row == 0) | (ring_row == 8),
            roll(x, 1, 0),
            jnp.where((ring_row == 7) | (ring_row == 15), roll(x, -1, 0), 0.0),
        )
        return jnp.where(
            (ring_lane == 0) | (ring_lane == 128),
            roll(x, 1, 1),
            jnp.where((ring_lane == 127) | (ring_lane == 255), roll(x, -1, 1), 0.0),
        )

    sea_all = around(sea, [geo_near[n, 0] * exists[n] for n in range(8)])
    damping_all = around(geo[1], [geo_near[n, 1] for n in range(8)])
    forced = sea_all * damping_all * around(geo[2], [geo_near[n, 2] for n in range(8)])
    missing = [
        ((-2.0 * hyper_visc) / levels)
        * over_corners(sea_all * around(sums_own[m], [sums_near[n, m] for n in range(8)]))
        for m in range(2)
    ]
    own_part = sea_all * ((damping_all - 0.5) * 0.25)
    own_split = split(own_part)
    beside_part = sea_all * -0.25

    for copy in beside:
        copy.wait_recv()
    east_all = sea_all * (around(transport[0], [transport_near[n, 0] for n in range(8)]) + missing[0])
    north_all = sea_all * (around(transport[1], [transport_near[n, 1] for n in range(8)]) + missing[1])
    divergence = 0.5 * (roll(east_all, -1, 0) - roll(east_all, 1, 0) + roll(north_all, -1, 1) - roll(north_all, 1, 1))
    v0 = forced - (gravity * sea_all) * divergence

    def apply(s):
        high, low = s
        up, down = (roll(high, 1, 0), low if low is None else roll(low, 1, 0)), (roll(high, -1, 0), low if low is None else roll(low, -1, 0))
        west, east = (roll(high, 1, 1), low if low is None else roll(low, 1, 1)), (roll(high, -1, 1), low if low is None else roll(low, -1, 1))
        total = join(join(up, down), join(west, east))
        high_split = split(high)
        p = own_part * high
        (ah, al), (bh, bl) = own_split, high_split
        e = ((ah * bh - p) + ah * bl + al * bh) + al * bl
        if low is not None:
            e = e + own_part * low
        return add((p, e), (beside_part * total[0], beside_part * total[1]))

    v1 = apply((v0, None))
    v2 = apply(v1)
    v3 = apply(v2)
    v0 = v0[0:8, 0:128]
    v1, v2, v3 = (tuple(x[0:8, 0:128] for x in v) for v in (v1, v2, v3))
    v0 = (v0, zero)

    high, low = zero, zero
    for m, (a, b) in enumerate(((v0, v0), (v0, v1), (v1, v1), (v1, v2), (v2, v2), (v2, v3))):
        p, e = two_prod(a[0], b[0])
        e = e + (a[0] * b[1] + a[1] * b[0])
        part_sum = (p, e)
        for shift in (4, 2, 1):
            part_sum = join(part_sum, (roll(part_sum[0], shift, 0), roll(part_sum[1], shift, 0)))
        high = jnp.where(row == m, part_sum[0], high)
        low = jnp.where(row == m, part_sum[1], low)
    total = (high, low)
    for shift in (64, 32, 16, 8, 4, 2, 1):
        total = join(total, (roll(total[0], shift, 1), roll(total[1], shift, 1)))
    value = jnp.sum(
        jnp.where(lane == row, total[0], jnp.where(lane == row + 64, total[1], 0.0)), axis=0, keepdims=True
    )

    greeted(2)
    at = 0
    for number, phase in enumerate(phases):
        count = len(phase)
        size = -(-(count + 1) // 8) * 8
        row_out[number, 0:1, :] = value
        copies = []
        for s, partner in enumerate(phase):
            copies.append(
                send(row_out.at[number, 0:1, :], rows_in.at[number, s : s + 1, :], partner, sum_sems.at[at + s])
            )
        at += count
        for copy in copies:
            copy.wait_recv()
        got = rows_in[number, 0:size, :]
        row_number = lax.broadcasted_iota(jnp.int32, (size, 128), 0)
        got = jnp.where(row_number < count, got, jnp.where(row_number == count, row_out[number, 0:1, :], 0.0))
        summed, lost = sum_rows_of(got)
        value = jnp.where(lane < 64, summed, summed + roll(lost, 64, 1))[0:1, :]

    spread = jnp.broadcast_to(value, (8, 128))

    def pick(m):
        return jnp.sum(jnp.where(lane == m, spread, 0.0), axis=1, keepdims=True)

    mu = [quick_sum(pick(m), pick(64 + m)) for m in range(6)]
    surface[...] = combine(mu, v0, v1, v2)

    for copy in sends:
        copy.wait_send()


def combine(mu, v0, v1, v2):
    a = [add(scale(add(mu[k], mu[k + 1]), 4.0), scale(mu[k], 0.5)) for k in range(5)]
    l1, l2 = div(a[1], a[0]), div(a[2], a[0])
    s11 = minus(a[2], mul(l1, a[1]))
    s12 = minus(a[3], mul(l1, a[2]))
    s22 = minus(a[4], mul(l2, a[2]))
    y1 = minus(mu[1], mul(l1, mu[0]))
    y2 = minus(mu[2], mul(l2, mu[0]))
    sound = s11[0] > 0.0
    one = jnp.ones_like(s11[0])
    none = jnp.zeros_like(s11[0])
    s11 = (jnp.where(sound, s11[0], one), jnp.where(sound, s11[1], none))
    l21 = div(s12, s11)
    inside = sound & (jnp.abs(l21[0] - l1[0]) <= REACH)
    bounded = jnp.clip(l21[0], l1[0] - REACH, l1[0] + REACH)
    l21 = (
        jnp.where(sound, jnp.where(inside, l21[0], bounded), l1[0]),
        jnp.where(sound, jnp.where(inside, l21[1], none), l1[1]),
    )
    t22 = minus(s22, mul(l21, s12))
    z2 = minus(y2, mul(l21, y1))

    def step_of(quotient):
        return jnp.clip(quotient, 1.0 / HIGH, 1.0 / LOW)

    alpha0 = step_of(mu[0][0] / a[0][0])
    alpha1 = step_of(y1[0] / (s11[0] * (-4.0 * alpha0)))
    firm = t22[0] > 0.0
    alpha2 = step_of(z2[0] / (jnp.where(firm, t22[0], one) * (16.0 * alpha0 * alpha1)))

    def wide(pair):
        return tuple(jnp.broadcast_to(x, v0[0].shape) for x in pair)

    l1, l2, l21 = wide(l1), wide(l2), wide(l21)
    p1 = minus(v1, mul(l1, v0))
    p2 = minus(v2, add(mul(l2, v0), mul(l21, p1)))
    return alpha0 * (v0[0] + alpha1 * (-4.0 * p1[0] + (16.0 * alpha2) * p2[0]))


def on_device(n_blocks, n_group, inner, ocean_state, surface_height, surface_damping, land_mask):
    levels = ocean_state.shape[0]
    groups = levels // GROUP_LEVELS
    f32 = jnp.float32
    any_space = pl.BlockSpec(memory_space=pl.ANY)
    vmem = pl.BlockSpec(memory_space=pltpu.VMEM)
    n_sums = (n_blocks - 1) + (n_group - 1)
    dma = pltpu.SemaphoreType.DMA
    return pl.pallas_call(
        functools.partial(kernel, n_blocks, n_group, inner),
        out_shape=(pltpu.VMEM(ocean_state.shape, f32), pltpu.VMEM(surface_height.shape, f32)),
        in_specs=[any_space] * 4,
        out_specs=(vmem, vmem),
        scratch_shapes=[
            pltpu.VMEM((levels + 2, 4, 8, 128), f32),
            pltpu.VMEM((8, 128), jnp.int32),
            pltpu.VMEM((3, 8, 128), f32),
            pltpu.VMEM((8, 3, 8, 128), f32),
            pltpu.VMEM((2, levels, 128), f32),
            pltpu.VMEM((2, 2, 4, levels, 128), f32),
            pltpu.VMEM((2, 2, 4, levels, 128), f32),
            pltpu.VMEM((groups, 8, 128), f32),
            pltpu.VMEM((2, groups, 8, 128), f32),
            pltpu.VMEM((4, groups, 8, 128), f32),
            pltpu.VMEM((groups, 8, 128), f32),
            pltpu.VMEM((2, 8, 128), f32),
            pltpu.VMEM((8, 2, 8, 128), f32),
            pltpu.VMEM((2, 8, 128), f32),
            pltpu.VMEM((8, 2, 8, 128), f32),
            pltpu.VMEM((2, 8, 128), f32),
            pltpu.VMEM((2, max(n_blocks, 16), 128), f32),
            dma((8,)),
            dma((46 + n_sums,)),
            dma((46,)),
            dma((n_sums,)),
            pltpu.SemaphoreType.REGULAR((len(ROUNDS),)),
        ],
        compiler_params=pltpu.CompilerParams(collective_id=0, has_side_effects=True),
    )(ocean_state, surface_height, surface_damping, land_mask)


def solution(mesh):
    n_blocks, n_group = mesh.shape["blocks"], mesh.shape["group"]
    inner = 8 if n_blocks % 8 == 0 and n_blocks > 8 else max(1, n_blocks // 2)
    placed = (
        P(None, None, "blocks", "group"),
        P("blocks", "group"),
        P("blocks", "group"),
        P("blocks", "group"),
    )
    return jax.shard_map(
        functools.partial(on_device, n_blocks, n_group, inner),
        mesh=mesh,
        in_specs=placed,
        out_specs=(P(None, None, "blocks", "group"), P("blocks", "group")),
        check_vma=False,
    )
```

```python
import functools

import jax
import jax.numpy as jnp
from jax import lax
from jax.experimental import pallas as pl
from jax.experimental.pallas import tpu as pltpu
from jax.sharding import PartitionSpec as P

MESH = pl.DeviceIdType.MESH

time_step = 0.25
hyper_visc = 0.025
mixing = 0.2
gravity = 4.0
rotation = 0.2

LOW, HIGH = 0.05, 9.0
REACH = 1.125

GROUP_LEVELS = 6
NEAR = ((-1, 0), (1, 0), (0, -1), (0, 1), (-1, -1), (-1, 1), (1, -1), (1, 1))
OPPOSITE = (1, 0, 3, 2, 7, 6, 5, 4)
UP, DOWN, LEFT, RIGHT, UP_LEFT, UP_RIGHT, DOWN_LEFT, DOWN_RIGHT = range(8)
ROUNDS = ((1, 1), (2, 2), (1, 2))


def roll(x, shift, axis):
    return pltpu.roll(x, shift % x.shape[axis], axis)


def two_sum(a, b):
    s = a + b
    t = s - a
    return s, (a - (s - t)) + (b - t)


def quick_sum(a, b):
    s = a + b
    return s, b - (s - a)


def split(a):
    c = 4097.0 * a
    high = c - (c - a)
    return high, a - high


def two_prod(a, b):
    p = a * b
    (ah, al), (bh, bl) = split(a), split(b)
    return p, ((ah * bh - p) + ah * bl + al * bh) + al * bl


def add(a, b):
    s, e = two_sum(a[0], b[0])
    return quick_sum(s, e + (a[1] + b[1]))


def scale(a, power_of_two):
    return a[0] * power_of_two, a[1] * power_of_two


def minus(a, b):
    return add(a, (-b[0], -b[1]))


def mul(a, b):
    p, e = two_prod(a[0], b[0])
    return quick_sum(p, e + (a[0] * b[1] + a[1] * b[0]))


def div(a, b):
    first = a[0] / b[0]
    rest = minus(a, mul(b, (first, jnp.zeros_like(first))))
    return quick_sum(first, rest[0] / b[0])


def sum_rows_of(x):
    parts = [(x[i : i + 8], None) for i in range(0, x.shape[0], 8)]
    while len(parts) > 1:
        parts = [join(*parts[i : i + 2]) for i in range(0, len(parts), 2)]
    part = parts[0]
    for shift in (4, 2, 1):
        other = (roll(part[0], shift, 0), None if part[1] is None else roll(part[1], shift, 0))
        part = join(part, other)
    return part


def join(a, b=None):
    if b is None:
        return a
    s, e = two_sum(a[0], b[0])
    for low in (a[1], b[1]):
        if low is not None:
            e = e + low
    return s, e


def kernel(
    n_blocks, n_group, inner,
    ocean, height, damping, land,
    out, surface,
    own, sea_int, geo, geo_near, rows_own, rows_near, rows_fix, packed, packed_near, corner_near, packed_fix,
    flow, flow_near, sums_own, sums_near, row_out, rows_in,
    load_sems, send_sems, near_sems, greet_sems,
):
    levels = ocean.shape[0]
    groups = levels // GROUP_LEVELS
    block = lax.axis_index("blocks")
    part = lax.axis_index("group")
    outer = n_blocks // inner

    def near(n):
        db, dg = NEAR[n]
        return (lax.rem(block + (n_blocks + db), n_blocks), lax.rem(part + (n_group + dg), n_group))

    base = (block // inner) * inner

    def along_blocks(distance):
        return (lax.rem(block + (distance % n_blocks), n_blocks), part)

    def along_group(distance):
        return (block, lax.rem(part + (distance % n_group), n_group))

    def far_first(n):
        return sorted(range(1, n), key=lambda s: -min(s, n - s))

    phases = [[along_blocks(s) for s in far_first(n_blocks)], [along_group(s) for s in far_first(n_group)]]
    rounds = []
    for rows_off, group_off in ROUNDS:
        targets = []
        if rows_off % outer:
            targets += [along_blocks(rows_off * inner), along_blocks(-rows_off * inner)]
        if group_off % n_group:
            targets += [along_group(group_off), along_group(-group_off)]
        rounds.append(targets)

    loads = [
        pltpu.make_async_copy(land, sea_int, load_sems.at[0]),
        pltpu.make_async_copy(damping, geo.at[1], load_sems.at[1]),
        pltpu.make_async_copy(height, geo.at[2], load_sems.at[2]),
        pltpu.make_async_copy(ocean, own.at[1 : levels + 1], load_sems.at[3]),
        pltpu.make_async_copy(ocean.at[0], own.at[0], load_sems.at[4]),
        pltpu.make_async_copy(ocean.at[levels - 1], own.at[levels + 1], load_sems.at[5]),
    ]
    for side in range(2):
        for c in range(2):
            loads.append(
                pltpu.make_async_copy(
                    ocean.at[:, c + 2, 7 * side, :], rows_own.at[side, c], load_sems.at[6 + 2 * side + c]
                )
            )

    barrier = pltpu.get_barrier_semaphore()
    partners = (
        [near(n) for n in range(8)]
        + [(base + lax.rem(block - base + s, inner), part) for s in range(1, inner)]
        + ([along_blocks(inner), along_blocks(-inner)] if outer > 1 else [])
    )
    for partner in partners:
        pl.semaphore_signal(barrier, inc=1, device_id=partner, device_id_type=MESH)
    for load in loads:
        load.start()

    row = lax.broadcasted_iota(jnp.int32, (8, 128), 0)
    lane = lax.broadcasted_iota(jnp.int32, (8, 128), 1)
    first_row, last_row = row == 0, row == 7
    first_lane, last_lane = lane == 0, lane == 127
    quarter = lax.rem(lane, 4)
    field_of = lane // 4
    zero = jnp.zeros((8, 128), jnp.float32)

    def flag(condition):
        return jnp.where(condition, jnp.float32(1.0), jnp.float32(0.0))

    has_up, has_down = flag(block > 0), flag(block < n_blocks - 1)
    has_left, has_right = flag(part > 0), flag(part < n_group - 1)
    exists = (
        has_up, has_down, has_left, has_right,
        has_up * has_left, has_up * has_right, has_down * has_left, has_down * has_right,
    )

    sends = []

    def send(source, target, partner):
        copy = pltpu.make_async_remote_copy(
            src_ref=source, dst_ref=target, send_sem=send_sems.at[len(sends)], recv_sem=near_sems.at[len(sends)],
            device_id=partner, device_id_type=MESH,
        )
        copy.start()
        sends.append(copy)
        return copy

    pl.semaphore_wait(barrier, len(partners))

    def greet(n):
        for target in rounds[n]:
            pl.semaphore_signal(greet_sems.at[n], inc=1, device_id=target, device_id_type=MESH)

    def greeted(n):
        if rounds[n]:
            pl.semaphore_wait(greet_sems.at[n], len(rounds[n]))

    greet(0)

    def send_rows(c, r):
        return [
            send(ocean.at[:, c, r, :], rows_near.at[1, r, c], near(UP)),
            send(ocean.at[:, c, 7 - r, :], rows_near.at[0, r, c], near(DOWN)),
        ]

    flow_rows = send_rows(2, 0) + send_rows(3, 0)

    for load in loads[:3]:
        load.wait()
    sea = sea_int[...].astype(jnp.float32)
    geo[0] = sea
    shapes = [send(geo, geo_near.at[OPPOSITE[n]], near(n)) for n in range(8)]

    for load in loads[3:]:
        load.wait()

    eighth = lax.rem(lane, 8)
    sea_flow = jnp.where(lane < 8, roll(sea, 4, 1), 0.0)
    for shift in (8, 16, 32, 64):
        sea_flow = sea_flow + roll(sea_flow, shift, 1)
    for group in range(groups):
        held = [zero, zero, zero, zero]
        for i in range(2 * GROUP_LEVELS):
            field = own[group * GROUP_LEVELS + (i // 2 + 1), 2 + i % 2]
            held[i % 4] = jnp.where(lane // 8 == i, roll(field, 4 + 8 * i, 1), held[i % 4])
        flow[group] = ((held[0] + held[1]) + (held[2] + held[3])) * sea_flow
    flows = []
    for n in range(8):
        rows = {-1: pl.ds(0, 4), 0: pl.ds(0, 8), 1: pl.ds(4, 4)}[NEAR[n][0]]
        flows.append(send(flow.at[:, rows, :], flow_near.at[OPPOSITE[n], :, rows, :], near(n)))

    not_first, not_last = flag(row > 0), flag(row < 7)

    def advection(level, carry):
        u, v = own[level + 1, 2] * sea, own[level + 1, 3] * sea
        east, north = (0.5 * time_step) * u, (0.5 * time_step) * v
        terms = []
        for g in (u, v):
            along = not_last * roll(g, -1, 0) - not_first * roll(g, 1, 0)
            across = jnp.where(last_lane, 0.0, roll(g, -1, 1)) - jnp.where(first_lane, 0.0, roll(g, 1, 1))
            terms.append(east * along + north * across)
        return carry[0] + u, carry[1] + v, carry[2] + terms[0], carry[3] + terms[1]

    for n, total in enumerate(lax.fori_loop(0, levels, advection, (zero, zero, zero, zero), unroll=4)):
        sums_own[n] = total
    shared = [send(sums_own, sums_near.at[OPPOSITE[n]], near(n)) for n in range(8)]

    sea_packed = jnp.where(lane < 4, roll(sea, 2, 1), 0.0)
    for shift in (4, 8, 16, 32, 64):
        sea_packed = sea_packed + roll(sea_packed, shift, 1)

    @pl.loop(0, groups)
    def _(group):
        held = [zero, zero, zero]
        for i in range(4 * GROUP_LEVELS):
            field = own[group * GROUP_LEVELS + (i // 4 + 1), i % 4]
            held[i % 3] = jnp.where(field_of == i, roll(field, 2 + 4 * i, 1), held[i % 3])
        packed[group] = (held[0] + held[1] + held[2]) * sea_packed

    sides = [send(packed, packed_near.at[OPPOSITE[n] - 2], near(n)) for n in (LEFT, RIGHT)]
    corners = []
    for n in (UP_LEFT, UP_RIGHT, DOWN_LEFT, DOWN_RIGHT):
        edge = 0 if NEAR[n][0] < 0 else 7
        corners.append(
            send(packed.at[:, edge : edge + 1, :], corner_near.at[OPPOSITE[n] - 4, :, 0:1, :], near(n))
        )
    other_rows = send_rows(2, 1) + send_rows(3, 1)
    for c in (0, 1):
        other_rows += send_rows(c, 0) + send_rows(c, 1)
    greeted(0)
    greet(1)

    column = (part * 128 + lane).astype(jnp.float32)
    coriolis = (rotation * time_step) * (2.0 * (column + 0.5) / (128 * n_group) - 1.0)
    middle = 2.0 - jnp.where(first_row, 1.0 - has_up, 0.0) - jnp.where(last_row, 1.0 - has_down, 0.0)
    def step(level, carry):
        above, now = carry
        below = tuple(own[level + 2, c] * sea for c in range(4))
        u, v = now[2], now[3]
        east, north = (0.5 * time_step) * u, (0.5 * time_step) * v
        for c in range(4):
            g = now[c]
            n1, s1 = not_first * roll(g, 1, 0), not_last * roll(g, -1, 0)
            n2, s2 = not_first * roll(n1, 1, 0), not_last * roll(s1, -1, 0)
            west = jnp.where(first_lane, 0.0, roll(g, 1, 1))
            east_of = jnp.where(last_lane, 0.0, roll(g, -1, 1))
            twice = 2.0 * (n1 + s1) + (west + east_of) - 4.0 * g
            biharm = (
                (n2 + s2)
                + middle * g
                - 4.0 * twice
                + jnp.where(first_lane, 0.0, roll(twice, 1, 1))
                + jnp.where(last_lane, 0.0, roll(twice, -1, 1))
            )
            advect = east * (s1 - n1) + north * (east_of - west)
            vertical = above[c] + below[c] - 2.0 * g
            new = g - advect - hyper_visc * biharm + mixing * vertical
            if c == 2:
                new = new + coriolis * v
            elif c == 3:
                new = new - coriolis * u
            new = new * sea
            out[level, c] = new
        return now, below

    top = tuple(own[0, c] * sea for c in range(4))
    now = tuple(own[1, c] * sea for c in range(4))
    lax.fori_loop(0, levels, step, (top, now))
    greeted(1)
    greet(2)

    def around(mine, others):
        low, west_half = row < 4, lane < 64
        side = jnp.where(west_half, others[RIGHT], others[LEFT])
        over = jnp.where(low, others[DOWN], others[UP])
        corner = jnp.where(
            low,
            jnp.where(west_half, others[DOWN_RIGHT], others[DOWN_LEFT]),
            jnp.where(west_half, others[UP_RIGHT], others[UP_LEFT]),
        )
        return jnp.concatenate(
            [jnp.concatenate([mine, side], axis=1), jnp.concatenate([over, corner], axis=1)], axis=0
        )

    for copy in flow_rows + shapes + flows + shared:
        copy.wait_recv()

    sea_near = [geo_near[n, 0] * exists[n] for n in range(8)]
    sea_all = around(sea, sea_near)
    damping_all = around(geo[1], [geo_near[n, 1] for n in range(8)])
    forced = sea_all * damping_all * around(geo[2], [geo_near[n, 2] for n in range(8)])

    def around_whole(mine, others):
        west_half = lane < 64
        blocks = [
            [mine, jnp.where(west_half, others[RIGHT], others[LEFT])],
            [others[DOWN], jnp.where(west_half, others[DOWN_RIGHT], others[DOWN_LEFT])],
            [others[UP], jnp.where(west_half, others[UP_RIGHT], others[UP_LEFT])],
        ]
        return jnp.concatenate([jnp.concatenate(b, axis=1) for b in blocks], axis=0)

    def ring_laplace(x):
        return (roll(x, 1, 0) + roll(x, -1, 0)) + (roll(x, 1, 1) + roll(x, -1, 1)) - 4.0 * x

    inside = around_whole(zero + 1.0, [zero + exists[n] for n in range(8)])
    ring_lane = lax.broadcasted_iota(jnp.int32, (24, 256), 1)
    ring_column = (part * 128 + jnp.where(ring_lane < 192, ring_lane, ring_lane - 256)).astype(jnp.float32)
    ring_coriolis = (rotation * time_step) * (2.0 * (ring_column + 0.5) / (128 * n_group) - 1.0)
    level_sums = [
        around_whole(sums_own[m], [sums_near[n, m] * exists[n] for n in range(8)]) for m in range(2)
    ]
    linear = []
    for m in range(2):
        g = level_sums[m]
        linear.append(
            (g - hyper_visc * ring_laplace(inside * ring_laplace(g)))
            + (ring_coriolis if m == 0 else -ring_coriolis) * level_sums[1 - m]
        )

    flow_lane = lane // 8
    is_east_field = lax.rem(flow_lane, 2) == 0
    before_edge, after_edge = flag(eighth == 3), flag(eighth == 4)
    first, last = flag(first_row), flag(last_row)

    def of_u(x):
        x = jnp.where(is_east_field, x, 0.0)
        return x + roll(x, 8, 1)

    def of_v(x):
        x = jnp.where(is_east_field, 0.0, x)
        return x + roll(x, -8, 1)

    def across_columns(x, beside):
        return of_v(x) * (before_edge * roll(beside, -1, 1) - after_edge * roll(beside, 1, 1))

    def across_rows(x, beside):
        return of_u(x) * (last * roll(beside, -1, 0) - first * roll(beside, 1, 0))

    gathered = [zero, zero, zero, zero]
    for group in range(groups):
        tiles = [flow_near[n, group] * exists[n] for n in range(8)]
        low, ends = row < 4, eighth < 4
        mine = flow[group]
        over = jnp.where(low, tiles[DOWN], tiles[UP])
        side = jnp.where(ends, tiles[LEFT], tiles[RIGHT])
        over_side = jnp.where(
            low,
            jnp.where(ends, tiles[DOWN_LEFT], tiles[DOWN_RIGHT]),
            jnp.where(ends, tiles[UP_LEFT], tiles[UP_RIGHT]),
        )
        gathered[0] = gathered[0] + across_columns(mine, side)
        gathered[1] = gathered[1] + (across_columns(side, mine) + across_rows(side, over_side))
        gathered[2] = gathered[2] + across_columns(over, over_side)
        gathered[3] = gathered[3] + (across_columns(over_side, over) + across_rows(over_side, side))

    def by_component(x, edge):
        total = x
        for l in range(1, GROUP_LEVELS):
            total = total + roll(x, -16 * l, 1)
        return [jnp.where(edge, roll(total, -(8 * c + 4), 1), 0.0) for c in range(2)]

    at_edge = first_lane | last_lane
    near_edge = (lane < 4) | (lane >= 124)
    edges = [by_component(gathered[n], at_edge if n in (0, 2) else near_edge) for n in range(4)]

    def met(x, g, weight):
        return jnp.broadcast_to(jnp.sum(x * g, axis=0, keepdims=True) * weight, (8, 128))

    above_weight = geo[0, 0:1, :] * (geo_near[UP, 0, 7:8, :] * has_up)
    below_weight = geo[0, 7:8, :] * (geo_near[DOWN, 0, 0:1, :] * has_down)
    advected = []
    for m in range(2):
        up_g, down_g = rows_near[0, 0, 2 + m], rows_near[1, 0, 2 + m]
        inner_rows = last * met(rows_own[1, 0], down_g, below_weight) - first * met(rows_own[0, 0], up_g, above_weight)
        outer_rows = last * met(rows_near[0, 0, 2], rows_own[0, m], above_weight) - first * met(
            rows_near[1, 0, 2], rows_own[1, m], below_weight
        )
        crossing = jnp.concatenate(
            [
                jnp.concatenate([edges[0][m] + inner_rows, edges[1][m]], axis=1),
                jnp.concatenate([edges[2][m] + outer_rows, edges[3][m]], axis=1),
            ],
            axis=0,
        )
        advected.append(
            around(sums_own[2 + m], [sums_near[n, 2 + m] for n in range(8)]) + (0.5 * time_step) * crossing
        )

    ring_low = lax.broadcasted_iota(jnp.int32, (8, 256), 0) < 4
    transport = []
    for m in range(2):
        nearest = jnp.concatenate(
            [linear[m][0:8], jnp.where(ring_low, linear[m][8:16], linear[m][16:24])], axis=0
        )
        transport.append(sea_all * ((nearest - advected[m]) / levels))
    east_all, north_all = transport
    own_part = sea_all * ((damping_all - 0.5) * 0.25)
    own_split = split(own_part)
    beside_part = sea_all * -0.25

    divergence = 0.5 * (roll(east_all, -1, 0) - roll(east_all, 1, 0) + roll(north_all, -1, 1) - roll(north_all, 1, 1))
    v0 = forced - (gravity * sea_all) * divergence

    def finish_state():
        own_flow = []
        for group in range(groups):
            north = jnp.where(lax.rem(field_of, 4) == 3, packed[group], 0.0)
            north = north + roll(north, -4, 1)
            own_flow.append((0.5 * time_step) * (north + roll(north, -8, 1)))

        for copy in sides + corners + other_rows:
            copy.wait_recv()

        sea_rows = (
            (geo_near[UP, 0, 7:8, :] * has_up, geo_near[UP, 0, 6:7, :] * has_up),
            (geo_near[DOWN, 0, 0:1, :] * has_down, geo_near[DOWN, 0, 1:2, :] * has_down),
        )
        own_rows = ((geo[0, 0:1, :], geo[0, 1:2, :]), (geo[0, 7:8, :], geo[0, 6:7, :]))
        edge_lane = lax.broadcasted_iota(jnp.int32, (levels, 128), 1)
        no_west, no_east = edge_lane == 0, edge_lane == 127

        def fix_rows(c):
            for side in range(2):
                outer_sign = (0.5 * time_step) if side == 0 else -(0.5 * time_step)
                a = rows_near[side, 0, c] * sea_rows[side][0]
                b = rows_near[side, 1, c] * sea_rows[side][1]
                across = jnp.where(no_west, 0.0, roll(a, 1, 1)) + jnp.where(no_east, 0.0, roll(a, -1, 1))
                nearest = (
                    -hyper_visc * (b - 8.0 * a + 2.0 * across) + (outer_sign * own_rows[side][0]) * rows_own[side, 0] * a
                ) * own_rows[side][0]
                second = (-hyper_visc * a) * own_rows[side][1]
                rows_fix[side, 0, c] = nearest
                rows_fix[side, 1, c] = second

        def fix_columns(group):
            mine = packed[group]
            left = packed_near[0, group] * has_left
            right = packed_near[1, group] * has_right
            left_rows = not_first * roll(left, 1, 0) + not_last * roll(left, -1, 0)
            right_rows = not_first * roll(right, 1, 0) + not_last * roll(right, -1, 0)
            at_left = 2.0 * left_rows + roll(left, 1, 1) + has_left * roll(mine, -1, 1) - 8.0 * left
            at_right = 2.0 * right_rows + roll(right, -1, 1) + has_right * roll(mine, 1, 1) - 8.0 * right
            swept = own_flow[group]
            fixed = jnp.where(
                quarter == 0,
                -hyper_visc * roll(right, -2, 1),
                jnp.where(
                    quarter == 1,
                    -hyper_visc * roll(at_right, -1, 1) - swept * roll(right, -1, 1),
                    jnp.where(
                        quarter == 2,
                        -hyper_visc * roll(at_left, 1, 1) + swept * roll(left, 1, 1),
                        -hyper_visc * roll(left, 2, 1),
                    ),
                ),
            )
            return fixed * sea_packed

        beside_edges = (lane < 2) | (lane >= 126)
        for group in range(groups):
            packed_fix[group] = fix_columns(group)
        for c in range(4):
            fix_rows(c)

        def finish(group, carry):
            def at_corner(n):
                return jnp.broadcast_to(corner_near[n - 4, group, 0:1, :] * exists[n], (8, 128))

            left_corner = jnp.where(first_row, at_corner(UP_LEFT), jnp.where(last_row, at_corner(DOWN_LEFT), 0.0))
            right_corner = jnp.where(first_row, at_corner(UP_RIGHT), jnp.where(last_row, at_corner(DOWN_RIGHT), 0.0))
            corner = jnp.where(
                quarter == 1, roll(right_corner, -1, 1), jnp.where(quarter == 2, roll(left_corner, 1, 1), 0.0)
            )
            fixed = packed_fix[group] - (2.0 * hyper_visc) * corner * sea_packed
            for i in range(4 * GROUP_LEVELS):
                level, c = group * GROUP_LEVELS + i // 4, i % 4
                first, second, last, before_last = (
                    jnp.broadcast_to(rows_fix[side, r, c, pl.ds(level, 1), :], (8, 128))
                    for side in range(2)
                    for r in range(2)
                )
                by_rows = jnp.where(
                    first_row,
                    first,
                    jnp.where(row == 1, second, jnp.where(last_row, last, jnp.where(row == 6, before_last, 0.0))),
                )
                by_columns = jnp.where(beside_edges, roll(fixed, -(4 * i + 2), 1), 0.0)
                out[level, c] = out[level, c] + by_rows + by_columns
            return carry

        lax.fori_loop(0, groups, finish, 0)

    def apply(s):
        high, low = s
        up, down = (roll(high, 1, 0), low if low is None else roll(low, 1, 0)), (roll(high, -1, 0), low if low is None else roll(low, -1, 0))
        west, east = (roll(high, 1, 1), low if low is None else roll(low, 1, 1)), (roll(high, -1, 1), low if low is None else roll(low, -1, 1))
        total = join(join(up, down), join(west, east))
        high_split = split(high)
        p = own_part * high
        (ah, al), (bh, bl) = own_split, high_split
        e = ((ah * bh - p) + ah * bl + al * bh) + al * bl
        if low is not None:
            e = e + own_part * low
        return add((p, e), (beside_part * total[0], beside_part * total[1]))

    v1 = apply((v0, None))
    v2 = apply(v1)
    v3 = apply(v2)
    v0 = v0[0:8, 0:128]
    v1, v2, v3 = (tuple(x[0:8, 0:128] for x in v) for v in (v1, v2, v3))
    v0 = (v0, zero)

    high, low = zero, zero
    for m, (a, b) in enumerate(((v0, v0), (v0, v1), (v1, v1), (v1, v2), (v2, v2), (v2, v3))):
        p, e = two_prod(a[0], b[0])
        e = e + (a[0] * b[1] + a[1] * b[0])
        part_sum = (p, e)
        for shift in (4, 2, 1):
            part_sum = join(part_sum, (roll(part_sum[0], shift, 0), roll(part_sum[1], shift, 0)))
        high = jnp.where(row == m, part_sum[0], high)
        low = jnp.where(row == m, part_sum[1], low)
    total = (high, low)
    for shift in (64, 32, 16, 8, 4, 2, 1):
        total = join(total, (roll(total[0], shift, 1), roll(total[1], shift, 1)))
    value = jnp.sum(
        jnp.where(lane == row, total[0], jnp.where(lane == row + 64, total[1], 0.0)), axis=0, keepdims=True
    )

    greeted(2)
    for number, phase in enumerate(phases):
        count = len(phase)
        size = -(-(count + 1) // 8) * 8
        row_out[number, 0:1, :] = value
        copies = []
        for s, partner in enumerate(phase):
            copies.append(
                send(row_out.at[number, 0:1, :], rows_in.at[number, s : s + 1, :], partner)
            )
        if number == 0:
            finish_state()
        for copy in copies:
            copy.wait_recv()
        got = rows_in[number, 0:size, :]
        row_number = lax.broadcasted_iota(jnp.int32, (size, 128), 0)
        got = jnp.where(row_number < count, got, jnp.where(row_number == count, row_out[number, 0:1, :], 0.0))
        summed, lost = sum_rows_of(got)
        value = jnp.where(lane < 64, summed, summed + roll(lost, 64, 1))[0:1, :]

    spread = jnp.broadcast_to(value, (8, 128))

    def pick(m):
        return jnp.sum(jnp.where(lane == m, spread, 0.0), axis=1, keepdims=True)

    mu = [quick_sum(pick(m), pick(64 + m)) for m in range(6)]
    surface[...] = combine(mu, v0, v1, v2)

    for copy in sends:
        copy.wait_send()


def combine(mu, v0, v1, v2):
    a = [add(scale(add(mu[k], mu[k + 1]), 4.0), scale(mu[k], 0.5)) for k in range(5)]
    l1, l2 = div(a[1], a[0]), div(a[2], a[0])
    s11 = minus(a[2], mul(l1, a[1]))
    s12 = minus(a[3], mul(l1, a[2]))
    s22 = minus(a[4], mul(l2, a[2]))
    y1 = minus(mu[1], mul(l1, mu[0]))
    y2 = minus(mu[2], mul(l2, mu[0]))
    sound = s11[0] > 0.0
    one = jnp.ones_like(s11[0])
    none = jnp.zeros_like(s11[0])
    s11 = (jnp.where(sound, s11[0], one), jnp.where(sound, s11[1], none))
    l21 = div(s12, s11)
    inside = sound & (jnp.abs(l21[0] - l1[0]) <= REACH)
    bounded = jnp.clip(l21[0], l1[0] - REACH, l1[0] + REACH)
    l21 = (
        jnp.where(sound, jnp.where(inside, l21[0], bounded), l1[0]),
        jnp.where(sound, jnp.where(inside, l21[1], none), l1[1]),
    )
    t22 = minus(s22, mul(l21, s12))
    z2 = minus(y2, mul(l21, y1))

    def step_of(quotient):
        return jnp.clip(quotient, 1.0 / HIGH, 1.0 / LOW)

    alpha0 = step_of(mu[0][0] / a[0][0])
    alpha1 = step_of(y1[0] / (s11[0] * (-4.0 * alpha0)))
    firm = t22[0] > 0.0
    alpha2 = step_of(z2[0] / (jnp.where(firm, t22[0], one) * (16.0 * alpha0 * alpha1)))

    def wide(pair):
        return tuple(jnp.broadcast_to(x, v0[0].shape) for x in pair)

    l1, l2, l21 = wide(l1), wide(l2), wide(l21)
    p1 = minus(v1, mul(l1, v0))
    p2 = minus(v2, add(mul(l2, v0), mul(l21, p1)))
    return alpha0 * (v0[0] + alpha1 * (-4.0 * p1[0] + (16.0 * alpha2) * p2[0]))


def on_device(n_blocks, n_group, inner, ocean_state, surface_height, surface_damping, land_mask):
    levels = ocean_state.shape[0]
    groups = levels // GROUP_LEVELS
    f32 = jnp.float32
    any_space = pl.BlockSpec(memory_space=pl.ANY)
    vmem = pl.BlockSpec(memory_space=pltpu.VMEM)
    n_sums = (n_blocks - 1) + (n_group - 1)
    dma = pltpu.SemaphoreType.DMA
    return pl.pallas_call(
        functools.partial(kernel, n_blocks, n_group, inner),
        out_shape=(pltpu.VMEM(ocean_state.shape, f32), pltpu.VMEM(surface_height.shape, f32)),
        in_specs=[any_space] * 4,
        out_specs=(vmem, vmem),
        scratch_shapes=[
            pltpu.VMEM((levels + 2, 4, 8, 128), f32),
            pltpu.VMEM((8, 128), jnp.int32),
            pltpu.VMEM((3, 8, 128), f32),
            pltpu.VMEM((8, 3, 8, 128), f32),
            pltpu.VMEM((2, 2, levels, 128), f32),
            pltpu.VMEM((2, 2, 4, levels, 128), f32),
            pltpu.VMEM((2, 2, 4, levels, 128), f32),
            pltpu.VMEM((groups, 8, 128), f32),
            pltpu.VMEM((2, groups, 8, 128), f32),
            pltpu.VMEM((4, groups, 8, 128), f32),
            pltpu.VMEM((groups, 8, 128), f32),
            pltpu.VMEM((groups, 8, 128), f32),
            pltpu.VMEM((8, groups, 8, 128), f32),
            pltpu.VMEM((4, 8, 128), f32),
            pltpu.VMEM((8, 4, 8, 128), f32),
            pltpu.VMEM((2, 8, 128), f32),
            pltpu.VMEM((2, max(n_blocks, 16), 128), f32),
            dma((10,)),
            dma((46 + n_sums,)),
            dma((46 + n_sums,)),
            pltpu.SemaphoreType.REGULAR((len(ROUNDS),)),
        ],
        compiler_params=pltpu.CompilerParams(collective_id=0, has_side_effects=True),
    )(ocean_state, surface_height, surface_damping, land_mask)


def solution(mesh):
    n_blocks, n_group = mesh.shape["blocks"], mesh.shape["group"]
    inner = 8 if n_blocks % 8 == 0 and n_blocks > 8 else max(1, n_blocks // 2)
    placed = (
        P(None, None, "blocks", "group"),
        P("blocks", "group"),
        P("blocks", "group"),
        P("blocks", "group"),
    )
    return jax.shard_map(
        functools.partial(on_device, n_blocks, n_group, inner),
        mesh=mesh,
        in_specs=placed,
        out_specs=(P(None, None, "blocks", "group"), P("blocks", "group")),
        check_vma=False,
    )
```

```python
import functools

import jax
import jax.numpy as jnp
from jax import lax
from jax.experimental import pallas as pl
from jax.experimental.pallas import tpu as pltpu
from jax.sharding import PartitionSpec as P

MESH = pl.DeviceIdType.MESH

time_step = 0.25
hyper_visc = 0.025
mixing = 0.2
gravity = 4.0
rotation = 0.2

LOW, HIGH = 0.05, 9.0
REACH = 1.125

GROUP_LEVELS = 6
FLOW_LEVELS = 12
NEAR = ((-1, 0), (1, 0), (0, -1), (0, 1), (-1, -1), (-1, 1), (1, -1), (1, 1))
OPPOSITE = (1, 0, 3, 2, 7, 6, 5, 4)
UP, DOWN, LEFT, RIGHT, UP_LEFT, UP_RIGHT, DOWN_LEFT, DOWN_RIGHT = range(8)
FIRST = ((1, 2, 3), (2, 3))
ROUNDS = (((1, 2, 3), (3,)), ((1,), ()))


def roll(x, shift, axis):
    return pltpu.roll(x, shift % x.shape[axis], axis)


def two_sum(a, b):
    s = a + b
    t = s - a
    return s, (a - (s - t)) + (b - t)


def quick_sum(a, b):
    s = a + b
    return s, b - (s - a)


def split(a):
    c = 4097.0 * a
    high = c - (c - a)
    return high, a - high


def two_prod(a, b):
    p = a * b
    (ah, al), (bh, bl) = split(a), split(b)
    return p, ((ah * bh - p) + ah * bl + al * bh) + al * bl


def add(a, b):
    s, e = two_sum(a[0], b[0])
    return quick_sum(s, e + (a[1] + b[1]))


def scale(a, power_of_two):
    return a[0] * power_of_two, a[1] * power_of_two


def minus(a, b):
    return add(a, (-b[0], -b[1]))


def mul(a, b):
    p, e = two_prod(a[0], b[0])
    return quick_sum(p, e + (a[0] * b[1] + a[1] * b[0]))


def div(a, b):
    first = a[0] / b[0]
    rest = minus(a, mul(b, (first, jnp.zeros_like(first))))
    return quick_sum(first, rest[0] / b[0])


def sum_rows_of(x):
    parts = [(x[i : i + 8], None) for i in range(0, x.shape[0], 8)]
    while len(parts) > 1:
        parts = [join(*parts[i : i + 2]) for i in range(0, len(parts), 2)]
    part = parts[0]
    for shift in (4, 2, 1):
        other = (roll(part[0], shift, 0), None if part[1] is None else roll(part[1], shift, 0))
        part = join(part, other)
    return part


def join(a, b=None):
    if b is None:
        return a
    s, e = two_sum(a[0], b[0])
    for low in (a[1], b[1]):
        if low is not None:
            e = e + low
    return s, e


def kernel(
    n_blocks, n_group, inner,
    ocean, height, damping, land,
    out, surface,
    own, sea_int, geo, geo_near, rows_own, rows_near, rows_fix, packed, packed_near, corner_near, packed_fix,
    flow, flow_over, flow_side, flow_corner, sums_own, sums_near, rim, rim_near, row_out, rows_in,
    load_sems, send_sems, near_sems, sum_sems, greet_sems,
):
    levels = ocean.shape[0]
    groups = levels // GROUP_LEVELS
    flow_groups = levels // FLOW_LEVELS
    block = lax.axis_index("blocks")
    part = lax.axis_index("group")
    outer = n_blocks // inner

    def near(n):
        db, dg = NEAR[n]
        return (lax.rem(block + (n_blocks + db), n_blocks), lax.rem(part + (n_group + dg), n_group))

    base = (block // inner) * inner

    def along_blocks(distance):
        return (lax.rem(block + (distance % n_blocks), n_blocks), part)

    def along_group(distance):
        return (block, lax.rem(part + (distance % n_group), n_group))

    def far_first(n):
        return sorted(range(1, n), key=lambda s: -min(s, n - s))

    phases = [[along_blocks(s) for s in far_first(n_blocks)], [along_group(s) for s in far_first(n_group)]]

    def apart(rows, along):
        found = [along_blocks(sign * d * inner) for d in rows if d % outer for sign in (1, -1)]
        return found + [along_group(sign * d) for d in along if d % n_group for sign in (1, -1)]

    rounds = [apart(*reach) for reach in ROUNDS]

    loads = [
        pltpu.make_async_copy(land, sea_int, load_sems.at[0]),
        pltpu.make_async_copy(damping, geo.at[1], load_sems.at[1]),
        pltpu.make_async_copy(height, geo.at[2], load_sems.at[2]),
        pltpu.make_async_copy(ocean, own.at[1 : levels + 1], load_sems.at[3]),
        pltpu.make_async_copy(ocean.at[0], own.at[0], load_sems.at[4]),
        pltpu.make_async_copy(ocean.at[levels - 1], own.at[levels + 1], load_sems.at[5]),
    ]
    for side in range(2):
        for c in range(2):
            loads.append(
                pltpu.make_async_copy(
                    ocean.at[:, c + 2, 7 * side, :], rows_own.at[side, c], load_sems.at[6 + 2 * side + c]
                )
            )

    barrier = pltpu.get_barrier_semaphore()
    partners = (
        [near(n) for n in range(8)]
        + [(base + lax.rem(block - base + s, inner), part) for s in range(1, inner)]
        + apart(*FIRST)
    )
    for partner in partners:
        pl.semaphore_signal(barrier, inc=1, device_id=partner, device_id_type=MESH)
    for load in loads:
        load.start()

    row = lax.broadcasted_iota(jnp.int32, (8, 128), 0)
    lane = lax.broadcasted_iota(jnp.int32, (8, 128), 1)
    first_row, last_row = row == 0, row == 7
    first_lane, last_lane = lane == 0, lane == 127
    quarter = lax.rem(lane, 4)
    field_of = lane // 4
    zero = jnp.zeros((8, 128), jnp.float32)

    def flag(condition):
        return jnp.where(condition, jnp.float32(1.0), jnp.float32(0.0))

    has_up, has_down = flag(block > 0), flag(block < n_blocks - 1)
    has_left, has_right = flag(part > 0), flag(part < n_group - 1)
    exists = (
        has_up, has_down, has_left, has_right,
        has_up * has_left, has_up * has_right, has_down * has_left, has_down * has_right,
    )

    sends = []

    def send(source, target, partner):
        copy = pltpu.make_async_remote_copy(
            src_ref=source, dst_ref=target, send_sem=send_sems.at[len(sends)], recv_sem=near_sems.at[len(sends)],
            device_id=partner, device_id_type=MESH,
        )
        copy.start()
        sends.append(copy)
        return copy

    def greet(n):
        for target in rounds[n]:
            pl.semaphore_signal(greet_sems.at[n], inc=1, device_id=target, device_id_type=MESH)

    def greeted(n):
        if rounds[n]:
            pl.semaphore_wait(greet_sems.at[n], len(rounds[n]))

    def send_rows(c, r):
        return [
            send(ocean.at[:, c, r, :], rows_near.at[1, r, c], near(UP)),
            send(ocean.at[:, c, 7 - r, :], rows_near.at[0, r, c], near(DOWN)),
        ]

    for load in loads[:3]:
        load.wait()
    sea = sea_int[...].astype(jnp.float32)
    geo[0] = sea

    for load in loads[3:]:
        load.wait()

    for group in range(flow_groups):
        west, east = [zero, zero], [zero, zero]
        for i in range(2 * FLOW_LEVELS):
            field = roll(own[group * FLOW_LEVELS + (i // 2 + 1), 2 + i % 2] * sea, 4 * i + 4, 1)
            east[i % 2] = jnp.where(field_of == i, field, east[i % 2])
            west[i % 2] = jnp.where(field_of == i + 1, field, west[i % 2])
        flow[0, group] = roll(west[0] + west[1], -4, 1)
        flow[1, group] = east[0] + east[1]

    not_first, not_last = flag(row > 0), flag(row < 7)

    def advection(level, carry):
        u, v = own[level + 1, 2] * sea, own[level + 1, 3] * sea
        east, north = (0.5 * time_step) * u, (0.5 * time_step) * v
        terms = []
        for g in (u, v):
            along = not_last * roll(g, -1, 0) - not_first * roll(g, 1, 0)
            across = jnp.where(last_lane, 0.0, roll(g, -1, 1)) - jnp.where(first_lane, 0.0, roll(g, 1, 1))
            terms.append(east * along + north * across)
        return carry[0] + u, carry[1] + v, carry[2] + terms[0], carry[3] + terms[1]

    for n, total in enumerate(lax.fori_loop(0, levels, advection, (zero, zero, zero, zero), unroll=4)):
        sums_own[n] = total

    held = zero
    for n, plane in enumerate((sea, geo[1], geo[2], sums_own[0], sums_own[1], sums_own[2], sums_own[3])):
        held = jnp.where(lane // 16 == n, roll(plane, 16 * n + 8, 1), held)
    rim[...] = held

    pl.semaphore_wait(barrier, len(partners))
    greet(0)
    halves = {-1: pl.ds(0, 4), 1: pl.ds(4, 4)}
    beside = []
    for n in (UP_LEFT, UP_RIGHT, DOWN_LEFT, DOWN_RIGHT):
        rows, edge = halves[NEAR[n][0]], max(NEAR[n][1], 0)
        beside.append(send(rim, rim_near.at[OPPOSITE[n] - 2], near(n)))
        beside.append(
            send(flow.at[edge, :, rows, :], flow_corner.at[OPPOSITE[n] - 4, :, rows, :], near(n))
        )
    for n in (DOWN, UP):
        rows = halves[NEAR[n][0]]
        beside.append(send(geo, geo_near.at[OPPOSITE[n]], near(n)))
        beside.append(send(sums_own, sums_near.at[OPPOSITE[n]], near(n)))
        beside.append(send(flow.at[:, :, rows, :], flow_over.at[OPPOSITE[n], :, :, rows, :], near(n)))
    for n in (LEFT, RIGHT):
        beside.append(send(rim, rim_near.at[OPPOSITE[n] - 2], near(n)))
        beside.append(send(flow.at[max(NEAR[n][1], 0)], flow_side.at[OPPOSITE[n] - 2], near(n)))
    flow_rows = send_rows(2, 0) + send_rows(3, 0)

    sea_packed = jnp.where(lane < 4, roll(sea, 2, 1), 0.0)
    for shift in (4, 8, 16, 32, 64):
        sea_packed = sea_packed + roll(sea_packed, shift, 1)

    @pl.loop(0, groups)
    def _(group):
        held = [zero, zero, zero]
        for i in range(4 * GROUP_LEVELS):
            field = own[group * GROUP_LEVELS + (i // 4 + 1), i % 4]
            held[i % 3] = jnp.where(field_of == i, roll(field, 2 + 4 * i, 1), held[i % 3])
        packed[group] = (held[0] + held[1] + held[2]) * sea_packed

    sides = [send(packed, packed_near.at[OPPOSITE[n] - 2], near(n)) for n in (LEFT, RIGHT)]
    corners = []
    for n in (UP_LEFT, UP_RIGHT, DOWN_LEFT, DOWN_RIGHT):
        edge = 0 if NEAR[n][0] < 0 else 7
        corners.append(
            send(packed.at[:, edge : edge + 1, :], corner_near.at[OPPOSITE[n] - 4, :, 0:1, :], near(n))
        )
    other_rows = send_rows(2, 1) + send_rows(3, 1)
    for c in (0, 1):
        other_rows += send_rows(c, 0) + send_rows(c, 1)
    column = (part * 128 + lane).astype(jnp.float32)
    coriolis = (rotation * time_step) * (2.0 * (column + 0.5) / (128 * n_group) - 1.0)
    middle = 2.0 - jnp.where(first_row, 1.0 - has_up, 0.0) - jnp.where(last_row, 1.0 - has_down, 0.0)
    def step(level, carry):
        above, now = carry
        below = tuple(own[level + 2, c] * sea for c in range(4))
        u, v = now[2], now[3]
        east, north = (0.5 * time_step) * u, (0.5 * time_step) * v
        for c in range(4):
            g = now[c]
            n1, s1 = not_first * roll(g, 1, 0), not_last * roll(g, -1, 0)
            n2, s2 = not_first * roll(n1, 1, 0), not_last * roll(s1, -1, 0)
            west = jnp.where(first_lane, 0.0, roll(g, 1, 1))
            east_of = jnp.where(last_lane, 0.0, roll(g, -1, 1))
            twice = 2.0 * (n1 + s1) + (west + east_of) - 4.0 * g
            biharm = (
                (n2 + s2)
                + middle * g
                - 4.0 * twice
                + jnp.where(first_lane, 0.0, roll(twice, 1, 1))
                + jnp.where(last_lane, 0.0, roll(twice, -1, 1))
            )
            advect = east * (s1 - n1) + north * (east_of - west)
            vertical = above[c] + below[c] - 2.0 * g
            new = g - advect - hyper_visc * biharm + mixing * vertical
            if c == 2:
                new = new + coriolis * v
            elif c == 3:
                new = new - coriolis * u
            new = new * sea
            out[level, c] = new
        return now, below

    top = tuple(own[0, c] * sea for c in range(4))
    now = tuple(own[1, c] * sea for c in range(4))
    half = levels // 2
    middle_pair = lax.fori_loop(0, half, step, (top, now))
    greeted(0)
    greet(1)
    lax.fori_loop(half, levels, step, middle_pair)

    for copy in beside + flow_rows:
        copy.wait_recv()

    low = row < 4
    before = lax.rem(lane, 16) < 8
    rims = [rim_near[n - 2] * exists[n] for n in range(2, 8)]
    rim_side = jnp.where(before, rims[LEFT - 2], rims[RIGHT - 2])
    rim_down = jnp.where(before, rims[DOWN_LEFT - 2], rims[DOWN_RIGHT - 2])
    rim_up = jnp.where(before, rims[UP_LEFT - 2], rims[UP_RIGHT - 2])
    rim_over = jnp.where(low, rim_down, rim_up)

    def edge_of(x, plane):
        return jnp.where((lane < 8) | (lane >= 120), roll(x, -(16 * plane + 8), 1), 0.0)

    def stack(*pairs):
        return jnp.concatenate([jnp.concatenate(pair, axis=1) for pair in pairs], axis=0)

    def around(mine, up, down, plane):
        return stack(
            (mine, edge_of(rim_side, plane)), (jnp.where(low, down, up), edge_of(rim_over, plane))
        )

    sea_all = around(sea, geo_near[UP, 0] * has_up, geo_near[DOWN, 0] * has_down, 0)
    damping_all = around(geo[1], geo_near[UP, 1], geo_near[DOWN, 1], 1)
    forced = sea_all * damping_all * around(geo[2], geo_near[UP, 2], geo_near[DOWN, 2], 2)

    def around_whole(m):
        plane = m + 3
        return stack(
            (sums_own[m], edge_of(rim_side, plane)),
            (sums_near[DOWN, m] * has_down, edge_of(rim_down, plane)),
            (sums_near[UP, m] * has_up, edge_of(rim_up, plane)),
        )

    def ring_laplace(x):
        return (roll(x, 1, 0) + roll(x, -1, 0)) + (roll(x, 1, 1) + roll(x, -1, 1)) - 4.0 * x

    def beside_exists(left, right):
        return jnp.where(lane < 64, zero + right, zero + left)

    inside = stack(
        (zero + 1.0, beside_exists(has_left, has_right)),
        (zero + has_down, beside_exists(exists[DOWN_LEFT], exists[DOWN_RIGHT])),
        (zero + has_up, beside_exists(exists[UP_LEFT], exists[UP_RIGHT])),
    )
    ring_lane = lax.broadcasted_iota(jnp.int32, (24, 256), 1)
    ring_column = (part * 128 + jnp.where(ring_lane < 192, ring_lane, ring_lane - 256)).astype(jnp.float32)
    ring_coriolis = (rotation * time_step) * (2.0 * (ring_column + 0.5) / (128 * n_group) - 1.0)
    level_sums = [around_whole(m) for m in range(2)]
    linear = []
    for m in range(2):
        g = level_sums[m]
        linear.append(
            (g - hyper_visc * ring_laplace(inside * ring_laplace(g)))
            + (ring_coriolis if m == 0 else -ring_coriolis) * level_sums[1 - m]
        )

    is_east_field = lax.rem(field_of, 2) == 0
    first, last = flag(first_row), flag(last_row)
    at_first, at_last = flag(quarter == 0), flag(quarter == 3)

    def of_u(x):
        x = jnp.where(is_east_field, x, 0.0)
        return x + roll(x, 4, 1)

    def of_v(x):
        x = jnp.where(is_east_field, 0.0, x)
        return x + roll(x, -4, 1)

    def across_rows(x, beside):
        return of_u(x) * (last * roll(beside, -1, 0) - first * roll(beside, 1, 0))

    def meet_after(x, after):
        return of_v(x) * (at_last * roll(after, 3, 1))

    def meet_before(x, ahead):
        return of_v(x) * (-at_first * roll(ahead, -3, 1))

    gathered = [zero] * 8
    for group in range(flow_groups):
        mine = flow[0, group], flow[1, group]
        over = [
            jnp.where(low, flow_over[DOWN, e, group] * has_down, flow_over[UP, e, group] * has_up) for e in range(2)
        ]
        left, right = flow_side[0, group] * has_left, flow_side[1, group] * has_right
        corner = [flow_corner[n - 4, group] * exists[n] for n in range(4, 8)]
        over_left = jnp.where(low, corner[DOWN_LEFT - 4], corner[UP_LEFT - 4])
        over_right = jnp.where(low, corner[DOWN_RIGHT - 4], corner[UP_RIGHT - 4])
        terms = (
            meet_before(mine[0], left),
            meet_after(mine[1], right),
            meet_before(right, mine[1]) + across_rows(right, over_right),
            meet_after(left, mine[0]) + across_rows(left, over_left),
            meet_before(over[0], over_left),
            meet_after(over[1], over_right),
            meet_before(over_right, over[1]) + across_rows(over_right, right),
            meet_after(over_left, over[0]) + across_rows(over_left, left),
        )
        gathered = [a + b for a, b in zip(gathered, terms)]

    def over_levels(x):
        x = x + roll(x, -48, 1)
        x = x + roll(x, -24, 1)
        return x + (roll(x, -8, 1) + roll(x, -16, 1))

    gathered = [over_levels(x) for x in gathered]

    def placed(n, c):
        return jnp.where(lane < 4, roll(gathered[n], -4 * c, 1), 0.0) + jnp.where(
            lane >= 124, roll(gathered[n + 1], -4 * c - 4, 1), 0.0
        )

    edges = [[placed(2 * n, c) for c in range(2)] for n in range(4)]

    def met(x, g, weight):
        return jnp.broadcast_to(jnp.sum(x * g, axis=0, keepdims=True) * weight, (8, 128))

    above_weight = geo[0, 0:1, :] * (geo_near[UP, 0, 7:8, :] * has_up)
    below_weight = geo[0, 7:8, :] * (geo_near[DOWN, 0, 0:1, :] * has_down)
    advected = []
    for m in range(2):
        up_g, down_g = rows_near[0, 0, 2 + m], rows_near[1, 0, 2 + m]
        inner_rows = last * met(rows_own[1, 0], down_g, below_weight) - first * met(rows_own[0, 0], up_g, above_weight)
        outer_rows = last * met(rows_near[0, 0, 2], rows_own[0, m], above_weight) - first * met(
            rows_near[1, 0, 2], rows_own[1, m], below_weight
        )
        crossing = stack((edges[0][m] + inner_rows, edges[1][m]), (edges[2][m] + outer_rows, edges[3][m]))
        advected.append(
            around(sums_own[2 + m], sums_near[UP, 2 + m], sums_near[DOWN, 2 + m], 5 + m)
            + (0.5 * time_step) * crossing
        )

    ring_low = lax.broadcasted_iota(jnp.int32, (8, 256), 0) < 4
    transport = []
    for m in range(2):
        nearest = jnp.concatenate(
            [linear[m][0:8], jnp.where(ring_low, linear[m][8:16], linear[m][16:24])], axis=0
        )
        transport.append(sea_all * ((nearest - advected[m]) / levels))
    east_all, north_all = transport
    own_part = sea_all * ((damping_all - 0.5) * 0.25)
    own_split = split(own_part)
    beside_part = sea_all * -0.25

    divergence = 0.5 * (roll(east_all, -1, 0) - roll(east_all, 1, 0) + roll(north_all, -1, 1) - roll(north_all, 1, 1))
    v0 = forced - (gravity * sea_all) * divergence

    def finish_state():
        own_flow = []
        for group in range(groups):
            north = jnp.where(lax.rem(field_of, 4) == 3, packed[group], 0.0)
            north = north + roll(north, -4, 1)
            own_flow.append((0.5 * time_step) * (north + roll(north, -8, 1)))

        for copy in sides + corners + other_rows:
            copy.wait_recv()

        sea_rows = (
            (geo_near[UP, 0, 7:8, :] * has_up, geo_near[UP, 0, 6:7, :] * has_up),
            (geo_near[DOWN, 0, 0:1, :] * has_down, geo_near[DOWN, 0, 1:2, :] * has_down),
        )
        own_rows = ((geo[0, 0:1, :], geo[0, 1:2, :]), (geo[0, 7:8, :], geo[0, 6:7, :]))
        edge_lane = lax.broadcasted_iota(jnp.int32, (levels, 128), 1)
        no_west, no_east = edge_lane == 0, edge_lane == 127

        def fix_rows(c):
            for side in range(2):
                outer_sign = (0.5 * time_step) if side == 0 else -(0.5 * time_step)
                a = rows_near[side, 0, c] * sea_rows[side][0]
                b = rows_near[side, 1, c] * sea_rows[side][1]
                across = jnp.where(no_west, 0.0, roll(a, 1, 1)) + jnp.where(no_east, 0.0, roll(a, -1, 1))
                nearest = (
                    -hyper_visc * (b - 8.0 * a + 2.0 * across) + (outer_sign * own_rows[side][0]) * rows_own[side, 0] * a
                ) * own_rows[side][0]
                second = (-hyper_visc * a) * own_rows[side][1]
                rows_fix[side, 0, c] = nearest
                rows_fix[side, 1, c] = second

        def fix_columns(group):
            mine = packed[group]
            left = packed_near[0, group] * has_left
            right = packed_near[1, group] * has_right
            left_rows = not_first * roll(left, 1, 0) + not_last * roll(left, -1, 0)
            right_rows = not_first * roll(right, 1, 0) + not_last * roll(right, -1, 0)
            at_left = 2.0 * left_rows + roll(left, 1, 1) + has_left * roll(mine, -1, 1) - 8.0 * left
            at_right = 2.0 * right_rows + roll(right, -1, 1) + has_right * roll(mine, 1, 1) - 8.0 * right
            swept = own_flow[group]
            fixed = jnp.where(
                quarter == 0,
                -hyper_visc * roll(right, -2, 1),
                jnp.where(
                    quarter == 1,
                    -hyper_visc * roll(at_right, -1, 1) - swept * roll(right, -1, 1),
                    jnp.where(
                        quarter == 2,
                        -hyper_visc * roll(at_left, 1, 1) + swept * roll(left, 1, 1),
                        -hyper_visc * roll(left, 2, 1),
                    ),
                ),
            )
            return fixed * sea_packed

        beside_edges = (lane < 2) | (lane >= 126)
        for group in range(groups):
            packed_fix[group] = fix_columns(group)
        for c in range(4):
            fix_rows(c)

        def finish(group, carry):
            def at_corner(n):
                return jnp.broadcast_to(corner_near[n - 4, group, 0:1, :] * exists[n], (8, 128))

            left_corner = jnp.where(first_row, at_corner(UP_LEFT), jnp.where(last_row, at_corner(DOWN_LEFT), 0.0))
            right_corner = jnp.where(first_row, at_corner(UP_RIGHT), jnp.where(last_row, at_corner(DOWN_RIGHT), 0.0))
            corner = jnp.where(
                quarter == 1, roll(right_corner, -1, 1), jnp.where(quarter == 2, roll(left_corner, 1, 1), 0.0)
            )
            fixed = packed_fix[group] - (2.0 * hyper_visc) * corner * sea_packed
            for i in range(4 * GROUP_LEVELS):
                level, c = group * GROUP_LEVELS + i // 4, i % 4
                first, second, last, before_last = (
                    jnp.broadcast_to(rows_fix[side, r, c, pl.ds(level, 1), :], (8, 128))
                    for side in range(2)
                    for r in range(2)
                )
                by_rows = jnp.where(
                    first_row,
                    first,
                    jnp.where(row == 1, second, jnp.where(last_row, last, jnp.where(row == 6, before_last, 0.0))),
                )
                by_columns = jnp.where(beside_edges, roll(fixed, -(4 * i + 2), 1), 0.0)
                out[level, c] = out[level, c] + by_rows + by_columns
            return carry

        lax.fori_loop(0, groups, finish, 0)

    def apply(s):
        high, low = s
        up, down = (roll(high, 1, 0), low if low is None else roll(low, 1, 0)), (roll(high, -1, 0), low if low is None else roll(low, -1, 0))
        west, east = (roll(high, 1, 1), low if low is None else roll(low, 1, 1)), (roll(high, -1, 1), low if low is None else roll(low, -1, 1))
        total = join(join(up, down), join(west, east))
        high_split = split(high)
        p = own_part * high
        (ah, al), (bh, bl) = own_split, high_split
        e = ((ah * bh - p) + ah * bl + al * bh) + al * bl
        if low is not None:
            e = e + own_part * low
        return add((p, e), (beside_part * total[0], beside_part * total[1]))

    v1 = apply((v0, None))
    v2 = apply(v1)
    v3 = apply(v2)
    v0 = v0[0:8, 0:128]
    v1, v2, v3 = (tuple(x[0:8, 0:128] for x in v) for v in (v1, v2, v3))
    v0 = (v0, zero)

    high, low = zero, zero
    for m, (a, b) in enumerate(((v0, v0), (v0, v1), (v1, v1), (v1, v2), (v2, v2), (v2, v3))):
        p, e = two_prod(a[0], b[0])
        e = e + (a[0] * b[1] + a[1] * b[0])
        part_sum = (p, e)
        for shift in (4, 2, 1):
            part_sum = join(part_sum, (roll(part_sum[0], shift, 0), roll(part_sum[1], shift, 0)))
        high = jnp.where(row == m, part_sum[0], high)
        low = jnp.where(row == m, part_sum[1], low)
    total = (high, low)
    for shift in (64, 32, 16, 8, 4, 2, 1):
        total = join(total, (roll(total[0], shift, 1), roll(total[1], shift, 1)))
    value = jnp.sum(
        jnp.where(lane == row, total[0], jnp.where(lane == row + 64, total[1], 0.0)), axis=0, keepdims=True
    )

    greeted(1)
    for number, phase in enumerate(phases):
        count = len(phase)
        size = -(-(count + 1) // 8) * 8
        row_out[number, 0:1, :] = value
        for s, partner in enumerate(phase):
            copy = pltpu.make_async_remote_copy(
                src_ref=row_out.at[number, 0:1, :], dst_ref=rows_in.at[number, s : s + 1, :],
                send_sem=send_sems.at[len(sends)], recv_sem=sum_sems.at[number],
                device_id=partner, device_id_type=MESH,
            )
            copy.start()
            sends.append(copy)
        if number == 0:
            finish_state()
        whole = rows_in.at[number, 0:count, :]
        pltpu.make_async_copy(whole, whole, sum_sems.at[number]).wait()
        got = rows_in[number, 0:size, :]
        row_number = lax.broadcasted_iota(jnp.int32, (size, 128), 0)
        got = jnp.where(row_number < count, got, jnp.where(row_number == count, row_out[number, 0:1, :], 0.0))
        summed, lost = sum_rows_of(got)
        value = jnp.where(lane < 64, summed, summed + roll(lost, 64, 1))[0:1, :]

    spread = jnp.broadcast_to(value, (8, 128))

    def pick(m):
        return jnp.sum(jnp.where(lane == m, spread, 0.0), axis=1, keepdims=True)

    mu = [quick_sum(pick(m), pick(64 + m)) for m in range(6)]
    surface[...] = combine(mu, v0, v1, v2)

    for copy in sends:
        copy.wait_send()


def combine(mu, v0, v1, v2):
    a = [add(scale(add(mu[k], mu[k + 1]), 4.0), scale(mu[k], 0.5)) for k in range(5)]
    l1, l2 = div(a[1], a[0]), div(a[2], a[0])
    s11 = minus(a[2], mul(l1, a[1]))
    s12 = minus(a[3], mul(l1, a[2]))
    s22 = minus(a[4], mul(l2, a[2]))
    y1 = minus(mu[1], mul(l1, mu[0]))
    y2 = minus(mu[2], mul(l2, mu[0]))
    sound = s11[0] > 0.0
    one = jnp.ones_like(s11[0])
    none = jnp.zeros_like(s11[0])
    s11 = (jnp.where(sound, s11[0], one), jnp.where(sound, s11[1], none))
    l21 = div(s12, s11)
    inside = sound & (jnp.abs(l21[0] - l1[0]) <= REACH)
    bounded = jnp.clip(l21[0], l1[0] - REACH, l1[0] + REACH)
    l21 = (
        jnp.where(sound, jnp.where(inside, l21[0], bounded), l1[0]),
        jnp.where(sound, jnp.where(inside, l21[1], none), l1[1]),
    )
    t22 = minus(s22, mul(l21, s12))
    z2 = minus(y2, mul(l21, y1))

    def step_of(quotient):
        return jnp.clip(quotient, 1.0 / HIGH, 1.0 / LOW)

    alpha0 = step_of(mu[0][0] / a[0][0])
    alpha1 = step_of(y1[0] / (s11[0] * (-4.0 * alpha0)))
    firm = t22[0] > 0.0
    alpha2 = step_of(z2[0] / (jnp.where(firm, t22[0], one) * (16.0 * alpha0 * alpha1)))

    def wide(pair):
        return tuple(jnp.broadcast_to(x, v0[0].shape) for x in pair)

    l1, l2, l21 = wide(l1), wide(l2), wide(l21)
    p1 = minus(v1, mul(l1, v0))
    p2 = minus(v2, add(mul(l2, v0), mul(l21, p1)))
    return alpha0 * (v0[0] + alpha1 * (-4.0 * p1[0] + (16.0 * alpha2) * p2[0]))


def on_device(n_blocks, n_group, inner, ocean_state, surface_height, surface_damping, land_mask):
    levels = ocean_state.shape[0]
    groups = levels // GROUP_LEVELS
    flow_groups = levels // FLOW_LEVELS
    f32 = jnp.float32
    any_space = pl.BlockSpec(memory_space=pl.ANY)
    vmem = pl.BlockSpec(memory_space=pltpu.VMEM)
    n_sums = (n_blocks - 1) + (n_group - 1)
    dma = pltpu.SemaphoreType.DMA
    return pl.pallas_call(
        functools.partial(kernel, n_blocks, n_group, inner),
        out_shape=(pltpu.VMEM(ocean_state.shape, f32), pltpu.VMEM(surface_height.shape, f32)),
        in_specs=[any_space] * 4,
        out_specs=(vmem, vmem),
        scratch_shapes=[
            pltpu.VMEM((levels + 2, 4, 8, 128), f32),
            pltpu.VMEM((8, 128), jnp.int32),
            pltpu.VMEM((3, 8, 128), f32),
            pltpu.VMEM((2, 3, 8, 128), f32),
            pltpu.VMEM((2, 2, levels, 128), f32),
            pltpu.VMEM((2, 2, 4, levels, 128), f32),
            pltpu.VMEM((2, 2, 4, levels, 128), f32),
            pltpu.VMEM((groups, 8, 128), f32),
            pltpu.VMEM((2, groups, 8, 128), f32),
            pltpu.VMEM((4, groups, 8, 128), f32),
            pltpu.VMEM((groups, 8, 128), f32),
            pltpu.VMEM((2, flow_groups, 8, 128), f32),
            pltpu.VMEM((2, 2, flow_groups, 8, 128), f32),
            pltpu.VMEM((2, flow_groups, 8, 128), f32),
            pltpu.VMEM((4, flow_groups, 8, 128), f32),
            pltpu.VMEM((4, 8, 128), f32),
            pltpu.VMEM((2, 4, 8, 128), f32),
            pltpu.VMEM((8, 128), f32),
            pltpu.VMEM((6, 8, 128), f32),
            pltpu.VMEM((2, 8, 128), f32),
            pltpu.VMEM((2, max(n_blocks, 16), 128), f32),
            dma((10,)),
            dma((40 + n_sums,)),
            dma((40,)),
            dma((2,)),
            pltpu.SemaphoreType.REGULAR((len(ROUNDS),)),
        ],
        compiler_params=pltpu.CompilerParams(collective_id=0, has_side_effects=True),
    )(ocean_state, surface_height, surface_damping, land_mask)


def solution(mesh):
    n_blocks, n_group = mesh.shape["blocks"], mesh.shape["group"]
    inner = 8 if n_blocks % 8 == 0 and n_blocks > 8 else max(1, n_blocks // 2)
    placed = (
        P(None, None, "blocks", "group"),
        P("blocks", "group"),
        P("blocks", "group"),
        P("blocks", "group"),
    )
    return jax.shard_map(
        functools.partial(on_device, n_blocks, n_group, inner),
        mesh=mesh,
        in_specs=placed,
        out_specs=(P(None, None, "blocks", "group"), P("blocks", "group")),
        check_vma=False,
    )
```

```python
import functools

import jax
import jax.numpy as jnp
from jax import lax
from jax.experimental import pallas as pl
from jax.experimental.pallas import tpu as pltpu
from jax.sharding import PartitionSpec as P

MESH = pl.DeviceIdType.MESH

time_step = 0.25
hyper_visc = 0.025
mixing = 0.2
gravity = 4.0
rotation = 0.2

LOW, HIGH = 0.05, 9.0
REACH = 1.125

GROUP_LEVELS = 6
FLOW_LEVELS = 12
NEAR = ((-1, 0), (1, 0), (0, -1), (0, 1), (-1, -1), (-1, 1), (1, -1), (1, 1))
OPPOSITE = (1, 0, 3, 2, 7, 6, 5, 4)
UP, DOWN, LEFT, RIGHT, UP_LEFT, UP_RIGHT, DOWN_LEFT, DOWN_RIGHT = range(8)
FIRST = ((1, 2, 3), (2, 3))
ROUNDS = (((1, 2, 3), (3,)), ((1,), ()))


def roll(x, shift, axis):
    return pltpu.roll(x, shift % x.shape[axis], axis)


def two_sum(a, b):
    s = a + b
    t = s - a
    return s, (a - (s - t)) + (b - t)


def quick_sum(a, b):
    s = a + b
    return s, b - (s - a)


def split(a):
    c = 4097.0 * a
    high = c - (c - a)
    return high, a - high


def two_prod(a, b):
    p = a * b
    (ah, al), (bh, bl) = split(a), split(b)
    return p, ((ah * bh - p) + ah * bl + al * bh) + al * bl


def add(a, b):
    s, e = two_sum(a[0], b[0])
    return quick_sum(s, e + (a[1] + b[1]))


def scale(a, power_of_two):
    return a[0] * power_of_two, a[1] * power_of_two


def minus(a, b):
    return add(a, (-b[0], -b[1]))


def mul(a, b):
    p, e = two_prod(a[0], b[0])
    return quick_sum(p, e + (a[0] * b[1] + a[1] * b[0]))


def div(a, b):
    first = a[0] / b[0]
    rest = minus(a, mul(b, (first, jnp.zeros_like(first))))
    return quick_sum(first, rest[0] / b[0])


def sum_rows_of(x):
    parts = [(x[i : i + 8], None) for i in range(0, x.shape[0], 8)]
    while len(parts) > 1:
        parts = [join(*parts[i : i + 2]) for i in range(0, len(parts), 2)]
    part = parts[0]
    for shift in (4, 2, 1):
        other = (roll(part[0], shift, 0), None if part[1] is None else roll(part[1], shift, 0))
        part = join(part, other)
    return part


def join(a, b=None):
    if b is None:
        return a
    s, e = two_sum(a[0], b[0])
    for low in (a[1], b[1]):
        if low is not None:
            e = e + low
    return s, e


def kernel(
    n_blocks, n_group, inner,
    ocean, height, damping, land,
    out, surface,
    own, sea_int, geo, geo_near, rows_own, rows_near, rows_fix, packed, packed_near, corner_near, packed_fix,
    flow, flow_over, flow_side, flow_corner, sums_own, sums_near, rim, rim_near, row_out, rows_in,
    load_sems, send_sems, near_sems, sum_sems, greet_sems,
):
    levels = ocean.shape[0]
    groups = levels // GROUP_LEVELS
    flow_groups = levels // FLOW_LEVELS
    block = lax.axis_index("blocks")
    part = lax.axis_index("group")
    outer = n_blocks // inner

    def near(n):
        db, dg = NEAR[n]
        return (lax.rem(block + (n_blocks + db), n_blocks), lax.rem(part + (n_group + dg), n_group))

    base = (block // inner) * inner

    def along_blocks(distance):
        return (lax.rem(block + (distance % n_blocks), n_blocks), part)

    def along_group(distance):
        return (block, lax.rem(part + (distance % n_group), n_group))

    def far_first(n):
        return sorted(range(1, n), key=lambda s: -min(s, n - s))

    phases = [[along_blocks(s) for s in far_first(n_blocks)], [along_group(s) for s in far_first(n_group)]]

    def apart(rows, along):
        found = [along_blocks(sign * d * inner) for d in rows if d % outer for sign in (1, -1)]
        return found + [along_group(sign * d) for d in along if d % n_group for sign in (1, -1)]

    rounds = [apart(*reach) for reach in ROUNDS]

    loads = [
        pltpu.make_async_copy(land, sea_int, load_sems.at[0]),
        pltpu.make_async_copy(damping, geo.at[1], load_sems.at[1]),
        pltpu.make_async_copy(height, geo.at[2], load_sems.at[2]),
        pltpu.make_async_copy(ocean, own.at[1 : levels + 1], load_sems.at[3]),
        pltpu.make_async_copy(ocean.at[0], own.at[0], load_sems.at[4]),
        pltpu.make_async_copy(ocean.at[levels - 1], own.at[levels + 1], load_sems.at[5]),
    ]
    for side in range(2):
        for c in range(2):
            loads.append(
                pltpu.make_async_copy(
                    ocean.at[:, c + 2, 7 * side, :], rows_own.at[side, c], load_sems.at[6 + 2 * side + c]
                )
            )

    barrier = pltpu.get_barrier_semaphore()
    partners = (
        [near(n) for n in range(8)]
        + [(base + lax.rem(block - base + s, inner), part) for s in range(1, inner)]
        + apart(*FIRST)
    )
    for partner in partners:
        pl.semaphore_signal(barrier, inc=1, device_id=partner, device_id_type=MESH)
    for load in loads:
        load.start()

    row = lax.broadcasted_iota(jnp.int32, (8, 128), 0)
    lane = lax.broadcasted_iota(jnp.int32, (8, 128), 1)
    first_row, last_row = row == 0, row == 7
    first_lane, last_lane = lane == 0, lane == 127
    quarter = lax.rem(lane, 4)
    field_of = lane // 4
    zero = jnp.zeros((8, 128), jnp.float32)

    def flag(condition):
        return jnp.where(condition, jnp.float32(1.0), jnp.float32(0.0))

    has_up, has_down = flag(block > 0), flag(block < n_blocks - 1)
    has_left, has_right = flag(part > 0), flag(part < n_group - 1)
    exists = (
        has_up, has_down, has_left, has_right,
        has_up * has_left, has_up * has_right, has_down * has_left, has_down * has_right,
    )

    sends = []

    def send(source, target, partner):
        copy = pltpu.make_async_remote_copy(
            src_ref=source, dst_ref=target, send_sem=send_sems.at[len(sends)], recv_sem=near_sems.at[len(sends)],
            device_id=partner, device_id_type=MESH,
        )
        copy.start()
        sends.append(copy)
        return copy

    def greet(n):
        for target in rounds[n]:
            pl.semaphore_signal(greet_sems.at[n], inc=1, device_id=target, device_id_type=MESH)

    def greeted(n):
        if rounds[n]:
            pl.semaphore_wait(greet_sems.at[n], len(rounds[n]))

    def send_rows(c, r):
        return [
            send(ocean.at[:, c, r, :], rows_near.at[1, r, c], near(UP)),
            send(ocean.at[:, c, 7 - r, :], rows_near.at[0, r, c], near(DOWN)),
        ]

    for load in loads[:3]:
        load.wait()
    sea = sea_int[...].astype(jnp.float32)
    geo[0] = sea

    for load in loads[3:]:
        load.wait()

    for group in range(flow_groups):
        west, east = [zero, zero], [zero, zero]
        for i in range(2 * FLOW_LEVELS):
            field = roll(own[group * FLOW_LEVELS + (i // 2 + 1), 2 + i % 2] * sea, 4 * i + 4, 1)
            east[i % 2] = jnp.where(field_of == i, field, east[i % 2])
            west[i % 2] = jnp.where(field_of == i + 1, field, west[i % 2])
        flow[0, group] = roll(west[0] + west[1], -4, 1)
        flow[1, group] = east[0] + east[1]

    not_first, not_last = flag(row > 0), flag(row < 7)

    def advection(level, carry):
        u, v = own[level + 1, 2] * sea, own[level + 1, 3] * sea
        east, north = (0.5 * time_step) * u, (0.5 * time_step) * v
        terms = []
        for g in (u, v):
            along = not_last * roll(g, -1, 0) - not_first * roll(g, 1, 0)
            across = jnp.where(last_lane, 0.0, roll(g, -1, 1)) - jnp.where(first_lane, 0.0, roll(g, 1, 1))
            terms.append(east * along + north * across)
        return carry[0] + u, carry[1] + v, carry[2] + terms[0], carry[3] + terms[1]

    for n, total in enumerate(lax.fori_loop(0, levels, advection, (zero, zero, zero, zero), unroll=4)):
        sums_own[n] = total

    held = zero
    for n, plane in enumerate((sea, geo[1], geo[2], sums_own[0], sums_own[1], sums_own[2], sums_own[3])):
        held = jnp.where(lane // 16 == n, roll(plane, 16 * n + 8, 1), held)
    rim[...] = held

    pl.semaphore_wait(barrier, len(partners))
    greet(0)
    halves = {-1: pl.ds(0, 4), 1: pl.ds(4, 4)}
    beside = []
    for n in (UP_LEFT, UP_RIGHT, DOWN_LEFT, DOWN_RIGHT):
        rows, edge = halves[NEAR[n][0]], max(NEAR[n][1], 0)
        beside.append(send(rim, rim_near.at[OPPOSITE[n] - 2], near(n)))
        beside.append(
            send(flow.at[edge, :, rows, :], flow_corner.at[OPPOSITE[n] - 4, :, rows, :], near(n))
        )
    for n in (DOWN, UP):
        rows = halves[NEAR[n][0]]
        beside.append(send(geo, geo_near.at[OPPOSITE[n]], near(n)))
        beside.append(send(sums_own, sums_near.at[OPPOSITE[n]], near(n)))
        beside.append(send(flow.at[:, :, rows, :], flow_over.at[OPPOSITE[n], :, :, rows, :], near(n)))
    for n in (LEFT, RIGHT):
        beside.append(send(rim, rim_near.at[OPPOSITE[n] - 2], near(n)))
        beside.append(send(flow.at[max(NEAR[n][1], 0)], flow_side.at[OPPOSITE[n] - 2], near(n)))
    flow_rows = send_rows(2, 0) + send_rows(3, 0)

    sea_packed = jnp.where(lane < 4, roll(sea, 2, 1), 0.0)
    for shift in (4, 8, 16, 32, 64):
        sea_packed = sea_packed + roll(sea_packed, shift, 1)

    @pl.loop(0, groups)
    def _(group):
        held = [zero, zero, zero]
        for i in range(4 * GROUP_LEVELS):
            field = own[group * GROUP_LEVELS + (i // 4 + 1), i % 4]
            held[i % 3] = jnp.where(field_of == i, roll(field, 2 + 4 * i, 1), held[i % 3])
        packed[group] = (held[0] + held[1] + held[2]) * sea_packed

    sides = [send(packed, packed_near.at[OPPOSITE[n] - 2], near(n)) for n in (LEFT, RIGHT)]
    corners = []
    for n in (UP_LEFT, UP_RIGHT, DOWN_LEFT, DOWN_RIGHT):
        edge = 0 if NEAR[n][0] < 0 else 7
        corners.append(
            send(packed.at[:, edge : edge + 1, :], corner_near.at[OPPOSITE[n] - 4, :, 0:1, :], near(n))
        )
    other_rows = send_rows(2, 1) + send_rows(3, 1)
    for c in (0, 1):
        other_rows += send_rows(c, 0) + send_rows(c, 1)
    column = (part * 128 + lane).astype(jnp.float32)
    coriolis = (rotation * time_step) * (2.0 * (column + 0.5) / (128 * n_group) - 1.0)
    middle = 2.0 - jnp.where(first_row, 1.0 - has_up, 0.0) - jnp.where(last_row, 1.0 - has_down, 0.0)
    def step(level, carry):
        above, now = carry
        below = tuple(own[level + 2, c] * sea for c in range(4))
        u, v = now[2], now[3]
        east, north = (0.5 * time_step) * u, (0.5 * time_step) * v
        for c in range(4):
            g = now[c]
            n1, s1 = not_first * roll(g, 1, 0), not_last * roll(g, -1, 0)
            n2, s2 = not_first * roll(n1, 1, 0), not_last * roll(s1, -1, 0)
            west = jnp.where(first_lane, 0.0, roll(g, 1, 1))
            east_of = jnp.where(last_lane, 0.0, roll(g, -1, 1))
            twice = 2.0 * (n1 + s1) + (west + east_of) - 4.0 * g
            biharm = (
                (n2 + s2)
                + middle * g
                - 4.0 * twice
                + jnp.where(first_lane, 0.0, roll(twice, 1, 1))
                + jnp.where(last_lane, 0.0, roll(twice, -1, 1))
            )
            advect = east * (s1 - n1) + north * (east_of - west)
            vertical = above[c] + below[c] - 2.0 * g
            new = g - advect - hyper_visc * biharm + mixing * vertical
            if c == 2:
                new = new + coriolis * v
            elif c == 3:
                new = new - coriolis * u
            new = new * sea
            out[level, c] = new
        return now, below

    top = tuple(own[0, c] * sea for c in range(4))
    now = tuple(own[1, c] * sea for c in range(4))
    half = levels // 2
    middle_pair = lax.fori_loop(0, half, step, (top, now))
    greeted(0)
    greet(1)
    lax.fori_loop(half, levels, step, middle_pair)

    for copy in beside + flow_rows:
        copy.wait_recv()

    low = row < 4
    before = lax.rem(lane, 16) < 8
    rims = [rim_near[n - 2] * exists[n] for n in range(2, 8)]
    rim_side = jnp.where(before, rims[LEFT - 2], rims[RIGHT - 2])
    rim_down = jnp.where(before, rims[DOWN_LEFT - 2], rims[DOWN_RIGHT - 2])
    rim_up = jnp.where(before, rims[UP_LEFT - 2], rims[UP_RIGHT - 2])
    rim_over = jnp.where(low, rim_down, rim_up)

    def edge_of(x, plane):
        return jnp.where((lane < 8) | (lane >= 120), roll(x, -(16 * plane + 8), 1), 0.0)

    def stack(*pairs):
        return jnp.concatenate([jnp.concatenate(pair, axis=1) for pair in pairs], axis=0)

    def around(mine, up, down, plane):
        return stack(
            (mine, edge_of(rim_side, plane)), (jnp.where(low, down, up), edge_of(rim_over, plane))
        )

    sea_all = around(sea, geo_near[UP, 0] * has_up, geo_near[DOWN, 0] * has_down, 0)
    damping_all = around(geo[1], geo_near[UP, 1], geo_near[DOWN, 1], 1)
    forced = sea_all * damping_all * around(geo[2], geo_near[UP, 2], geo_near[DOWN, 2], 2)

    def around_whole(m):
        plane = m + 3
        return stack(
            (sums_own[m], edge_of(rim_side, plane)),
            (sums_near[DOWN, m] * has_down, edge_of(rim_down, plane)),
            (sums_near[UP, m] * has_up, edge_of(rim_up, plane)),
        )

    def ring_laplace(x):
        return (roll(x, 1, 0) + roll(x, -1, 0)) + (roll(x, 1, 1) + roll(x, -1, 1)) - 4.0 * x

    def beside_exists(left, right):
        return jnp.where(lane < 64, zero + right, zero + left)

    inside = stack(
        (zero + 1.0, beside_exists(has_left, has_right)),
        (zero + has_down, beside_exists(exists[DOWN_LEFT], exists[DOWN_RIGHT])),
        (zero + has_up, beside_exists(exists[UP_LEFT], exists[UP_RIGHT])),
    )
    ring_lane = lax.broadcasted_iota(jnp.int32, (24, 256), 1)
    ring_column = (part * 128 + jnp.where(ring_lane < 192, ring_lane, ring_lane - 256)).astype(jnp.float32)
    ring_coriolis = (rotation * time_step) * (2.0 * (ring_column + 0.5) / (128 * n_group) - 1.0)
    level_sums = [around_whole(m) for m in range(2)]
    linear = []
    for m in range(2):
        g = level_sums[m]
        linear.append(
            (g - hyper_visc * ring_laplace(inside * ring_laplace(g)))
            + (ring_coriolis if m == 0 else -ring_coriolis) * level_sums[1 - m]
        )

    is_east_field = lax.rem(field_of, 2) == 0
    first, last = flag(first_row), flag(last_row)
    at_first, at_last = flag(quarter == 0), flag(quarter == 3)

    def of_u(x):
        x = jnp.where(is_east_field, x, 0.0)
        return x + roll(x, 4, 1)

    def of_v(x):
        x = jnp.where(is_east_field, 0.0, x)
        return x + roll(x, -4, 1)

    def across_rows(x, beside):
        return of_u(x) * (last * roll(beside, -1, 0) - first * roll(beside, 1, 0))

    def meet_after(x, after):
        return of_v(x) * (at_last * roll(after, 3, 1))

    def meet_before(x, ahead):
        return of_v(x) * (-at_first * roll(ahead, -3, 1))

    gathered = [zero] * 8
    for group in range(flow_groups):
        mine = flow[0, group], flow[1, group]
        over = [
            jnp.where(low, flow_over[DOWN, e, group] * has_down, flow_over[UP, e, group] * has_up) for e in range(2)
        ]
        left, right = flow_side[0, group] * has_left, flow_side[1, group] * has_right
        corner = [flow_corner[n - 4, group] * exists[n] for n in range(4, 8)]
        over_left = jnp.where(low, corner[DOWN_LEFT - 4], corner[UP_LEFT - 4])
        over_right = jnp.where(low, corner[DOWN_RIGHT - 4], corner[UP_RIGHT - 4])
        terms = (
            meet_before(mine[0], left),
            meet_after(mine[1], right),
            meet_before(right, mine[1]) + across_rows(right, over_right),
            meet_after(left, mine[0]) + across_rows(left, over_left),
            meet_before(over[0], over_left),
            meet_after(over[1], over_right),
            meet_before(over_right, over[1]) + across_rows(over_right, right),
            meet_after(over_left, over[0]) + across_rows(over_left, left),
        )
        gathered = [a + b for a, b in zip(gathered, terms)]

    def over_levels(x):
        x = x + roll(x, -48, 1)
        x = x + roll(x, -24, 1)
        return x + (roll(x, -8, 1) + roll(x, -16, 1))

    gathered = [over_levels(x) for x in gathered]

    def placed(n, c):
        return jnp.where(lane < 4, roll(gathered[n], -4 * c, 1), 0.0) + jnp.where(
            lane >= 124, roll(gathered[n + 1], -4 * c - 4, 1), 0.0
        )

    edges = [[placed(2 * n, c) for c in range(2)] for n in range(4)]

    def met(x, g, weight):
        return jnp.broadcast_to(jnp.sum(x * g, axis=0, keepdims=True) * weight, (8, 128))

    above_weight = geo[0, 0:1, :] * (geo_near[UP, 0, 7:8, :] * has_up)
    below_weight = geo[0, 7:8, :] * (geo_near[DOWN, 0, 0:1, :] * has_down)
    advected = []
    for m in range(2):
        up_g, down_g = rows_near[0, 0, 2 + m], rows_near[1, 0, 2 + m]
        inner_rows = last * met(rows_own[1, 0], down_g, below_weight) - first * met(rows_own[0, 0], up_g, above_weight)
        outer_rows = last * met(rows_near[0, 0, 2], rows_own[0, m], above_weight) - first * met(
            rows_near[1, 0, 2], rows_own[1, m], below_weight
        )
        crossing = stack((edges[0][m] + inner_rows, edges[1][m]), (edges[2][m] + outer_rows, edges[3][m]))
        advected.append(
            around(sums_own[2 + m], sums_near[UP, 2 + m], sums_near[DOWN, 2 + m], 5 + m)
            + (0.5 * time_step) * crossing
        )

    ring_low = lax.broadcasted_iota(jnp.int32, (8, 256), 0) < 4
    transport = []
    for m in range(2):
        nearest = jnp.concatenate(
            [linear[m][0:8], jnp.where(ring_low, linear[m][8:16], linear[m][16:24])], axis=0
        )
        transport.append(sea_all * ((nearest - advected[m]) / levels))
    east_all, north_all = transport
    own_part = sea_all * ((damping_all - 0.5) * 0.25)
    own_split = split(own_part)
    beside_part = sea_all * -0.25

    divergence = 0.5 * (roll(east_all, -1, 0) - roll(east_all, 1, 0) + roll(north_all, -1, 1) - roll(north_all, 1, 1))
    v0 = forced - (gravity * sea_all) * divergence

    def finish_state():
        own_flow = []
        for group in range(groups):
            north = jnp.where(lax.rem(field_of, 4) == 3, packed[group], 0.0)
            north = north + roll(north, -4, 1)
            own_flow.append((0.5 * time_step) * (north + roll(north, -8, 1)))

        for copy in sides + corners + other_rows:
            copy.wait_recv()

        sea_rows = (
            (geo_near[UP, 0, 7:8, :] * has_up, geo_near[UP, 0, 6:7, :] * has_up),
            (geo_near[DOWN, 0, 0:1, :] * has_down, geo_near[DOWN, 0, 1:2, :] * has_down),
        )
        own_rows = ((geo[0, 0:1, :], geo[0, 1:2, :]), (geo[0, 7:8, :], geo[0, 6:7, :]))
        edge_lane = lax.broadcasted_iota(jnp.int32, (levels, 128), 1)
        no_west, no_east = edge_lane == 0, edge_lane == 127

        def fix_rows(c):
            for side in range(2):
                outer_sign = (0.5 * time_step) if side == 0 else -(0.5 * time_step)
                a = rows_near[side, 0, c] * sea_rows[side][0]
                b = rows_near[side, 1, c] * sea_rows[side][1]
                across = jnp.where(no_west, 0.0, roll(a, 1, 1)) + jnp.where(no_east, 0.0, roll(a, -1, 1))
                nearest = (
                    -hyper_visc * (b - 8.0 * a + 2.0 * across) + (outer_sign * own_rows[side][0]) * rows_own[side, 0] * a
                ) * own_rows[side][0]
                second = (-hyper_visc * a) * own_rows[side][1]
                rows_fix[side, 0, c] = nearest
                rows_fix[side, 1, c] = second

        def fix_columns(group):
            mine = packed[group]
            left = packed_near[0, group] * has_left
            right = packed_near[1, group] * has_right
            left_rows = not_first * roll(left, 1, 0) + not_last * roll(left, -1, 0)
            right_rows = not_first * roll(right, 1, 0) + not_last * roll(right, -1, 0)
            at_left = 2.0 * left_rows + roll(left, 1, 1) + has_left * roll(mine, -1, 1) - 8.0 * left
            at_right = 2.0 * right_rows + roll(right, -1, 1) + has_right * roll(mine, 1, 1) - 8.0 * right
            swept = own_flow[group]
            fixed = jnp.where(
                quarter == 0,
                -hyper_visc * roll(right, -2, 1),
                jnp.where(
                    quarter == 1,
                    -hyper_visc * roll(at_right, -1, 1) - swept * roll(right, -1, 1),
                    jnp.where(
                        quarter == 2,
                        -hyper_visc * roll(at_left, 1, 1) + swept * roll(left, 1, 1),
                        -hyper_visc * roll(left, 2, 1),
                    ),
                ),
            )
            return fixed * sea_packed

        beside_edges = (lane < 2) | (lane >= 126)
        for group in range(groups):
            packed_fix[group] = fix_columns(group)
        for c in range(4):
            fix_rows(c)

        def finish(group, carry):
            def at_corner(n):
                return jnp.broadcast_to(corner_near[n - 4, group, 0:1, :] * exists[n], (8, 128))

            left_corner = jnp.where(first_row, at_corner(UP_LEFT), jnp.where(last_row, at_corner(DOWN_LEFT), 0.0))
            right_corner = jnp.where(first_row, at_corner(UP_RIGHT), jnp.where(last_row, at_corner(DOWN_RIGHT), 0.0))
            corner = jnp.where(
                quarter == 1, roll(right_corner, -1, 1), jnp.where(quarter == 2, roll(left_corner, 1, 1), 0.0)
            )
            fixed = packed_fix[group] - (2.0 * hyper_visc) * corner * sea_packed
            for i in range(4 * GROUP_LEVELS):
                level, c = group * GROUP_LEVELS + i // 4, i % 4
                first, second, last, before_last = (
                    jnp.broadcast_to(rows_fix[side, r, c, pl.ds(level, 1), :], (8, 128))
                    for side in range(2)
                    for r in range(2)
                )
                by_rows = jnp.where(
                    first_row,
                    first,
                    jnp.where(row == 1, second, jnp.where(last_row, last, jnp.where(row == 6, before_last, 0.0))),
                )
                by_columns = jnp.where(beside_edges, roll(fixed, -(4 * i + 2), 1), 0.0)
                out[level, c] = out[level, c] + by_rows + by_columns
            return carry

        lax.fori_loop(0, groups, finish, 0)

    def apply(s):
        high, low = s
        up, down = (roll(high, 1, 0), low if low is None else roll(low, 1, 0)), (roll(high, -1, 0), low if low is None else roll(low, -1, 0))
        west, east = (roll(high, 1, 1), low if low is None else roll(low, 1, 1)), (roll(high, -1, 1), low if low is None else roll(low, -1, 1))
        total = join(join(up, down), join(west, east))
        high_split = split(high)
        p = own_part * high
        (ah, al), (bh, bl) = own_split, high_split
        e = ((ah * bh - p) + ah * bl + al * bh) + al * bl
        if low is not None:
            e = e + own_part * low
        return add((p, e), (beside_part * total[0], beside_part * total[1]))

    v1 = apply((v0, None))
    v2 = apply(v1)
    v3 = apply(v2)
    v0 = v0[0:8, 0:128]
    v1, v2, v3 = (tuple(x[0:8, 0:128] for x in v) for v in (v1, v2, v3))
    v0 = (v0, zero)

    high, low = zero, zero
    for m, (a, b) in enumerate(((v0, v0), (v0, v1), (v1, v1), (v1, v2), (v2, v2), (v2, v3))):
        p, e = two_prod(a[0], b[0])
        e = e + (a[0] * b[1] + a[1] * b[0])
        part_sum = (p, e)
        for shift in (4, 2, 1):
            part_sum = join(part_sum, (roll(part_sum[0], shift, 0), roll(part_sum[1], shift, 0)))
        high = jnp.where(row == m, part_sum[0], high)
        low = jnp.where(row == m, part_sum[1], low)
    total = (high, low)
    for shift in (64, 32, 16, 8, 4, 2, 1):
        total = join(total, (roll(total[0], shift, 1), roll(total[1], shift, 1)))
    value = jnp.sum(
        jnp.where(lane == row, total[0], jnp.where(lane == row + 64, total[1], 0.0)), axis=0, keepdims=True
    )

    greeted(1)
    for number, phase in enumerate(phases):
        count = len(phase)
        size = -(-(count + 1) // 8) * 8
        row_out[number, 0:1, :] = value
        for s, partner in enumerate(phase):
            copy = pltpu.make_async_remote_copy(
                src_ref=row_out.at[number, 0:1, :], dst_ref=rows_in.at[number, s : s + 1, :],
                send_sem=send_sems.at[len(sends)], recv_sem=sum_sems.at[number],
                device_id=partner, device_id_type=MESH,
            )
            copy.start()
            sends.append(copy)
        if number == 0:
            finish_state()
        whole = rows_in.at[number, 0:count, :]
        pltpu.make_async_copy(whole, whole, sum_sems.at[number]).wait()
        got = rows_in[number, 0:size, :]
        row_number = lax.broadcasted_iota(jnp.int32, (size, 128), 0)
        got = jnp.where(row_number < count, got, jnp.where(row_number == count, row_out[number, 0:1, :], 0.0))
        summed, lost = sum_rows_of(got)
        value = jnp.where(lane < 64, summed, summed + roll(lost, 64, 1))[0:1, :]

    spread = jnp.broadcast_to(value, (8, 128))

    def pick(m):
        return jnp.sum(jnp.where(lane == m, spread, 0.0), axis=1, keepdims=True)

    mu = [quick_sum(pick(m), pick(64 + m)) for m in range(6)]
    surface[...] = combine(mu, v0, v1, v2)

    for copy in sends:
        copy.wait_send()


def combine(mu, v0, v1, v2):
    a = [add(scale(add(mu[k], mu[k + 1]), 4.0), scale(mu[k], 0.5)) for k in range(5)]
    l1, l2 = div(a[1], a[0]), div(a[2], a[0])
    s11 = minus(a[2], mul(l1, a[1]))
    s12 = minus(a[3], mul(l1, a[2]))
    s22 = minus(a[4], mul(l2, a[2]))
    y1 = minus(mu[1], mul(l1, mu[0]))
    y2 = minus(mu[2], mul(l2, mu[0]))
    sound = s11[0] > 0.0
    one = jnp.ones_like(s11[0])
    none = jnp.zeros_like(s11[0])
    s11 = (jnp.where(sound, s11[0], one), jnp.where(sound, s11[1], none))
    l21 = div(s12, s11)
    inside = sound & (jnp.abs(l21[0] - l1[0]) <= REACH)
    bounded = jnp.clip(l21[0], l1[0] - REACH, l1[0] + REACH)
    l21 = (
        jnp.where(sound, jnp.where(inside, l21[0], bounded), l1[0]),
        jnp.where(sound, jnp.where(inside, l21[1], none), l1[1]),
    )
    t22 = minus(s22, mul(l21, s12))
    z2 = minus(y2, mul(l21, y1))

    def step_of(quotient):
        return jnp.clip(quotient, 1.0 / HIGH, 1.0 / LOW)

    alpha0 = step_of(mu[0][0] / a[0][0])
    alpha1 = step_of(y1[0] / (s11[0] * (-4.0 * alpha0)))
    firm = t22[0] > 0.0
    alpha2 = step_of(z2[0] / (jnp.where(firm, t22[0], one) * (16.0 * alpha0 * alpha1)))

    def wide(pair):
        return tuple(jnp.broadcast_to(x, v0[0].shape) for x in pair)

    l1, l2, l21 = wide(l1), wide(l2), wide(l21)
    p1 = minus(v1, mul(l1, v0))
    p2 = minus(v2, add(mul(l2, v0), mul(l21, p1)))
    return alpha0 * (v0[0] + alpha1 * (-4.0 * p1[0] + (16.0 * alpha2) * p2[0]))


def on_device(n_blocks, n_group, inner, ocean_state, surface_height, surface_damping, land_mask):
    levels = ocean_state.shape[0]
    groups = levels // GROUP_LEVELS
    flow_groups = levels // FLOW_LEVELS
    f32 = jnp.float32
    any_space = pl.BlockSpec(memory_space=pl.ANY)
    vmem = pl.BlockSpec(memory_space=pltpu.VMEM)
    n_sums = (n_blocks - 1) + (n_group - 1)
    dma = pltpu.SemaphoreType.DMA
    new_state, surface = pl.pallas_call(
        functools.partial(kernel, n_blocks, n_group, inner),
        out_shape=(pltpu.VMEM(ocean_state.shape, f32), pltpu.VMEM(surface_height.shape, f32)),
        in_specs=[any_space] * 4,
        out_specs=(vmem, vmem),
        scratch_shapes=[
            pltpu.VMEM((levels + 2, 4, 8, 128), f32),
            pltpu.VMEM((8, 128), jnp.int32),
            pltpu.VMEM((3, 8, 128), f32),
            pltpu.VMEM((2, 3, 8, 128), f32),
            pltpu.VMEM((2, 2, levels, 128), f32),
            pltpu.VMEM((2, 2, 4, levels, 128), f32),
            pltpu.VMEM((2, 2, 4, levels, 128), f32),
            pltpu.VMEM((groups, 8, 128), f32),
            pltpu.VMEM((2, groups, 8, 128), f32),
            pltpu.VMEM((4, groups, 8, 128), f32),
            pltpu.VMEM((groups, 8, 128), f32),
            pltpu.VMEM((2, flow_groups, 8, 128), f32),
            pltpu.VMEM((2, 2, flow_groups, 8, 128), f32),
            pltpu.VMEM((2, flow_groups, 8, 128), f32),
            pltpu.VMEM((4, flow_groups, 8, 128), f32),
            pltpu.VMEM((4, 8, 128), f32),
            pltpu.VMEM((2, 4, 8, 128), f32),
            pltpu.VMEM((8, 128), f32),
            pltpu.VMEM((6, 8, 128), f32),
            pltpu.VMEM((2, 8, 128), f32),
            pltpu.VMEM((2, max(n_blocks, 16), 128), f32),
            dma((10,)),
            dma((40 + n_sums,)),
            dma((40,)),
            dma((2,)),
            pltpu.SemaphoreType.REGULAR((len(ROUNDS),)),
        ],
        compiler_params=pltpu.CompilerParams(collective_id=0, has_side_effects=True),
    )(ocean_state, surface_height, surface_damping, land_mask)
    return pl.pallas_call(
        put_out,
        out_shape=(
            jax.ShapeDtypeStruct(ocean_state.shape, f32),
            jax.ShapeDtypeStruct(surface_height.shape, f32),
        ),
        in_specs=[any_space, any_space],
        out_specs=(any_space, any_space),
        scratch_shapes=[dma((3,))],
    )(
        pltpu.with_memory_space_constraint(new_state, pltpu.VMEM),
        pltpu.with_memory_space_constraint(surface, pltpu.VMEM),
    )


def put_out(state, surface, state_out, surface_out, sems):
    half = state.shape[0] // 2
    copies = (
        pltpu.make_async_copy(state.at[:half], state_out.at[:half], sems.at[0]),
        pltpu.make_async_copy(state.at[half:], state_out.at[half:], sems.at[1]),
        pltpu.make_async_copy(surface, surface_out, sems.at[2]),
    )
    for copy in copies:
        copy.start()
    for copy in copies:
        copy.wait()


def solution(mesh):
    n_blocks, n_group = mesh.shape["blocks"], mesh.shape["group"]
    inner = 8 if n_blocks % 8 == 0 and n_blocks > 8 else max(1, n_blocks // 2)
    placed = (
        P(None, None, "blocks", "group"),
        P("blocks", "group"),
        P("blocks", "group"),
        P("blocks", "group"),
    )
    return jax.shard_map(
        functools.partial(on_device, n_blocks, n_group, inner),
        mesh=mesh,
        in_specs=placed,
        out_specs=(P(None, None, "blocks", "group"), P("blocks", "group")),
        check_vma=False,
    )
```

```python
import functools

import jax
import jax.numpy as jnp
from jax import lax
from jax.experimental import pallas as pl
from jax.experimental.pallas import tpu as pltpu
from jax.sharding import PartitionSpec as P

MESH = pl.DeviceIdType.MESH

time_step = 0.25
hyper_visc = 0.025
mixing = 0.2
gravity = 4.0
rotation = 0.2

LOW, HIGH = 0.05, 9.0
REACH = 1.125

GROUP_LEVELS = 6
FLOW_LEVELS = 12
NEAR = ((-1, 0), (1, 0), (0, -1), (0, 1), (-1, -1), (-1, 1), (1, -1), (1, 1))
OPPOSITE = (1, 0, 3, 2, 7, 6, 5, 4)
UP, DOWN, LEFT, RIGHT, UP_LEFT, UP_RIGHT, DOWN_LEFT, DOWN_RIGHT = range(8)
FIRST = ((1, 2, 3), (2, 3))
ROUNDS = (((1, 2, 3), (3,)), ((1,), ()))


def roll(x, shift, axis):
    return pltpu.roll(x, shift % x.shape[axis], axis)


def two_sum(a, b):
    s = a + b
    t = s - a
    return s, (a - (s - t)) + (b - t)


def quick_sum(a, b):
    s = a + b
    return s, b - (s - a)


def split(a):
    c = 4097.0 * a
    high = c - (c - a)
    return high, a - high


def two_prod(a, b):
    p = a * b
    (ah, al), (bh, bl) = split(a), split(b)
    return p, ((ah * bh - p) + ah * bl + al * bh) + al * bl


def add(a, b):
    s, e = two_sum(a[0], b[0])
    return quick_sum(s, e + (a[1] + b[1]))


def scale(a, power_of_two):
    return a[0] * power_of_two, a[1] * power_of_two


def minus(a, b):
    return add(a, (-b[0], -b[1]))


def mul(a, b):
    p, e = two_prod(a[0], b[0])
    return quick_sum(p, e + (a[0] * b[1] + a[1] * b[0]))


def div(a, b):
    first = a[0] / b[0]
    rest = minus(a, mul(b, (first, jnp.zeros_like(first))))
    return quick_sum(first, rest[0] / b[0])


def sum_rows_of(x):
    parts = [(x[i : i + 8], None) for i in range(0, x.shape[0], 8)]
    while len(parts) > 1:
        parts = [join(*parts[i : i + 2]) for i in range(0, len(parts), 2)]
    part = parts[0]
    for shift in (4, 2, 1):
        other = (roll(part[0], shift, 0), None if part[1] is None else roll(part[1], shift, 0))
        part = join(part, other)
    return part


def join(a, b=None):
    if b is None:
        return a
    s, e = two_sum(a[0], b[0])
    for low in (a[1], b[1]):
        if low is not None:
            e = e + low
    return s, e


def kernel(
    n_blocks, n_group, inner,
    ocean, height, damping, land,
    out, surface,
    own, sea_int, geo, geo_near, rows_own, rows_near, rows_fix, packed, packed_near, corner_near, packed_fix,
    flow, flow_over, flow_side, flow_corner, sums_own, sums_near, rim, rim_near, row_out, rows_in,
    load_sems, send_sems, near_sems, sum_sems, greet_sems,
):
    levels = ocean.shape[0]
    groups = levels // GROUP_LEVELS
    flow_groups = levels // FLOW_LEVELS
    block = lax.axis_index("blocks")
    part = lax.axis_index("group")
    outer = n_blocks // inner

    def near(n):
        db, dg = NEAR[n]
        return (lax.rem(block + (n_blocks + db), n_blocks), lax.rem(part + (n_group + dg), n_group))

    base = (block // inner) * inner

    def along_blocks(distance):
        return (lax.rem(block + (distance % n_blocks), n_blocks), part)

    def along_group(distance):
        return (block, lax.rem(part + (distance % n_group), n_group))

    def far_first(n):
        return sorted(range(1, n), key=lambda s: -min(s, n - s))

    phases = [[along_blocks(s) for s in far_first(n_blocks)], [along_group(s) for s in far_first(n_group)]]

    def apart(rows, along):
        found = [along_blocks(sign * d * inner) for d in rows if d % outer for sign in (1, -1)]
        return found + [along_group(sign * d) for d in along if d % n_group for sign in (1, -1)]

    rounds = [apart(*reach) for reach in ROUNDS]

    loads = [
        pltpu.make_async_copy(land, sea_int, load_sems.at[0]),
        pltpu.make_async_copy(damping, geo.at[1], load_sems.at[1]),
        pltpu.make_async_copy(height, geo.at[2], load_sems.at[2]),
        pltpu.make_async_copy(ocean, own.at[1 : levels + 1], load_sems.at[3]),
        pltpu.make_async_copy(ocean.at[0], own.at[0], load_sems.at[4]),
        pltpu.make_async_copy(ocean.at[levels - 1], own.at[levels + 1], load_sems.at[5]),
    ]
    for side in range(2):
        for c in range(2):
            loads.append(
                pltpu.make_async_copy(
                    ocean.at[:, c + 2, 7 * side, :], rows_own.at[side, c], load_sems.at[6 + 2 * side + c]
                )
            )

    barrier = pltpu.get_barrier_semaphore()
    partners = (
        [near(n) for n in range(8)]
        + [(base + lax.rem(block - base + s, inner), part) for s in range(1, inner)]
        + apart(*FIRST)
    )
    for partner in partners:
        pl.semaphore_signal(barrier, inc=1, device_id=partner, device_id_type=MESH)
    for load in loads:
        load.start()

    row = lax.broadcasted_iota(jnp.int32, (8, 128), 0)
    lane = lax.broadcasted_iota(jnp.int32, (8, 128), 1)
    first_row, last_row = row == 0, row == 7
    first_lane, last_lane = lane == 0, lane == 127
    quarter = lax.rem(lane, 4)
    field_of = lane // 4
    zero = jnp.zeros((8, 128), jnp.float32)

    def flag(condition):
        return jnp.where(condition, jnp.float32(1.0), jnp.float32(0.0))

    has_up, has_down = flag(block > 0), flag(block < n_blocks - 1)
    has_left, has_right = flag(part > 0), flag(part < n_group - 1)
    exists = (
        has_up, has_down, has_left, has_right,
        has_up * has_left, has_up * has_right, has_down * has_left, has_down * has_right,
    )

    sends = []

    def send(source, target, partner):
        copy = pltpu.make_async_remote_copy(
            src_ref=source, dst_ref=target, send_sem=send_sems.at[len(sends)], recv_sem=near_sems.at[len(sends)],
            device_id=partner, device_id_type=MESH,
        )
        copy.start()
        sends.append(copy)
        return copy

    def greet(n):
        for target in rounds[n]:
            pl.semaphore_signal(greet_sems.at[n], inc=1, device_id=target, device_id_type=MESH)

    def greeted(n):
        if rounds[n]:
            pl.semaphore_wait(greet_sems.at[n], len(rounds[n]))

    def send_rows(c, r):
        return [
            send(ocean.at[:, c, r, :], rows_near.at[1, r, c], near(UP)),
            send(ocean.at[:, c, 7 - r, :], rows_near.at[0, r, c], near(DOWN)),
        ]

    for load in loads[:3]:
        load.wait()
    sea = sea_int[...].astype(jnp.float32)
    geo[0] = sea

    for load in loads[3:]:
        load.wait()

    for group in range(flow_groups):
        west, east = [zero, zero], [zero, zero]
        for i in range(2 * FLOW_LEVELS):
            field = roll(own[group * FLOW_LEVELS + (i // 2 + 1), 2 + i % 2] * sea, 4 * i + 4, 1)
            east[i % 2] = jnp.where(field_of == i, field, east[i % 2])
            west[i % 2] = jnp.where(field_of == i + 1, field, west[i % 2])
        flow[0, group] = roll(west[0] + west[1], -4, 1)
        flow[1, group] = east[0] + east[1]

    not_first, not_last = flag(row > 0), flag(row < 7)

    def advection(level, carry):
        u, v = own[level + 1, 2] * sea, own[level + 1, 3] * sea
        east, north = (0.5 * time_step) * u, (0.5 * time_step) * v
        terms = []
        for g in (u, v):
            along = not_last * roll(g, -1, 0) - not_first * roll(g, 1, 0)
            across = jnp.where(last_lane, 0.0, roll(g, -1, 1)) - jnp.where(first_lane, 0.0, roll(g, 1, 1))
            terms.append(east * along + north * across)
        return carry[0] + u, carry[1] + v, carry[2] + terms[0], carry[3] + terms[1]

    for n, total in enumerate(lax.fori_loop(0, levels, advection, (zero, zero, zero, zero), unroll=4)):
        sums_own[n] = total

    held = zero
    for n, plane in enumerate((sea, geo[1], geo[2], sums_own[0], sums_own[1], sums_own[2], sums_own[3])):
        held = jnp.where(lane // 16 == n, roll(plane, 16 * n + 8, 1), held)
    rim[...] = held

    pl.semaphore_wait(barrier, len(partners))
    greet(0)
    halves = {-1: pl.ds(0, 4), 1: pl.ds(4, 4)}
    beside = []
    for n in (UP_LEFT, UP_RIGHT, DOWN_LEFT, DOWN_RIGHT):
        rows, edge = halves[NEAR[n][0]], max(NEAR[n][1], 0)
        beside.append(send(rim, rim_near.at[OPPOSITE[n] - 2], near(n)))
        beside.append(
            send(flow.at[edge, :, rows, :], flow_corner.at[OPPOSITE[n] - 4, :, rows, :], near(n))
        )
    for n in (DOWN, UP):
        rows = halves[NEAR[n][0]]
        beside.append(send(geo, geo_near.at[OPPOSITE[n]], near(n)))
        beside.append(send(sums_own, sums_near.at[OPPOSITE[n]], near(n)))
        beside.append(send(flow.at[:, :, rows, :], flow_over.at[OPPOSITE[n], :, :, rows, :], near(n)))
    for n in (LEFT, RIGHT):
        beside.append(send(rim, rim_near.at[OPPOSITE[n] - 2], near(n)))
        beside.append(send(flow.at[max(NEAR[n][1], 0)], flow_side.at[OPPOSITE[n] - 2], near(n)))
    flow_rows = send_rows(2, 0) + send_rows(3, 0)

    sea_packed = jnp.where(lane < 4, roll(sea, 2, 1), 0.0)
    for shift in (4, 8, 16, 32, 64):
        sea_packed = sea_packed + roll(sea_packed, shift, 1)

    @pl.loop(0, groups)
    def _(group):
        held = [zero, zero, zero]
        for i in range(4 * GROUP_LEVELS):
            field = own[group * GROUP_LEVELS + (i // 4 + 1), i % 4]
            held[i % 3] = jnp.where(field_of == i, roll(field, 2 + 4 * i, 1), held[i % 3])
        packed[group] = (held[0] + held[1] + held[2]) * sea_packed

    sides = [send(packed, packed_near.at[OPPOSITE[n] - 2], near(n)) for n in (LEFT, RIGHT)]
    corners = []
    for n in (UP_LEFT, UP_RIGHT, DOWN_LEFT, DOWN_RIGHT):
        edge = 0 if NEAR[n][0] < 0 else 7
        corners.append(
            send(packed.at[:, edge : edge + 1, :], corner_near.at[OPPOSITE[n] - 4, :, 0:1, :], near(n))
        )
    other_rows = send_rows(2, 1) + send_rows(3, 1)
    for c in (0, 1):
        other_rows += send_rows(c, 0) + send_rows(c, 1)
    column = (part * 128 + lane).astype(jnp.float32)
    coriolis = (rotation * time_step) * (2.0 * (column + 0.5) / (128 * n_group) - 1.0)
    middle = 2.0 - jnp.where(first_row, 1.0 - has_up, 0.0) - jnp.where(last_row, 1.0 - has_down, 0.0)
    def step(level, carry):
        above, now = carry
        below = tuple(own[level + 2, c] * sea for c in range(4))
        u, v = now[2], now[3]
        east, north = (0.5 * time_step) * u, (0.5 * time_step) * v
        for c in range(4):
            g = now[c]
            n1, s1 = not_first * roll(g, 1, 0), not_last * roll(g, -1, 0)
            n2, s2 = not_first * roll(n1, 1, 0), not_last * roll(s1, -1, 0)
            west = jnp.where(first_lane, 0.0, roll(g, 1, 1))
            east_of = jnp.where(last_lane, 0.0, roll(g, -1, 1))
            twice = 2.0 * (n1 + s1) + (west + east_of) - 4.0 * g
            biharm = (
                (n2 + s2)
                + middle * g
                - 4.0 * twice
                + jnp.where(first_lane, 0.0, roll(twice, 1, 1))
                + jnp.where(last_lane, 0.0, roll(twice, -1, 1))
            )
            advect = east * (s1 - n1) + north * (east_of - west)
            vertical = above[c] + below[c] - 2.0 * g
            new = g - advect - hyper_visc * biharm + mixing * vertical
            if c == 2:
                new = new + coriolis * v
            elif c == 3:
                new = new - coriolis * u
            new = new * sea
            out[level, c] = new
        return now, below

    def step_alone():
        top = tuple(own[0, c] * sea for c in range(4))
        now = tuple(own[1, c] * sea for c in range(4))
        lax.fori_loop(0, levels, step, (top, now))

    greeted(0)
    greet(1)

    for copy in beside + flow_rows:
        copy.wait_recv()

    low = row < 4
    before = lax.rem(lane, 16) < 8
    rims = [rim_near[n - 2] * exists[n] for n in range(2, 8)]
    rim_side = jnp.where(before, rims[LEFT - 2], rims[RIGHT - 2])
    rim_down = jnp.where(before, rims[DOWN_LEFT - 2], rims[DOWN_RIGHT - 2])
    rim_up = jnp.where(before, rims[UP_LEFT - 2], rims[UP_RIGHT - 2])
    rim_over = jnp.where(low, rim_down, rim_up)

    def edge_of(x, plane):
        return jnp.where((lane < 8) | (lane >= 120), roll(x, -(16 * plane + 8), 1), 0.0)

    def stack(*pairs):
        return jnp.concatenate([jnp.concatenate(pair, axis=1) for pair in pairs], axis=0)

    def around(mine, up, down, plane):
        return stack(
            (mine, edge_of(rim_side, plane)), (jnp.where(low, down, up), edge_of(rim_over, plane))
        )

    sea_all = around(sea, geo_near[UP, 0] * has_up, geo_near[DOWN, 0] * has_down, 0)
    damping_all = around(geo[1], geo_near[UP, 1], geo_near[DOWN, 1], 1)
    forced = sea_all * damping_all * around(geo[2], geo_near[UP, 2], geo_near[DOWN, 2], 2)

    def around_whole(m):
        plane = m + 3
        return stack(
            (sums_own[m], edge_of(rim_side, plane)),
            (sums_near[DOWN, m] * has_down, edge_of(rim_down, plane)),
            (sums_near[UP, m] * has_up, edge_of(rim_up, plane)),
        )

    def ring_laplace(x):
        return (roll(x, 1, 0) + roll(x, -1, 0)) + (roll(x, 1, 1) + roll(x, -1, 1)) - 4.0 * x

    def beside_exists(left, right):
        return jnp.where(lane < 64, zero + right, zero + left)

    inside = stack(
        (zero + 1.0, beside_exists(has_left, has_right)),
        (zero + has_down, beside_exists(exists[DOWN_LEFT], exists[DOWN_RIGHT])),
        (zero + has_up, beside_exists(exists[UP_LEFT], exists[UP_RIGHT])),
    )
    ring_lane = lax.broadcasted_iota(jnp.int32, (24, 256), 1)
    ring_column = (part * 128 + jnp.where(ring_lane < 192, ring_lane, ring_lane - 256)).astype(jnp.float32)
    ring_coriolis = (rotation * time_step) * (2.0 * (ring_column + 0.5) / (128 * n_group) - 1.0)
    level_sums = [around_whole(m) for m in range(2)]
    linear = []
    for m in range(2):
        g = level_sums[m]
        linear.append(
            (g - hyper_visc * ring_laplace(inside * ring_laplace(g)))
            + (ring_coriolis if m == 0 else -ring_coriolis) * level_sums[1 - m]
        )

    is_east_field = lax.rem(field_of, 2) == 0
    first, last = flag(first_row), flag(last_row)
    at_first, at_last = flag(quarter == 0), flag(quarter == 3)

    def of_u(x):
        x = jnp.where(is_east_field, x, 0.0)
        return x + roll(x, 4, 1)

    def of_v(x):
        x = jnp.where(is_east_field, 0.0, x)
        return x + roll(x, -4, 1)

    def across_rows(x, beside):
        return of_u(x) * (last * roll(beside, -1, 0) - first * roll(beside, 1, 0))

    def meet_after(x, after):
        return of_v(x) * (at_last * roll(after, 3, 1))

    def meet_before(x, ahead):
        return of_v(x) * (-at_first * roll(ahead, -3, 1))

    gathered = [zero] * 8
    for group in range(flow_groups):
        mine = flow[0, group], flow[1, group]
        over = [
            jnp.where(low, flow_over[DOWN, e, group] * has_down, flow_over[UP, e, group] * has_up) for e in range(2)
        ]
        left, right = flow_side[0, group] * has_left, flow_side[1, group] * has_right
        corner = [flow_corner[n - 4, group] * exists[n] for n in range(4, 8)]
        over_left = jnp.where(low, corner[DOWN_LEFT - 4], corner[UP_LEFT - 4])
        over_right = jnp.where(low, corner[DOWN_RIGHT - 4], corner[UP_RIGHT - 4])
        terms = (
            meet_before(mine[0], left),
            meet_after(mine[1], right),
            meet_before(right, mine[1]) + across_rows(right, over_right),
            meet_after(left, mine[0]) + across_rows(left, over_left),
            meet_before(over[0], over_left),
            meet_after(over[1], over_right),
            meet_before(over_right, over[1]) + across_rows(over_right, right),
            meet_after(over_left, over[0]) + across_rows(over_left, left),
        )
        gathered = [a + b for a, b in zip(gathered, terms)]

    def over_levels(x):
        x = x + roll(x, -48, 1)
        x = x + roll(x, -24, 1)
        return x + (roll(x, -8, 1) + roll(x, -16, 1))

    gathered = [over_levels(x) for x in gathered]

    def placed(n, c):
        return jnp.where(lane < 4, roll(gathered[n], -4 * c, 1), 0.0) + jnp.where(
            lane >= 124, roll(gathered[n + 1], -4 * c - 4, 1), 0.0
        )

    edges = [[placed(2 * n, c) for c in range(2)] for n in range(4)]

    def met(x, g, weight):
        return jnp.broadcast_to(jnp.sum(x * g, axis=0, keepdims=True) * weight, (8, 128))

    above_weight = geo[0, 0:1, :] * (geo_near[UP, 0, 7:8, :] * has_up)
    below_weight = geo[0, 7:8, :] * (geo_near[DOWN, 0, 0:1, :] * has_down)
    advected = []
    for m in range(2):
        up_g, down_g = rows_near[0, 0, 2 + m], rows_near[1, 0, 2 + m]
        inner_rows = last * met(rows_own[1, 0], down_g, below_weight) - first * met(rows_own[0, 0], up_g, above_weight)
        outer_rows = last * met(rows_near[0, 0, 2], rows_own[0, m], above_weight) - first * met(
            rows_near[1, 0, 2], rows_own[1, m], below_weight
        )
        crossing = stack((edges[0][m] + inner_rows, edges[1][m]), (edges[2][m] + outer_rows, edges[3][m]))
        advected.append(
            around(sums_own[2 + m], sums_near[UP, 2 + m], sums_near[DOWN, 2 + m], 5 + m)
            + (0.5 * time_step) * crossing
        )

    ring_low = lax.broadcasted_iota(jnp.int32, (8, 256), 0) < 4
    transport = []
    for m in range(2):
        nearest = jnp.concatenate(
            [linear[m][0:8], jnp.where(ring_low, linear[m][8:16], linear[m][16:24])], axis=0
        )
        transport.append(sea_all * ((nearest - advected[m]) / levels))
    east_all, north_all = transport
    own_part = sea_all * ((damping_all - 0.5) * 0.25)
    own_split = split(own_part)
    beside_part = sea_all * -0.25

    divergence = 0.5 * (roll(east_all, -1, 0) - roll(east_all, 1, 0) + roll(north_all, -1, 1) - roll(north_all, 1, 1))
    v0 = forced - (gravity * sea_all) * divergence

    beside_edges = (lane < 2) | (lane >= 126)

    def start_state():
        step_alone()
        own_flow = []
        for group in range(groups):
            north = jnp.where(lax.rem(field_of, 4) == 3, packed[group], 0.0)
            north = north + roll(north, -4, 1)
            own_flow.append((0.5 * time_step) * (north + roll(north, -8, 1)))

        for copy in sides + corners + other_rows:
            copy.wait_recv()

        sea_rows = (
            (geo_near[UP, 0, 7:8, :] * has_up, geo_near[UP, 0, 6:7, :] * has_up),
            (geo_near[DOWN, 0, 0:1, :] * has_down, geo_near[DOWN, 0, 1:2, :] * has_down),
        )
        own_rows = ((geo[0, 0:1, :], geo[0, 1:2, :]), (geo[0, 7:8, :], geo[0, 6:7, :]))
        edge_lane = lax.broadcasted_iota(jnp.int32, (levels, 128), 1)
        no_west, no_east = edge_lane == 0, edge_lane == 127

        def fix_rows(c):
            for side in range(2):
                outer_sign = (0.5 * time_step) if side == 0 else -(0.5 * time_step)
                a = rows_near[side, 0, c] * sea_rows[side][0]
                b = rows_near[side, 1, c] * sea_rows[side][1]
                across = jnp.where(no_west, 0.0, roll(a, 1, 1)) + jnp.where(no_east, 0.0, roll(a, -1, 1))
                nearest = (
                    -hyper_visc * (b - 8.0 * a + 2.0 * across) + (outer_sign * own_rows[side][0]) * rows_own[side, 0] * a
                ) * own_rows[side][0]
                second = (-hyper_visc * a) * own_rows[side][1]
                rows_fix[side, 0, c] = nearest
                rows_fix[side, 1, c] = second

        def fix_columns(group):
            mine = packed[group]
            left = packed_near[0, group] * has_left
            right = packed_near[1, group] * has_right
            left_rows = not_first * roll(left, 1, 0) + not_last * roll(left, -1, 0)
            right_rows = not_first * roll(right, 1, 0) + not_last * roll(right, -1, 0)
            at_left = 2.0 * left_rows + roll(left, 1, 1) + has_left * roll(mine, -1, 1) - 8.0 * left
            at_right = 2.0 * right_rows + roll(right, -1, 1) + has_right * roll(mine, 1, 1) - 8.0 * right
            swept = own_flow[group]
            fixed = jnp.where(
                quarter == 0,
                -hyper_visc * roll(right, -2, 1),
                jnp.where(
                    quarter == 1,
                    -hyper_visc * roll(at_right, -1, 1) - swept * roll(right, -1, 1),
                    jnp.where(
                        quarter == 2,
                        -hyper_visc * roll(at_left, 1, 1) + swept * roll(left, 1, 1),
                        -hyper_visc * roll(left, 2, 1),
                    ),
                ),
            )
            return fixed * sea_packed

        for group in range(groups):
            packed_fix[group] = fix_columns(group)
        for c in range(4):
            fix_rows(c)

    def finish_state():
        def finish(group, carry):
            def at_corner(n):
                return jnp.broadcast_to(corner_near[n - 4, group, 0:1, :] * exists[n], (8, 128))

            left_corner = jnp.where(first_row, at_corner(UP_LEFT), jnp.where(last_row, at_corner(DOWN_LEFT), 0.0))
            right_corner = jnp.where(first_row, at_corner(UP_RIGHT), jnp.where(last_row, at_corner(DOWN_RIGHT), 0.0))
            corner = jnp.where(
                quarter == 1, roll(right_corner, -1, 1), jnp.where(quarter == 2, roll(left_corner, 1, 1), 0.0)
            )
            fixed = packed_fix[group] - (2.0 * hyper_visc) * corner * sea_packed
            for i in range(4 * GROUP_LEVELS):
                level, c = group * GROUP_LEVELS + i // 4, i % 4
                first, second, last, before_last = (
                    jnp.broadcast_to(rows_fix[side, r, c, pl.ds(level, 1), :], (8, 128))
                    for side in range(2)
                    for r in range(2)
                )
                by_rows = jnp.where(
                    first_row,
                    first,
                    jnp.where(row == 1, second, jnp.where(last_row, last, jnp.where(row == 6, before_last, 0.0))),
                )
                by_columns = jnp.where(beside_edges, roll(fixed, -(4 * i + 2), 1), 0.0)
                out[level, c] = out[level, c] + by_rows + by_columns
            return carry

        lax.fori_loop(0, groups, finish, 0)

    def apply(s):
        high, low = s
        up, down = (roll(high, 1, 0), low if low is None else roll(low, 1, 0)), (roll(high, -1, 0), low if low is None else roll(low, -1, 0))
        west, east = (roll(high, 1, 1), low if low is None else roll(low, 1, 1)), (roll(high, -1, 1), low if low is None else roll(low, -1, 1))
        total = join(join(up, down), join(west, east))
        high_split = split(high)
        p = own_part * high
        (ah, al), (bh, bl) = own_split, high_split
        e = ((ah * bh - p) + ah * bl + al * bh) + al * bl
        if low is not None:
            e = e + own_part * low
        return add((p, e), (beside_part * total[0], beside_part * total[1]))

    v1 = apply((v0, None))
    v2 = apply(v1)
    v3 = apply(v2)
    v0 = v0[0:8, 0:128]
    v1, v2, v3 = (tuple(x[0:8, 0:128] for x in v) for v in (v1, v2, v3))
    v0 = (v0, zero)

    high, low = zero, zero
    for m, (a, b) in enumerate(((v0, v0), (v0, v1), (v1, v1), (v1, v2), (v2, v2), (v2, v3))):
        p, e = two_prod(a[0], b[0])
        e = e + (a[0] * b[1] + a[1] * b[0])
        part_sum = (p, e)
        for shift in (4, 2, 1):
            part_sum = join(part_sum, (roll(part_sum[0], shift, 0), roll(part_sum[1], shift, 0)))
        high = jnp.where(row == m, part_sum[0], high)
        low = jnp.where(row == m, part_sum[1], low)
    total = (high, low)
    for shift in (64, 32, 16, 8, 4, 2, 1):
        total = join(total, (roll(total[0], shift, 1), roll(total[1], shift, 1)))
    value = jnp.sum(
        jnp.where(lane == row, total[0], jnp.where(lane == row + 64, total[1], 0.0)), axis=0, keepdims=True
    )

    greeted(1)
    for number, phase in enumerate(phases):
        count = len(phase)
        size = -(-(count + 1) // 8) * 8
        row_out[number, 0:1, :] = value
        for s, partner in enumerate(phase):
            copy = pltpu.make_async_remote_copy(
                src_ref=row_out.at[number, 0:1, :], dst_ref=rows_in.at[number, s : s + 1, :],
                send_sem=send_sems.at[len(sends)], recv_sem=sum_sems.at[number],
                device_id=partner, device_id_type=MESH,
            )
            copy.start()
            sends.append(copy)
        if number == 0:
            start_state()
        else:
            finish_state()
        whole = rows_in.at[number, 0:count, :]
        pltpu.make_async_copy(whole, whole, sum_sems.at[number]).wait()
        got = rows_in[number, 0:size, :]
        row_number = lax.broadcasted_iota(jnp.int32, (size, 128), 0)
        got = jnp.where(row_number < count, got, jnp.where(row_number == count, row_out[number, 0:1, :], 0.0))
        summed, lost = sum_rows_of(got)
        value = jnp.where(lane < 64, summed, summed + roll(lost, 64, 1))[0:1, :]

    spread = jnp.broadcast_to(value, (8, 128))

    def pick(m):
        return jnp.sum(jnp.where(lane == m, spread, 0.0), axis=1, keepdims=True)

    mu = [quick_sum(pick(m), pick(64 + m)) for m in range(6)]
    surface[...] = combine(mu, v0, v1, v2)

    for copy in sends:
        copy.wait_send()


def combine(mu, v0, v1, v2):
    a = [add(scale(add(mu[k], mu[k + 1]), 4.0), scale(mu[k], 0.5)) for k in range(5)]
    l1, l2 = div(a[1], a[0]), div(a[2], a[0])
    s11 = minus(a[2], mul(l1, a[1]))
    s12 = minus(a[3], mul(l1, a[2]))
    s22 = minus(a[4], mul(l2, a[2]))
    y1 = minus(mu[1], mul(l1, mu[0]))
    y2 = minus(mu[2], mul(l2, mu[0]))
    sound = s11[0] > 0.0
    one = jnp.ones_like(s11[0])
    none = jnp.zeros_like(s11[0])
    s11 = (jnp.where(sound, s11[0], one), jnp.where(sound, s11[1], none))
    l21 = div(s12, s11)
    inside = sound & (jnp.abs(l21[0] - l1[0]) <= REACH)
    bounded = jnp.clip(l21[0], l1[0] - REACH, l1[0] + REACH)
    l21 = (
        jnp.where(sound, jnp.where(inside, l21[0], bounded), l1[0]),
        jnp.where(sound, jnp.where(inside, l21[1], none), l1[1]),
    )
    t22 = minus(s22, mul(l21, s12))
    z2 = minus(y2, mul(l21, y1))

    def step_of(quotient):
        return jnp.clip(quotient, 1.0 / HIGH, 1.0 / LOW)

    alpha0 = step_of(mu[0][0] / a[0][0])
    alpha1 = step_of(y1[0] / (s11[0] * (-4.0 * alpha0)))
    firm = t22[0] > 0.0
    alpha2 = step_of(z2[0] / (jnp.where(firm, t22[0], one) * (16.0 * alpha0 * alpha1)))

    def wide(pair):
        return tuple(jnp.broadcast_to(x, v0[0].shape) for x in pair)

    l1, l2, l21 = wide(l1), wide(l2), wide(l21)
    p1 = minus(v1, mul(l1, v0))
    p2 = minus(v2, add(mul(l2, v0), mul(l21, p1)))
    return alpha0 * (v0[0] + alpha1 * (-4.0 * p1[0] + (16.0 * alpha2) * p2[0]))


def on_device(n_blocks, n_group, inner, ocean_state, surface_height, surface_damping, land_mask):
    levels = ocean_state.shape[0]
    groups = levels // GROUP_LEVELS
    flow_groups = levels // FLOW_LEVELS
    f32 = jnp.float32
    any_space = pl.BlockSpec(memory_space=pl.ANY)
    vmem = pl.BlockSpec(memory_space=pltpu.VMEM)
    n_sums = (n_blocks - 1) + (n_group - 1)
    dma = pltpu.SemaphoreType.DMA
    new_state, surface = pl.pallas_call(
        functools.partial(kernel, n_blocks, n_group, inner),
        out_shape=(pltpu.VMEM(ocean_state.shape, f32), pltpu.VMEM(surface_height.shape, f32)),
        in_specs=[any_space] * 4,
        out_specs=(vmem, vmem),
        scratch_shapes=[
            pltpu.VMEM((levels + 2, 4, 8, 128), f32),
            pltpu.VMEM((8, 128), jnp.int32),
            pltpu.VMEM((3, 8, 128), f32),
            pltpu.VMEM((2, 3, 8, 128), f32),
            pltpu.VMEM((2, 2, levels, 128), f32),
            pltpu.VMEM((2, 2, 4, levels, 128), f32),
            pltpu.VMEM((2, 2, 4, levels, 128), f32),
            pltpu.VMEM((groups, 8, 128), f32),
            pltpu.VMEM((2, groups, 8, 128), f32),
            pltpu.VMEM((4, groups, 8, 128), f32),
            pltpu.VMEM((groups, 8, 128), f32),
            pltpu.VMEM((2, flow_groups, 8, 128), f32),
            pltpu.VMEM((2, 2, flow_groups, 8, 128), f32),
            pltpu.VMEM((2, flow_groups, 8, 128), f32),
            pltpu.VMEM((4, flow_groups, 8, 128), f32),
            pltpu.VMEM((4, 8, 128), f32),
            pltpu.VMEM((2, 4, 8, 128), f32),
            pltpu.VMEM((8, 128), f32),
            pltpu.VMEM((6, 8, 128), f32),
            pltpu.VMEM((2, 8, 128), f32),
            pltpu.VMEM((2, max(n_blocks, 16), 128), f32),
            dma((10,)),
            dma((40 + n_sums,)),
            dma((40,)),
            dma((2,)),
            pltpu.SemaphoreType.REGULAR((len(ROUNDS),)),
        ],
        compiler_params=pltpu.CompilerParams(collective_id=0, has_side_effects=True),
    )(ocean_state, surface_height, surface_damping, land_mask)
    return pl.pallas_call(
        put_out,
        out_shape=(
            jax.ShapeDtypeStruct(ocean_state.shape, f32),
            jax.ShapeDtypeStruct(surface_height.shape, f32),
        ),
        in_specs=[any_space, any_space],
        out_specs=(any_space, any_space),
        scratch_shapes=[dma((3,))],
    )(
        pltpu.with_memory_space_constraint(new_state, pltpu.VMEM),
        pltpu.with_memory_space_constraint(surface, pltpu.VMEM),
    )


def put_out(state, surface, state_out, surface_out, sems):
    half = state.shape[0] // 2
    copies = (
        pltpu.make_async_copy(state.at[:half], state_out.at[:half], sems.at[0]),
        pltpu.make_async_copy(state.at[half:], state_out.at[half:], sems.at[1]),
        pltpu.make_async_copy(surface, surface_out, sems.at[2]),
    )
    for copy in copies:
        copy.start()
    for copy in copies:
        copy.wait()


def solution(mesh):
    n_blocks, n_group = mesh.shape["blocks"], mesh.shape["group"]
    inner = 8 if n_blocks % 8 == 0 and n_blocks > 8 else max(1, n_blocks // 2)
    placed = (
        P(None, None, "blocks", "group"),
        P("blocks", "group"),
        P("blocks", "group"),
        P("blocks", "group"),
    )
    return jax.shard_map(
        functools.partial(on_device, n_blocks, n_group, inner),
        mesh=mesh,
        in_specs=placed,
        out_specs=(P(None, None, "blocks", "group"), P("blocks", "group")),
        check_vma=False,
    )
```

```python
import functools

import jax
import jax.numpy as jnp
from jax import lax
from jax.experimental import pallas as pl
from jax.experimental.pallas import tpu as pltpu
from jax.sharding import PartitionSpec as P

MESH = pl.DeviceIdType.MESH

time_step = 0.25
hyper_visc = 0.025
mixing = 0.2
gravity = 4.0
rotation = 0.2

LOW, HIGH = 0.05, 9.0
REACH = 1.125

GROUP_LEVELS = 6
FLOW_LEVELS = 12
NEAR = ((-1, 0), (1, 0), (0, -1), (0, 1), (-1, -1), (-1, 1), (1, -1), (1, 1))
OPPOSITE = (1, 0, 3, 2, 7, 6, 5, 4)
UP, DOWN, LEFT, RIGHT, UP_LEFT, UP_RIGHT, DOWN_LEFT, DOWN_RIGHT = range(8)
FIRST = ((1, 2, 3), (2, 3))
ROUNDS = (((1, 2, 3), (3,)), ((1,), ()))


def roll(x, shift, axis):
    return pltpu.roll(x, shift % x.shape[axis], axis)


def two_sum(a, b):
    s = a + b
    t = s - a
    return s, (a - (s - t)) + (b - t)


def quick_sum(a, b):
    s = a + b
    return s, b - (s - a)


def split(a):
    c = 4097.0 * a
    high = c - (c - a)
    return high, a - high


def two_prod(a, b):
    p = a * b
    (ah, al), (bh, bl) = split(a), split(b)
    return p, ((ah * bh - p) + ah * bl + al * bh) + al * bl


def add(a, b):
    s, e = two_sum(a[0], b[0])
    return quick_sum(s, e + (a[1] + b[1]))


def scale(a, power_of_two):
    return a[0] * power_of_two, a[1] * power_of_two


def minus(a, b):
    return add(a, (-b[0], -b[1]))


def mul(a, b):
    p, e = two_prod(a[0], b[0])
    return quick_sum(p, e + (a[0] * b[1] + a[1] * b[0]))


def div(a, b):
    first = a[0] / b[0]
    rest = minus(a, mul(b, (first, jnp.zeros_like(first))))
    return quick_sum(first, rest[0] / b[0])


def sum_rows_of(x):
    parts = [(x[i : i + 8], None) for i in range(0, x.shape[0], 8)]
    while len(parts) > 1:
        parts = [join(*parts[i : i + 2]) for i in range(0, len(parts), 2)]
    part = parts[0]
    for shift in (4, 2, 1):
        other = (roll(part[0], shift, 0), None if part[1] is None else roll(part[1], shift, 0))
        part = join(part, other)
    return part


def join(a, b=None):
    if b is None:
        return a
    s, e = two_sum(a[0], b[0])
    for low in (a[1], b[1]):
        if low is not None:
            e = e + low
    return s, e


def kernel(
    n_blocks, n_group, inner,
    ocean, height, damping, land,
    out, surface,
    own, sea_int, geo, geo_near, rows_own, rows_near, rows_fix, packed, packed_near, corner_near, packed_fix,
    flow, flow_over, flow_side, flow_corner, sums_own, sums_near, rim, rim_near, row_out, rows_in,
    load_sems, send_sems, near_sems, sum_sems, greet_sems,
):
    levels = ocean.shape[0]
    groups = levels // GROUP_LEVELS
    flow_groups = levels // FLOW_LEVELS
    block = lax.axis_index("blocks")
    part = lax.axis_index("group")
    outer = n_blocks // inner

    def near(n):
        db, dg = NEAR[n]
        return (lax.rem(block + (n_blocks + db), n_blocks), lax.rem(part + (n_group + dg), n_group))

    base = (block // inner) * inner

    def along_blocks(distance):
        return (lax.rem(block + (distance % n_blocks), n_blocks), part)

    def along_group(distance):
        return (block, lax.rem(part + (distance % n_group), n_group))

    def far_first(n):
        return sorted(range(1, n), key=lambda s: -min(s, n - s))

    phases = [[along_blocks(s) for s in far_first(n_blocks)], [along_group(s) for s in far_first(n_group)]]

    def apart(rows, along):
        found = [along_blocks(sign * d * inner) for d in rows if d % outer for sign in (1, -1)]
        return found + [along_group(sign * d) for d in along if d % n_group for sign in (1, -1)]

    rounds = [apart(*reach) for reach in ROUNDS]

    loads = [
        pltpu.make_async_copy(land, sea_int, load_sems.at[0]),
        pltpu.make_async_copy(damping, geo.at[1], load_sems.at[1]),
        pltpu.make_async_copy(height, geo.at[2], load_sems.at[2]),
        pltpu.make_async_copy(ocean, own.at[1 : levels + 1], load_sems.at[3]),
        pltpu.make_async_copy(ocean.at[0], own.at[0], load_sems.at[4]),
        pltpu.make_async_copy(ocean.at[levels - 1], own.at[levels + 1], load_sems.at[5]),
    ]
    for side in range(2):
        for c in range(2):
            loads.append(
                pltpu.make_async_copy(
                    ocean.at[:, c + 2, 7 * side, :], rows_own.at[side, c], load_sems.at[6 + 2 * side + c]
                )
            )

    barrier = pltpu.get_barrier_semaphore()
    partners = (
        [near(n) for n in range(8)]
        + [(base + lax.rem(block - base + s, inner), part) for s in range(1, inner)]
        + apart(*FIRST)
    )
    for partner in partners:
        pl.semaphore_signal(barrier, inc=1, device_id=partner, device_id_type=MESH)
    for load in loads:
        load.start()

    row = lax.broadcasted_iota(jnp.int32, (8, 128), 0)
    lane = lax.broadcasted_iota(jnp.int32, (8, 128), 1)
    first_row, last_row = row == 0, row == 7
    first_lane, last_lane = lane == 0, lane == 127
    quarter = lax.rem(lane, 4)
    field_of = lane // 4
    zero = jnp.zeros((8, 128), jnp.float32)

    def flag(condition):
        return jnp.where(condition, jnp.float32(1.0), jnp.float32(0.0))

    has_up, has_down = flag(block > 0), flag(block < n_blocks - 1)
    has_left, has_right = flag(part > 0), flag(part < n_group - 1)
    exists = (
        has_up, has_down, has_left, has_right,
        has_up * has_left, has_up * has_right, has_down * has_left, has_down * has_right,
    )

    sends = []

    def send(source, target, partner):
        copy = pltpu.make_async_remote_copy(
            src_ref=source, dst_ref=target, send_sem=send_sems.at[len(sends)], recv_sem=near_sems.at[len(sends)],
            device_id=partner, device_id_type=MESH,
        )
        copy.start()
        sends.append(copy)
        return copy

    def greet(n):
        for target in rounds[n]:
            pl.semaphore_signal(greet_sems.at[n], inc=1, device_id=target, device_id_type=MESH)

    def greeted(n):
        if rounds[n]:
            pl.semaphore_wait(greet_sems.at[n], len(rounds[n]))

    def send_rows(c, r):
        return [
            send(ocean.at[:, c, r, :], rows_near.at[1, r, c], near(UP)),
            send(ocean.at[:, c, 7 - r, :], rows_near.at[0, r, c], near(DOWN)),
        ]

    for load in loads[:3]:
        load.wait()
    sea = sea_int[...].astype(jnp.float32)
    geo[0] = sea

    for load in loads[3:]:
        load.wait()

    for group in range(flow_groups):
        west, east = [zero, zero], [zero, zero]
        for i in range(2 * FLOW_LEVELS):
            field = roll(own[group * FLOW_LEVELS + (i // 2 + 1), 2 + i % 2] * sea, 4 * i + 4, 1)
            east[i % 2] = jnp.where(field_of == i, field, east[i % 2])
            west[i % 2] = jnp.where(field_of == i + 1, field, west[i % 2])
        flow[0, group] = roll(west[0] + west[1], -4, 1)
        flow[1, group] = east[0] + east[1]

    not_first, not_last = flag(row > 0), flag(row < 7)

    def advection(level, carry):
        u, v = own[level + 1, 2] * sea, own[level + 1, 3] * sea
        east, north = (0.5 * time_step) * u, (0.5 * time_step) * v
        terms = []
        for g in (u, v):
            along = not_last * roll(g, -1, 0) - not_first * roll(g, 1, 0)
            across = jnp.where(last_lane, 0.0, roll(g, -1, 1)) - jnp.where(first_lane, 0.0, roll(g, 1, 1))
            terms.append(east * along + north * across)
        return carry[0] + u, carry[1] + v, carry[2] + terms[0], carry[3] + terms[1]

    for n, total in enumerate(lax.fori_loop(0, levels, advection, (zero, zero, zero, zero), unroll=4)):
        sums_own[n] = total

    held = zero
    for n, plane in enumerate((sea, geo[1], geo[2], sums_own[0], sums_own[1], sums_own[2], sums_own[3])):
        held = jnp.where(lane // 16 == n, roll(plane, 16 * n + 8, 1), held)
    rim[...] = held

    pl.semaphore_wait(barrier, len(partners))
    greet(0)
    halves = {-1: pl.ds(0, 4), 1: pl.ds(4, 4)}
    beside = []
    for n in (UP_LEFT, UP_RIGHT, DOWN_LEFT, DOWN_RIGHT):
        rows, edge = halves[NEAR[n][0]], max(NEAR[n][1], 0)
        beside.append(send(rim, rim_near.at[OPPOSITE[n] - 2], near(n)))
        beside.append(
            send(flow.at[edge, :, rows, :], flow_corner.at[OPPOSITE[n] - 4, :, rows, :], near(n))
        )
    for n in (DOWN, UP):
        rows = halves[NEAR[n][0]]
        beside.append(send(geo, geo_near.at[OPPOSITE[n]], near(n)))
        beside.append(send(sums_own, sums_near.at[OPPOSITE[n]], near(n)))
        beside.append(send(flow.at[:, :, rows, :], flow_over.at[OPPOSITE[n], :, :, rows, :], near(n)))
    for n in (LEFT, RIGHT):
        beside.append(send(rim, rim_near.at[OPPOSITE[n] - 2], near(n)))
        beside.append(send(flow.at[max(NEAR[n][1], 0)], flow_side.at[OPPOSITE[n] - 2], near(n)))
    flow_rows = send_rows(2, 0) + send_rows(3, 0)

    sea_packed = jnp.where(lane < 4, roll(sea, 2, 1), 0.0)
    for shift in (4, 8, 16, 32, 64):
        sea_packed = sea_packed + roll(sea_packed, shift, 1)

    @pl.loop(0, groups)
    def _(group):
        held = [zero, zero, zero]
        for i in range(4 * GROUP_LEVELS):
            field = own[group * GROUP_LEVELS + (i // 4 + 1), i % 4]
            held[i % 3] = jnp.where(field_of == i, roll(field, 2 + 4 * i, 1), held[i % 3])
        packed[group] = (held[0] + held[1] + held[2]) * sea_packed

    sides = [send(packed, packed_near.at[OPPOSITE[n] - 2], near(n)) for n in (LEFT, RIGHT)]
    corners = []
    for n in (UP_LEFT, UP_RIGHT, DOWN_LEFT, DOWN_RIGHT):
        edge = 0 if NEAR[n][0] < 0 else 7
        corners.append(
            send(packed.at[:, edge : edge + 1, :], corner_near.at[OPPOSITE[n] - 4, :, 0:1, :], near(n))
        )
    other_rows = send_rows(2, 1) + send_rows(3, 1)
    for c in (0, 1):
        other_rows += send_rows(c, 0) + send_rows(c, 1)
    column = (part * 128 + lane).astype(jnp.float32)
    coriolis = (rotation * time_step) * (2.0 * (column + 0.5) / (128 * n_group) - 1.0)
    middle = 2.0 - jnp.where(first_row, 1.0 - has_up, 0.0) - jnp.where(last_row, 1.0 - has_down, 0.0)
    def step(level, carry):
        above, now = carry
        below = tuple(own[level + 2, c] * sea for c in range(4))
        u, v = now[2], now[3]
        east, north = (0.5 * time_step) * u, (0.5 * time_step) * v
        for c in range(4):
            g = now[c]
            n1, s1 = not_first * roll(g, 1, 0), not_last * roll(g, -1, 0)
            n2, s2 = not_first * roll(n1, 1, 0), not_last * roll(s1, -1, 0)
            west = jnp.where(first_lane, 0.0, roll(g, 1, 1))
            east_of = jnp.where(last_lane, 0.0, roll(g, -1, 1))
            twice = 2.0 * (n1 + s1) + (west + east_of) - 4.0 * g
            biharm = (
                (n2 + s2)
                + middle * g
                - 4.0 * twice
                + jnp.where(first_lane, 0.0, roll(twice, 1, 1))
                + jnp.where(last_lane, 0.0, roll(twice, -1, 1))
            )
            advect = east * (s1 - n1) + north * (east_of - west)
            vertical = above[c] + below[c] - 2.0 * g
            new = g - advect - hyper_visc * biharm + mixing * vertical
            if c == 2:
                new = new + coriolis * v
            elif c == 3:
                new = new - coriolis * u
            new = new * sea
            out[level, c] = new
        return now, below

    def step_alone():
        top = tuple(own[0, c] * sea for c in range(4))
        now = tuple(own[1, c] * sea for c in range(4))
        lax.fori_loop(0, levels, step, (top, now), unroll=2)

    greeted(0)
    greet(1)

    for copy in beside + flow_rows:
        copy.wait_recv()

    low = row < 4
    before = lax.rem(lane, 16) < 8
    rims = [rim_near[n - 2] * exists[n] for n in range(2, 8)]
    rim_side = jnp.where(before, rims[LEFT - 2], rims[RIGHT - 2])
    rim_down = jnp.where(before, rims[DOWN_LEFT - 2], rims[DOWN_RIGHT - 2])
    rim_up = jnp.where(before, rims[UP_LEFT - 2], rims[UP_RIGHT - 2])
    rim_over = jnp.where(low, rim_down, rim_up)

    def edge_of(x, plane):
        return jnp.where((lane < 8) | (lane >= 120), roll(x, -(16 * plane + 8), 1), 0.0)

    def stack(*pairs):
        return jnp.concatenate([jnp.concatenate(pair, axis=1) for pair in pairs], axis=0)

    def around(mine, up, down, plane):
        return stack(
            (mine, edge_of(rim_side, plane)), (jnp.where(low, down, up), edge_of(rim_over, plane))
        )

    sea_all = around(sea, geo_near[UP, 0] * has_up, geo_near[DOWN, 0] * has_down, 0)
    damping_all = around(geo[1], geo_near[UP, 1], geo_near[DOWN, 1], 1)
    forced = sea_all * damping_all * around(geo[2], geo_near[UP, 2], geo_near[DOWN, 2], 2)

    def around_whole(m):
        plane = m + 3
        return stack(
            (sums_own[m], edge_of(rim_side, plane)),
            (sums_near[DOWN, m] * has_down, edge_of(rim_down, plane)),
            (sums_near[UP, m] * has_up, edge_of(rim_up, plane)),
        )

    def ring_laplace(x):
        return (roll(x, 1, 0) + roll(x, -1, 0)) + (roll(x, 1, 1) + roll(x, -1, 1)) - 4.0 * x

    def beside_exists(left, right):
        return jnp.where(lane < 64, zero + right, zero + left)

    inside = stack(
        (zero + 1.0, beside_exists(has_left, has_right)),
        (zero + has_down, beside_exists(exists[DOWN_LEFT], exists[DOWN_RIGHT])),
        (zero + has_up, beside_exists(exists[UP_LEFT], exists[UP_RIGHT])),
    )
    ring_lane = lax.broadcasted_iota(jnp.int32, (24, 256), 1)
    ring_column = (part * 128 + jnp.where(ring_lane < 192, ring_lane, ring_lane - 256)).astype(jnp.float32)
    ring_coriolis = (rotation * time_step) * (2.0 * (ring_column + 0.5) / (128 * n_group) - 1.0)
    level_sums = [around_whole(m) for m in range(2)]
    linear = []
    for m in range(2):
        g = level_sums[m]
        linear.append(
            (g - hyper_visc * ring_laplace(inside * ring_laplace(g)))
            + (ring_coriolis if m == 0 else -ring_coriolis) * level_sums[1 - m]
        )

    is_east_field = lax.rem(field_of, 2) == 0
    first, last = flag(first_row), flag(last_row)
    at_first, at_last = flag(quarter == 0), flag(quarter == 3)

    def of_u(x):
        x = jnp.where(is_east_field, x, 0.0)
        return x + roll(x, 4, 1)

    def of_v(x):
        x = jnp.where(is_east_field, 0.0, x)
        return x + roll(x, -4, 1)

    def across_rows(x, beside):
        return of_u(x) * (last * roll(beside, -1, 0) - first * roll(beside, 1, 0))

    def meet_after(x, after):
        return of_v(x) * (at_last * roll(after, 3, 1))

    def meet_before(x, ahead):
        return of_v(x) * (-at_first * roll(ahead, -3, 1))

    gathered = [zero] * 8
    for group in range(flow_groups):
        mine = flow[0, group], flow[1, group]
        over = [
            jnp.where(low, flow_over[DOWN, e, group] * has_down, flow_over[UP, e, group] * has_up) for e in range(2)
        ]
        left, right = flow_side[0, group] * has_left, flow_side[1, group] * has_right
        corner = [flow_corner[n - 4, group] * exists[n] for n in range(4, 8)]
        over_left = jnp.where(low, corner[DOWN_LEFT - 4], corner[UP_LEFT - 4])
        over_right = jnp.where(low, corner[DOWN_RIGHT - 4], corner[UP_RIGHT - 4])
        terms = (
            meet_before(mine[0], left),
            meet_after(mine[1], right),
            meet_before(right, mine[1]) + across_rows(right, over_right),
            meet_after(left, mine[0]) + across_rows(left, over_left),
            meet_before(over[0], over_left),
            meet_after(over[1], over_right),
            meet_before(over_right, over[1]) + across_rows(over_right, right),
            meet_after(over_left, over[0]) + across_rows(over_left, left),
        )
        gathered = [a + b for a, b in zip(gathered, terms)]

    def over_levels(x):
        x = x + roll(x, -48, 1)
        x = x + roll(x, -24, 1)
        return x + (roll(x, -8, 1) + roll(x, -16, 1))

    gathered = [over_levels(x) for x in gathered]

    def placed(n, c):
        return jnp.where(lane < 4, roll(gathered[n], -4 * c, 1), 0.0) + jnp.where(
            lane >= 124, roll(gathered[n + 1], -4 * c - 4, 1), 0.0
        )

    edges = [[placed(2 * n, c) for c in range(2)] for n in range(4)]

    def met(x, g, weight):
        return jnp.broadcast_to(jnp.sum(x * g, axis=0, keepdims=True) * weight, (8, 128))

    above_weight = geo[0, 0:1, :] * (geo_near[UP, 0, 7:8, :] * has_up)
    below_weight = geo[0, 7:8, :] * (geo_near[DOWN, 0, 0:1, :] * has_down)
    advected = []
    for m in range(2):
        up_g, down_g = rows_near[0, 0, 2 + m], rows_near[1, 0, 2 + m]
        inner_rows = last * met(rows_own[1, 0], down_g, below_weight) - first * met(rows_own[0, 0], up_g, above_weight)
        outer_rows = last * met(rows_near[0, 0, 2], rows_own[0, m], above_weight) - first * met(
            rows_near[1, 0, 2], rows_own[1, m], below_weight
        )
        crossing = stack((edges[0][m] + inner_rows, edges[1][m]), (edges[2][m] + outer_rows, edges[3][m]))
        advected.append(
            around(sums_own[2 + m], sums_near[UP, 2 + m], sums_near[DOWN, 2 + m], 5 + m)
            + (0.5 * time_step) * crossing
        )

    ring_low = lax.broadcasted_iota(jnp.int32, (8, 256), 0) < 4
    transport = []
    for m in range(2):
        nearest = jnp.concatenate(
            [linear[m][0:8], jnp.where(ring_low, linear[m][8:16], linear[m][16:24])], axis=0
        )
        transport.append(sea_all * ((nearest - advected[m]) / levels))
    east_all, north_all = transport
    own_part = sea_all * ((damping_all - 0.5) * 0.25)
    own_split = split(own_part)
    beside_part = sea_all * -0.25

    divergence = 0.5 * (roll(east_all, -1, 0) - roll(east_all, 1, 0) + roll(north_all, -1, 1) - roll(north_all, 1, 1))
    v0 = forced - (gravity * sea_all) * divergence

    beside_edges = (lane < 2) | (lane >= 126)

    def start_state():
        step_alone()
        own_flow = []
        for group in range(groups):
            north = jnp.where(lax.rem(field_of, 4) == 3, packed[group], 0.0)
            north = north + roll(north, -4, 1)
            own_flow.append((0.5 * time_step) * (north + roll(north, -8, 1)))

        for copy in sides + corners + other_rows:
            copy.wait_recv()

        sea_rows = (
            (geo_near[UP, 0, 7:8, :] * has_up, geo_near[UP, 0, 6:7, :] * has_up),
            (geo_near[DOWN, 0, 0:1, :] * has_down, geo_near[DOWN, 0, 1:2, :] * has_down),
        )
        own_rows = ((geo[0, 0:1, :], geo[0, 1:2, :]), (geo[0, 7:8, :], geo[0, 6:7, :]))
        edge_lane = lax.broadcasted_iota(jnp.int32, (levels, 128), 1)
        no_west, no_east = edge_lane == 0, edge_lane == 127

        def fix_rows(c):
            for side in range(2):
                outer_sign = (0.5 * time_step) if side == 0 else -(0.5 * time_step)
                a = rows_near[side, 0, c] * sea_rows[side][0]
                b = rows_near[side, 1, c] * sea_rows[side][1]
                across = jnp.where(no_west, 0.0, roll(a, 1, 1)) + jnp.where(no_east, 0.0, roll(a, -1, 1))
                nearest = (
                    -hyper_visc * (b - 8.0 * a + 2.0 * across) + (outer_sign * own_rows[side][0]) * rows_own[side, 0] * a
                ) * own_rows[side][0]
                second = (-hyper_visc * a) * own_rows[side][1]
                rows_fix[side, 0, c] = nearest
                rows_fix[side, 1, c] = second

        def fix_columns(group):
            mine = packed[group]
            left = packed_near[0, group] * has_left
            right = packed_near[1, group] * has_right
            left_rows = not_first * roll(left, 1, 0) + not_last * roll(left, -1, 0)
            right_rows = not_first * roll(right, 1, 0) + not_last * roll(right, -1, 0)
            at_left = 2.0 * left_rows + roll(left, 1, 1) + has_left * roll(mine, -1, 1) - 8.0 * left
            at_right = 2.0 * right_rows + roll(right, -1, 1) + has_right * roll(mine, 1, 1) - 8.0 * right
            swept = own_flow[group]
            fixed = jnp.where(
                quarter == 0,
                -hyper_visc * roll(right, -2, 1),
                jnp.where(
                    quarter == 1,
                    -hyper_visc * roll(at_right, -1, 1) - swept * roll(right, -1, 1),
                    jnp.where(
                        quarter == 2,
                        -hyper_visc * roll(at_left, 1, 1) + swept * roll(left, 1, 1),
                        -hyper_visc * roll(left, 2, 1),
                    ),
                ),
            )
            return fixed * sea_packed

        for group in range(groups):
            packed_fix[group] = fix_columns(group)
        for c in range(4):
            fix_rows(c)

    def finish_state():
        def finish(group, carry):
            def at_corner(n):
                return jnp.broadcast_to(corner_near[n - 4, group, 0:1, :] * exists[n], (8, 128))

            left_corner = jnp.where(first_row, at_corner(UP_LEFT), jnp.where(last_row, at_corner(DOWN_LEFT), 0.0))
            right_corner = jnp.where(first_row, at_corner(UP_RIGHT), jnp.where(last_row, at_corner(DOWN_RIGHT), 0.0))
            corner = jnp.where(
                quarter == 1, roll(right_corner, -1, 1), jnp.where(quarter == 2, roll(left_corner, 1, 1), 0.0)
            )
            fixed = packed_fix[group] - (2.0 * hyper_visc) * corner * sea_packed
            for i in range(4 * GROUP_LEVELS):
                level, c = group * GROUP_LEVELS + i // 4, i % 4
                first, second, last, before_last = (
                    jnp.broadcast_to(rows_fix[side, r, c, pl.ds(level, 1), :], (8, 128))
                    for side in range(2)
                    for r in range(2)
                )
                by_rows = jnp.where(
                    first_row,
                    first,
                    jnp.where(row == 1, second, jnp.where(last_row, last, jnp.where(row == 6, before_last, 0.0))),
                )
                by_columns = jnp.where(beside_edges, roll(fixed, -(4 * i + 2), 1), 0.0)
                out[level, c] = out[level, c] + by_rows + by_columns
            return carry

        lax.fori_loop(0, groups, finish, 0)

    def apply(s):
        high, low = s
        up, down = (roll(high, 1, 0), low if low is None else roll(low, 1, 0)), (roll(high, -1, 0), low if low is None else roll(low, -1, 0))
        west, east = (roll(high, 1, 1), low if low is None else roll(low, 1, 1)), (roll(high, -1, 1), low if low is None else roll(low, -1, 1))
        total = join(join(up, down), join(west, east))
        high_split = split(high)
        p = own_part * high
        (ah, al), (bh, bl) = own_split, high_split
        e = ((ah * bh - p) + ah * bl + al * bh) + al * bl
        if low is not None:
            e = e + own_part * low
        return add((p, e), (beside_part * total[0], beside_part * total[1]))

    v1 = apply((v0, None))
    v2 = apply(v1)
    v3 = apply(v2)
    v0 = v0[0:8, 0:128]
    v1, v2, v3 = (tuple(x[0:8, 0:128] for x in v) for v in (v1, v2, v3))
    v0 = (v0, zero)

    high, low = zero, zero
    for m, (a, b) in enumerate(((v0, v0), (v0, v1), (v1, v1), (v1, v2), (v2, v2), (v2, v3))):
        p, e = two_prod(a[0], b[0])
        e = e + (a[0] * b[1] + a[1] * b[0])
        part_sum = (p, e)
        for shift in (4, 2, 1):
            part_sum = join(part_sum, (roll(part_sum[0], shift, 0), roll(part_sum[1], shift, 0)))
        high = jnp.where(row == m, part_sum[0], high)
        low = jnp.where(row == m, part_sum[1], low)
    total = (high, low)
    for shift in (64, 32, 16, 8, 4, 2, 1):
        total = join(total, (roll(total[0], shift, 1), roll(total[1], shift, 1)))
    value = jnp.sum(
        jnp.where(lane == row, total[0], jnp.where(lane == row + 64, total[1], 0.0)), axis=0, keepdims=True
    )

    greeted(1)
    for number, phase in enumerate(phases):
        count = len(phase)
        size = -(-(count + 1) // 8) * 8
        row_out[number, 0:1, :] = value
        for s, partner in enumerate(phase):
            copy = pltpu.make_async_remote_copy(
                src_ref=row_out.at[number, 0:1, :], dst_ref=rows_in.at[number, s : s + 1, :],
                send_sem=send_sems.at[len(sends)], recv_sem=sum_sems.at[number],
                device_id=partner, device_id_type=MESH,
            )
            copy.start()
            sends.append(copy)
        if number == 0:
            start_state()
        else:
            finish_state()
        whole = rows_in.at[number, 0:count, :]
        pltpu.make_async_copy(whole, whole, sum_sems.at[number]).wait()
        got = rows_in[number, 0:size, :]
        row_number = lax.broadcasted_iota(jnp.int32, (size, 128), 0)
        got = jnp.where(row_number < count, got, jnp.where(row_number == count, row_out[number, 0:1, :], 0.0))
        summed, lost = sum_rows_of(got)
        value = jnp.where(lane < 64, summed, summed + roll(lost, 64, 1))[0:1, :]

    spread = jnp.broadcast_to(value, (8, 128))

    def pick(m):
        return jnp.sum(jnp.where(lane == m, spread, 0.0), axis=1, keepdims=True)

    mu = [quick_sum(pick(m), pick(64 + m)) for m in range(6)]
    surface[...] = combine(mu, v0, v1, v2)

    for copy in sends:
        copy.wait_send()


def combine(mu, v0, v1, v2):
    a = [add(scale(add(mu[k], mu[k + 1]), 4.0), scale(mu[k], 0.5)) for k in range(5)]
    l1, l2 = div(a[1], a[0]), div(a[2], a[0])
    s11 = minus(a[2], mul(l1, a[1]))
    s12 = minus(a[3], mul(l1, a[2]))
    s22 = minus(a[4], mul(l2, a[2]))
    y1 = minus(mu[1], mul(l1, mu[0]))
    y2 = minus(mu[2], mul(l2, mu[0]))
    sound = s11[0] > 0.0
    one = jnp.ones_like(s11[0])
    none = jnp.zeros_like(s11[0])
    s11 = (jnp.where(sound, s11[0], one), jnp.where(sound, s11[1], none))
    l21 = div(s12, s11)
    inside = sound & (jnp.abs(l21[0] - l1[0]) <= REACH)
    bounded = jnp.clip(l21[0], l1[0] - REACH, l1[0] + REACH)
    l21 = (
        jnp.where(sound, jnp.where(inside, l21[0], bounded), l1[0]),
        jnp.where(sound, jnp.where(inside, l21[1], none), l1[1]),
    )
    t22 = minus(s22, mul(l21, s12))
    z2 = minus(y2, mul(l21, y1))

    def step_of(quotient):
        return jnp.clip(quotient, 1.0 / HIGH, 1.0 / LOW)

    alpha0 = step_of(mu[0][0] / a[0][0])
    alpha1 = step_of(y1[0] / (s11[0] * (-4.0 * alpha0)))
    firm = t22[0] > 0.0
    alpha2 = step_of(z2[0] / (jnp.where(firm, t22[0], one) * (16.0 * alpha0 * alpha1)))

    def wide(pair):
        return tuple(jnp.broadcast_to(x, v0[0].shape) for x in pair)

    l1, l2, l21 = wide(l1), wide(l2), wide(l21)
    p1 = minus(v1, mul(l1, v0))
    p2 = minus(v2, add(mul(l2, v0), mul(l21, p1)))
    return alpha0 * (v0[0] + alpha1 * (-4.0 * p1[0] + (16.0 * alpha2) * p2[0]))


def on_device(n_blocks, n_group, inner, ocean_state, surface_height, surface_damping, land_mask):
    levels = ocean_state.shape[0]
    groups = levels // GROUP_LEVELS
    flow_groups = levels // FLOW_LEVELS
    f32 = jnp.float32
    any_space = pl.BlockSpec(memory_space=pl.ANY)
    vmem = pl.BlockSpec(memory_space=pltpu.VMEM)
    n_sums = (n_blocks - 1) + (n_group - 1)
    dma = pltpu.SemaphoreType.DMA
    new_state, surface = pl.pallas_call(
        functools.partial(kernel, n_blocks, n_group, inner),
        out_shape=(pltpu.VMEM(ocean_state.shape, f32), pltpu.VMEM(surface_height.shape, f32)),
        in_specs=[any_space] * 4,
        out_specs=(vmem, vmem),
        scratch_shapes=[
            pltpu.VMEM((levels + 2, 4, 8, 128), f32),
            pltpu.VMEM((8, 128), jnp.int32),
            pltpu.VMEM((3, 8, 128), f32),
            pltpu.VMEM((2, 3, 8, 128), f32),
            pltpu.VMEM((2, 2, levels, 128), f32),
            pltpu.VMEM((2, 2, 4, levels, 128), f32),
            pltpu.VMEM((2, 2, 4, levels, 128), f32),
            pltpu.VMEM((groups, 8, 128), f32),
            pltpu.VMEM((2, groups, 8, 128), f32),
            pltpu.VMEM((4, groups, 8, 128), f32),
            pltpu.VMEM((groups, 8, 128), f32),
            pltpu.VMEM((2, flow_groups, 8, 128), f32),
            pltpu.VMEM((2, 2, flow_groups, 8, 128), f32),
            pltpu.VMEM((2, flow_groups, 8, 128), f32),
            pltpu.VMEM((4, flow_groups, 8, 128), f32),
            pltpu.VMEM((4, 8, 128), f32),
            pltpu.VMEM((2, 4, 8, 128), f32),
            pltpu.VMEM((8, 128), f32),
            pltpu.VMEM((6, 8, 128), f32),
            pltpu.VMEM((2, 8, 128), f32),
            pltpu.VMEM((2, max(n_blocks, 16), 128), f32),
            dma((10,)),
            dma((40 + n_sums,)),
            dma((40,)),
            dma((2,)),
            pltpu.SemaphoreType.REGULAR((len(ROUNDS),)),
        ],
        compiler_params=pltpu.CompilerParams(collective_id=0, has_side_effects=True),
    )(ocean_state, surface_height, surface_damping, land_mask)
    return pl.pallas_call(
        put_out,
        out_shape=(
            jax.ShapeDtypeStruct(ocean_state.shape, f32),
            jax.ShapeDtypeStruct(surface_height.shape, f32),
        ),
        in_specs=[any_space, any_space],
        out_specs=(any_space, any_space),
        scratch_shapes=[dma((3,))],
    )(
        pltpu.with_memory_space_constraint(new_state, pltpu.VMEM),
        pltpu.with_memory_space_constraint(surface, pltpu.VMEM),
    )


def put_out(state, surface, state_out, surface_out, sems):
    half = state.shape[0] // 2
    copies = (
        pltpu.make_async_copy(state.at[:half], state_out.at[:half], sems.at[0]),
        pltpu.make_async_copy(state.at[half:], state_out.at[half:], sems.at[1]),
        pltpu.make_async_copy(surface, surface_out, sems.at[2]),
    )
    for copy in copies:
        copy.start()
    for copy in copies:
        copy.wait()


def solution(mesh):
    n_blocks, n_group = mesh.shape["blocks"], mesh.shape["group"]
    inner = 8 if n_blocks % 8 == 0 and n_blocks > 8 else max(1, n_blocks // 2)
    placed = (
        P(None, None, "blocks", "group"),
        P("blocks", "group"),
        P("blocks", "group"),
        P("blocks", "group"),
    )
    return jax.shard_map(
        functools.partial(on_device, n_blocks, n_group, inner),
        mesh=mesh,
        in_specs=placed,
        out_specs=(P(None, None, "blocks", "group"), P("blocks", "group")),
        check_vma=False,
    )
```
